256 devices in a mesh: tm: 64 (over z, x, core), col: 4 (over y).
Axes of the slice: x: 4, y: 4, z: 8, core: 2. Of those that a mesh axis runs over, the one named last changes fastest.
Arguments:
- couple: float32 [64, 1024, 1024], P('tm'), may hold values from -1 to 1
- free_term: float32 [64, 64, 1024], P('tm'), may hold values from -4 to 4
- slab_left: float32 [64, 4, 1024, 1024], P('tm', None, None, 'col'), may hold values from -0.125 to 0.125
- slab_right: float32 [64, 4, 1024, 1024], P('tm', None, None, 'col'), may hold values from -0.125 to 0.125
- arrow_rows: float32 [64, 64, 1024], P('tm', None, 'col'), may hold values from -0.0234375 to 0.0234375
- corner_base: float32 [64, 64], replicated, may hold values from -4 to 4
Outputs:
- boundary: float32 [64, 64, 1024], P('tm', None, 'col')
- slab_inverse: float32 [64, 4, 64, 1024], P('tm', None, None, 'col')
- corner: float32 [64, 64], replicated
The draws below stay inside these ranges and needn't reach their ends.
All inputs are finite; a program needn't handle non-finite values.
Results may differ from the reference program's by a relative error of at most 0.00015.
Values sent between devices are 32-bit elements; how exact they have to be, the bound alone decides.
No kernel may reach another device: no remote copies, remote signals or barrier semaphores. Data moves between devices by JAX's collectives and lax.ppermute only.
A program may use at most 128 MiB of HBM per device.

```python
import math
import jax
import jax.numpy as jnp
from jax import lax

SPATIAL_BLOCK = 1024
ARROW = 64
SLAB = 4
TIME_PARTITIONS = 64


def draw_couple(key, part):
    baseline_key, variation_key, spike_key, jitter_key = jax.random.split(key, 4)
    baseline_level = jax.random.uniform(baseline_key, (SPATIAL_BLOCK,), jnp.float32, 0.3, 0.8)
    noise = jax.random.truncated_normal(jitter_key, -2.0, 2.0, (TIME_PARTITIONS, SPATIAL_BLOCK, SPATIAL_BLOCK), jnp.float32)
    noise_scale = 0.7
    variation_factor = jax.random.uniform(variation_key, (TIME_PARTITIONS, SPATIAL_BLOCK), jnp.float32, 0.9, 1.0)
    spike_amount = jnp.where(jax.random.uniform(spike_key, (TIME_PARTITIONS, SPATIAL_BLOCK), jnp.float32) < 0.06, 0.6, 1.0)
    event_frequency = baseline_level[None, :] * variation_factor * spike_amount
    identity = jnp.eye(SPATIAL_BLOCK, dtype=jnp.float32)
    return noise * (noise_scale / math.sqrt(SPATIAL_BLOCK)) + identity[None, :, :] * event_frequency[:, None, :]


def block_levels(rng, extent, cuts, smallest, top_value):
    loudness, own = 1.0, jax.random.fold_in(rng, 6)
    for axis_at, parts in cuts:
        steps = jnp.exp(jax.random.uniform(jax.random.fold_in(own, axis_at), (parts,), jnp.float32, smallest / len(cuts), top_value / len(cuts)))
        loudness = loudness * jnp.repeat(steps, extent[axis_at] // parts).reshape([-1 if axis == axis_at else 1 for axis in range(len(extent))])
    return loudness


def scatter_about(key, dims, spread, limit, cuts=(), kind=jnp.bfloat16):
    array = jax.random.normal(key, dims, jnp.float32) * spread
    if len(cuts) > 0:
        array = block_levels(key, dims, cuts, -0.22, 0.18) * array
    return jnp.clip(array, min=-limit, max=limit).astype(kind)


def setup_inputs(seed: int = 0) -> dict:
    splits = jax.random.split(jax.random.key(seed), 7)
    return {
        "couple": draw_couple(jax.random.fold_in(splits[6], 71), 0),
        "free_term": scatter_about(splits[1], (TIME_PARTITIONS, ARROW, SPATIAL_BLOCK), 0.3, 4.0, ((0, 64),), jnp.float32),
        "slab_left": scatter_about(splits[2], (TIME_PARTITIONS, SLAB, SPATIAL_BLOCK, SPATIAL_BLOCK), (2 * SPATIAL_BLOCK) ** -0.5, 0.125, ((0, 64), (3, 4)), jnp.float32),
        "slab_right": scatter_about(splits[3], (TIME_PARTITIONS, SLAB, SPATIAL_BLOCK, SPATIAL_BLOCK), (2 * SPATIAL_BLOCK) ** -0.5, 0.125, ((0, 64), (3, 4)), jnp.float32),
        "arrow_rows": scatter_about(splits[4], (TIME_PARTITIONS, ARROW, SPATIAL_BLOCK), (SPATIAL_BLOCK * TIME_PARTITIONS) ** -0.5, 0.0234375, ((0, 64), (2, 4)), jnp.float32),
        "corner_base": scatter_about(splits[5], (ARROW, ARROW), 0.5, 4.0, (), jnp.float32),
    }


def sweep_back(couple, free_term):
    highest = lax.Precision.HIGHEST

    def advance(state, pieces):
        matrix, own_term = pieces
        result = jnp.dot(state, matrix, precision=highest, preferred_element_type=jnp.float32) + own_term
        return result, result

    start = jnp.zeros(free_term.shape[1:], jnp.float32)
    final, stacked = lax.scan(advance, start, (couple, free_term), reverse=True)
    return stacked


def reference(couple, free_term, slab_left, slab_right, arrow_rows, corner_base):
    highest = lax.Precision.HIGHEST
    boundary = sweep_back(couple, free_term)
    following = jnp.concatenate([boundary[1:], jnp.zeros_like(boundary[:1])], axis=0)
    slab_inverse = jnp.einsum("pab,pkbc->pkac", boundary, slab_left, precision=highest)
    slab_inverse = slab_inverse + jnp.einsum("pab,pkbc->pkac", following, slab_right, precision=highest)
    corner = corner_base + jnp.einsum("pab,pcb->ac", arrow_rows, boundary, precision=highest)
    return boundary, slab_inverse, corner
```

```python
import functools
import jax
import jax.numpy as jnp
from jax import lax
from jax.experimental import pallas as pl
from jax.experimental.pallas import tpu as pltpu
from jax.sharding import PartitionSpec as P

PARTS = 64
N = 1024
COLS = 4
ROWS = 16
BLOCK = 256
TOP = 20
GROUPS = (PARTS - TOP) // 4
F32 = jnp.float32
BF16 = jnp.bfloat16
VMEM = pl.BlockSpec(memory_space=pltpu.VMEM)
SMEM = pl.BlockSpec(memory_space=pltpu.SMEM)


def split(value):
    high = value.astype(BF16)
    return high, (value - high.astype(F32)).astype(BF16)


def product(left, high, low):
    rows = left.shape[0]
    left_high, left_low = split(left)
    both = jnp.dot(jnp.concatenate([left_high, left_low], 0), high, preferred_element_type=F32)
    return both[:rows] + both[rows:] + jnp.dot(left_high, low, preferred_element_type=F32)


def call(body, outs, specs, operands, flops=0, limit=8, **kw):
    return pl.pallas_call(
        body,
        out_shape=outs,
        in_specs=specs,
        out_specs=[VMEM] * len(outs),
        compiler_params=pltpu.CompilerParams(vmem_limit_bytes=limit << 20),
        cost_estimate=pl.CostEstimate(flops=flops, bytes_accessed=4 << 20, transcendentals=0),
        **kw,
    )(*operands)


def shape(*dims, dtype=F32):
    return jax.ShapeDtypeStruct(dims, dtype)


def tall_body(left_ref, bias_ref, high_ref, low_ref, out_ref):
    out_ref[...] = product(left_ref[...], high_ref[...], low_ref[...])
    out_ref[BLOCK:, :] += bias_ref[...]


def tall(left, bias, high, low):
    (out,) = call(tall_body, [shape(BLOCK + ROWS, N)], [VMEM] * 4, (left, bias, high, low), 6 * 272 * N * N)
    return out


def keep_or(meta_ref, test, run, states_in, states_out):
    active = test(meta_ref[0])

    @pl.when(active)
    def _():
        run()

    @pl.when(jnp.logical_not(active))
    def _():
        for before, after in zip(states_in, states_out):
            after[...] = before[...]


def two_body(test, meta, got, in_0, odd_0, even_0, fo, fe, oh, ol, eh, el, in_1, odd_1, even_1):
    def run():
        x = got[...]
        odd = product(x, oh[...], ol[...]) + fo[...]
        in_1[...] = x
        odd_1[...] = odd
        even_1[...] = product(odd, eh[...], el[...]) + fe[...]

    keep_or(meta, test, run, (in_0, odd_0, even_0), (in_1, odd_1, even_1))


def two_steps(test, meta, got, states, terms, mats):
    return call(
        functools.partial(two_body, test),
        [shape(ROWS, N)] * 3,
        [SMEM] + [VMEM] * 10,
        (meta, got, *states, *terms, *mats),
        12 * 16 * N * N,
        input_output_aliases={2: 0, 3: 1, 4: 2},
    )


def one_body(test, meta, got, in_0, state_0, term, high, low, in_1, state_1):
    def run():
        x = got[...]
        in_1[...] = x
        state_1[...] = product(x, high[...], low[...]) + term[...]

    keep_or(meta, test, run, (in_0, state_0), (in_1, state_1))


def one_step(test, meta, got, states, term, mats):
    return call(
        functools.partial(one_body, test),
        [shape(ROWS, N)] * 2,
        [SMEM] + [VMEM] * 6,
        (meta, got, *states, term, *mats),
        6 * 16 * N * N,
        input_output_aliases={2: 0, 3: 1},
    )


def place_body(place_ref, b0, b1, b2, b3, high_ref, low_ref):
    for index, block in enumerate((b0, b1, b2, b3)):
        high, low = split(block[...])
        at = pl.ds(pl.multiple_of(place_ref[1 + index] * BLOCK, BLOCK), BLOCK)
        high_ref[at, :] = high
        low_ref[at, :] = low


def slab_body(place_ref, b0, b1, b2, b3, lh, ll, rh, rl, x_ref, out_ref, next_ref):
    for index, block in enumerate((b0, b1, b2, b3)):
        at = pl.ds(pl.multiple_of(place_ref[1 + index] * ROWS, ROWS), ROWS)
        x_ref[at, :] = block[:ROWS, :]
        next_ref[at, :] = block[ROWS:, :]
    own = x_ref[...]
    later = next_ref[...]
    for k in range(4):
        out_ref[k] = product(own, lh[k * N : k * N + N, :], ll[k * N : k * N + N, :])
        out_ref[k] += product(later, rh[k * N : k * N + N, :], rl[k * N : k * N + N, :])


def split_body(value_ref, high_ref, low_ref):
    high_ref[...], low_ref[...] = split(value_ref[...])


def halves(value):
    rows, columns = value.shape
    tile = pl.BlockSpec((BLOCK, columns), lambda i: (i, 0))
    return pl.pallas_call(
        split_body,
        grid=(rows // BLOCK,),
        out_shape=[shape(rows, columns, dtype=BF16)] * 2,
        in_specs=[tile],
        out_specs=[tile, tile],
        compiler_params=pltpu.CompilerParams(vmem_limit_bytes=8 << 20),
        cost_estimate=pl.CostEstimate(flops=2 * rows * columns, bytes_accessed=8 * rows * columns, transcendentals=0),
    )(value)


def around(value, members):
    return [lax.ppermute(value, ("tm", "col"), [(t * COLS + j, t * COLS + (j + by) % COLS) for t in members for j in range(COLS)]) for by in (1, 3, 2)]


def local(couple, free_term, slab_left, slab_right, arrow_rows, corner_base):
    me = lax.axis_index("tm")
    c = lax.axis_index("col")
    own = couple[0]
    meta = jnp.stack([me, c, (c + 3) % COLS, (c + 1) % COLS, (c + 2) % COLS]).astype(jnp.int32)
    f = lax.dynamic_slice_in_dim(free_term[0], c * ROWS, ROWS, 0)
    groups = range(GROUPS)

    start = jnp.concatenate([lax.dynamic_slice_in_dim(own, c * BLOCK, BLOCK, 0), f], 0)
    start = lax.ppermute(start, "tm", [(4 * k + 3, 4 * k + 2) for k in groups])
    down = [(2 * j + 1, 2 * j) for j in range(PARTS // 2)]
    other = lax.ppermute(own, "tm", down)
    f_odd = lax.ppermute(f, "tm", down)
    even_mats = halves(own)
    odd_mats = halves(other)
    inner = [(4 * k + 2, 4 * k) for k in groups]

    rows = tall(start, f, *even_mats)
    rows = lax.ppermute(rows, "tm", inner)
    rows = tall(rows, f_odd, *odd_mats)
    rows = tall(rows, f, *even_mats)
    term = rows[BLOCK:]
    rows = rows[:BLOCK]
    blocks = [rows] + around(rows, [4 * k for k in groups])
    group_mats = call(place_body, [shape(N, N, dtype=BF16)] * 2, [SMEM] + [VMEM] * 4, (meta, *blocks))

    zero = jnp.zeros((ROWS, N), F32)
    mats = (*odd_mats, *even_mats)
    terms = (f_odd, f)
    states = (zero, zero, zero)
    chips = TOP // 2
    half = chips // 2
    got = zero
    for i in range(chips):
        device = PARTS - 2 - 2 * i
        if i:
            pairs = [(device + 2, device)]
            mate = i + half if i + half < chips else i - half
            if 0 < mate < chips:
                at = PARTS - 2 - 2 * mate
                pairs.append((at + 2, at))
            got = lax.ppermute(states[2], "tm", sorted(pairs))
        states = two_steps(lambda at, device=device: at == device, meta, got, states, terms, mats)
    x_in, x_odd, x_even = states
    for k in reversed(groups):
        got = lax.ppermute(x_even, "tm", [(4 * k + 4, 4 * k)])
        x_in, x_even = one_step(lambda at, k=k: at == 4 * k, meta, got, (x_in, x_even), term, group_mats)
    got = lax.ppermute(x_even, "tm", [(4 * k + 4, 4 * k + 2) for k in groups])
    states = two_steps(lambda at: (at % 4 == 2) & (at < 4 * GROUPS), meta, got, (x_in, x_odd, x_even), terms, mats)
    x_in, x_odd, x_even = states
    got = lax.ppermute(x_even, "tm", inner)
    x_in, x_odd = one_step(lambda at: (at % 4 == 0) & (at < 4 * GROUPS), meta, got, (x_in, x_odd), f_odd, odd_mats)

    up = [(b, a) for a, b in down]
    pair = lax.ppermute(jnp.concatenate([x_odd, x_in], 0), "tm", up)
    pair = jnp.where(me % 2 == 1, pair, jnp.concatenate([x_even, x_odd], 0))
    blocks = [pair] + around(pair, range(PARTS))
    left = halves(slab_left[0].reshape(4 * N, BLOCK))
    right = halves(slab_right[0].reshape(4 * N, BLOCK))
    x, slab = call(
        slab_body,
        [shape(64, N), shape(4, 64, BLOCK)],
        [SMEM] + [VMEM] * 8,
        (meta, *blocks, *left, *right),
        12 * 64 * N * N,
        scratch_shapes=[pltpu.VMEM((64, N), F32)],
    )
    columns = lax.dynamic_slice_in_dim(x, c * BLOCK, BLOCK, 1)
    total = jnp.dot(arrow_rows[0], columns.T, precision=lax.Precision.HIGHEST, preferred_element_type=F32)
    behind, ahead, across = around(total, range(PARTS))
    total = (total + across) + (behind + ahead)
    for bit in (1, 2, 4, 8, 16, 32):
        total = total + lax.ppermute(total, "tm", [(j, j ^ bit) for j in range(PARTS)])
    return (columns[None], slab[None], corner_base + total)


def solution(mesh):
    placed = (
        P("tm", None, None),
        P("tm", None, None),
        P("tm", None, None, "col"),
        P("tm", None, None, "col"),
        P("tm", None, "col"),
        P(),
    )
    return jax.shard_map(
        local,
        mesh=mesh,
        in_specs=placed,
        out_specs=(P("tm", None, "col"), P("tm", None, None, "col"), P()),
        check_vma=False,
    )
```

```python
import functools
import jax
import jax.numpy as jnp
from jax import lax
from jax.experimental import pallas as pl
from jax.experimental.pallas import tpu as pltpu
from jax.sharding import PartitionSpec as P

PARTS = 64
N = 1024
COLS = 4
ROWS = 16
BLOCK = 256
TOP = 24
GROUPS = (PARTS - TOP) // 4
F32 = jnp.float32
BF16 = jnp.bfloat16
VMEM = pl.BlockSpec(memory_space=pltpu.VMEM)


def split(value):
    high = value.astype(BF16)
    return high, (value - high.astype(F32)).astype(BF16)


def product(left, high, low):
    rows = left.shape[0]
    left_high, left_low = split(left)
    both = jnp.dot(jnp.concatenate([left_high, left_low], 0), high, preferred_element_type=F32)
    return both[:rows] + both[rows:] + jnp.dot(left_high, low, preferred_element_type=F32)


def call(body, outs, specs, operands, flops=0, limit=8, **kw):
    return pl.pallas_call(
        body,
        out_shape=outs,
        in_specs=specs,
        out_specs=[VMEM] * len(outs),
        compiler_params=pltpu.CompilerParams(vmem_limit_bytes=limit << 20),
        cost_estimate=pl.CostEstimate(flops=flops, bytes_accessed=4 << 20, transcendentals=0),
        **kw,
    )(*operands)


def shape(*dims, dtype=F32):
    return jax.ShapeDtypeStruct(dims, dtype)


def when_at(test, run):
    pl.when(test(lax.axis_index("tm")))(run)


def upper_chip(at):
    return (at % 4 == 2) & (at < 4 * GROUPS)


def lower_chip(at):
    return (at % 4 == 0) & (at < 4 * GROUPS)


def moved(at):
    return (at % 8 == 2) & (at < 4 * GROUPS)


def home(k):
    return 4 * k + 2 if k % 2 == 0 else 4 * k


def is_home(at):
    return ((at % 8 == 2) | (at % 8 == 4)) & (at < 4 * GROUPS)


def tall_body(test, left_ref, bias_ref, high_ref, low_ref, out_ref):
    def run():
        out_ref[...] = product(left_ref[...], high_ref[...], low_ref[...])
        out_ref[BLOCK:, :] += bias_ref[...]

    when_at(test, run)


def tall(test, left, bias, high, low):
    (out,) = call(
        functools.partial(tall_body, test),
        [shape(BLOCK + ROWS, N)],
        [VMEM] * 4,
        (left, bias, high, low),
        6 * 272 * N * N,
    )
    return out


def pick_body(own_ref, got_ref, rows_ref, term_ref):
    def take(source):
        rows_ref[...] = source[:BLOCK, :]
        term_ref[...] = source[BLOCK:, :]

    when_at(moved, lambda: take(got_ref))
    when_at(lambda at: jnp.logical_not(moved(at)), lambda: take(own_ref))


def two_body(tests, *refs):
    count = len(tests)
    gots, (in_0, odd_0, even_0, fo, fe, oh, ol, eh, el, in_1, odd_1, even_1) = refs[:count], refs[count:]

    def step(got):
        x = got[...]
        odd = product(x, oh[...], ol[...]) + fo[...]
        in_1[...] = x
        odd_1[...] = odd
        even_1[...] = product(odd, eh[...], el[...]) + fe[...]

    for test, got in zip(tests, gots):
        when_at(test, functools.partial(step, got))


def two_steps(tests, gots, states, terms, mats):
    count = len(gots)
    return call(
        functools.partial(two_body, tests),
        [shape(ROWS, N)] * 3,
        [VMEM] * (9 + count),
        (*gots, *states, *terms, *mats),
        12 * 16 * N * N,
        input_output_aliases={count: 0, count + 1: 1, count + 2: 2},
    )


def one_body(test, got, in_0, state_0, term, high, low, in_1, state_1):
    def run():
        x = got[...]
        in_1[...] = x
        state_1[...] = product(x, high[...], low[...]) + term[...]

    when_at(test, run)


def one_step(test, got, states, term, mats):
    return call(
        functools.partial(one_body, test),
        [shape(ROWS, N)] * 2,
        [VMEM] * 6,
        (got, *states, term, *mats),
        6 * 16 * N * N,
        input_output_aliases={1: 0, 2: 1},
    )


def places():
    c = lax.axis_index("col")
    return [c, (c + 3) % COLS, (c + 1) % COLS, (c + 2) % COLS]


def place_body(b0, b1, b2, b3, high_ref, low_ref):
    def run():
        for place, block in zip(places(), (b0, b1, b2, b3)):
            high, low = split(block[...])
            at = pl.ds(pl.multiple_of(place * BLOCK, BLOCK), BLOCK)
            high_ref[at, :] = high
            low_ref[at, :] = low

    when_at(is_home, run)


def slab_body(b0, b1, b2, b3, lh, ll, rh, rl, own_ref, out_ref, x_ref, next_ref):
    for place, block in zip(places(), (b0, b1, b2, b3)):
        at = pl.ds(pl.multiple_of(place * ROWS, ROWS), ROWS)
        x_ref[at, :] = block[:ROWS, :]
        next_ref[at, :] = block[ROWS:, :]
    own = x_ref[...]
    later = next_ref[...]
    own_ref[...] = x_ref[:, pl.ds(pl.multiple_of(places()[0] * BLOCK, BLOCK), BLOCK)]
    for k in range(4):
        at = slice(k * N, k * N + N)
        out_ref[k] = product(own, lh[at, :], ll[at, :]) + product(later, rh[at, :], rl[at, :])


def finish_body(in_ref, odd_ref, even_ref, arrow_odd, arrow_even, send_ref, keep_ref, total_ref):
    send_ref[:ROWS, :] = odd_ref[...]
    send_ref[ROWS:, :] = in_ref[...]
    keep_ref[:ROWS, :] = even_ref[...]
    keep_ref[ROWS:, :] = odd_ref[...]

    def across(x, arrow):
        (x_high, x_low), (high, low) = split(x), split(arrow)
        dims = (((1,), (1,)), ((), ()))
        both = lax.dot_general(jnp.concatenate([x_high, x_low], 0), high, dims, preferred_element_type=F32)
        return both[:ROWS] + both[ROWS:] + lax.dot_general(x_high, low, dims, preferred_element_type=F32)

    total_ref[...] = across(even_ref[...], arrow_even[...]) + across(odd_ref[...], arrow_odd[...])


def choose_body(got_ref, keep_ref, out_ref):
    def take(source):
        out_ref[...] = source[...]

    when_at(lambda at: at % 2 == 1, lambda: take(got_ref))
    when_at(lambda at: at % 2 == 0, lambda: take(keep_ref))


def choose(got, keep):
    (out,) = call(choose_body, [shape(*keep.shape)], [VMEM] * 2, (got, keep))
    return out


def arrow_body(b0, b1, b2, b3, out_ref):
    for place, block in zip(places(), (b0, b1, b2, b3)):
        out_ref[:, pl.ds(pl.multiple_of(place * BLOCK, BLOCK), BLOCK)] = block[...]


def corner_body(base_ref, b0, b1, b2, b3, out_ref, rows_ref):
    for place, block in zip(places(), (b0, b1, b2, b3)):
        rows_ref[pl.ds(pl.multiple_of(place * ROWS, ROWS), ROWS), :] = block[...]
    out_ref[...] = base_ref[...] + rows_ref[...].T


def split_body(value_ref, high_ref, low_ref):
    high_ref[...], low_ref[...] = split(value_ref[...])


def halves(value):
    rows, columns = value.shape
    tile = pl.BlockSpec((BLOCK, columns), lambda i: (i, 0))
    return pl.pallas_call(
        split_body,
        grid=(rows // BLOCK,),
        out_shape=[shape(rows, columns, dtype=BF16)] * 2,
        in_specs=[tile],
        out_specs=[tile, tile],
        compiler_params=pltpu.CompilerParams(vmem_limit_bytes=8 << 20),
        cost_estimate=pl.CostEstimate(flops=2 * rows * columns, bytes_accessed=8 * rows * columns, transcendentals=0),
    )(value)


def around(value, members):
    return [lax.ppermute(value, ("tm", "col"), [(t * COLS + j, t * COLS + (j + by) % COLS) for t in members for j in range(COLS)]) for by in (1, 3, 2)]


def local(couple, free_term, slab_left, slab_right, arrow_rows, corner_base):
    c = lax.axis_index("col")
    own = couple[0]
    f = lax.dynamic_slice_in_dim(free_term[0], c * ROWS, ROWS, 0)
    groups = range(GROUPS)
    down = [(2 * j + 1, 2 * j) for j in range(PARTS // 2)]
    up = [(b, a) for a, b in down]
    inner = [(4 * k + 2, 4 * k) for k in groups]

    start = jnp.concatenate([lax.dynamic_slice_in_dim(own, c * BLOCK, BLOCK, 0), f], 0)
    start = lax.ppermute(start, "tm", [(4 * k + 3, 4 * k + 2) for k in groups])
    other = lax.ppermute(own, "tm", down)
    f_odd = lax.ppermute(f, "tm", down)
    even_mats = halves(own)
    odd_mats = halves(other)
    mats = (*odd_mats, *even_mats)
    terms = (f_odd, f)
    rows = tall(upper_chip, start, f, *even_mats)
    zero = jnp.zeros((ROWS, N), F32)
    rows, zero = lax.optimization_barrier((rows, zero))
    rows = lax.ppermute(rows, "tm", inner)

    states = (zero, zero, zero)
    chips = TOP // 2
    half = chips // 2
    got = zero
    for i in range(chips):
        device = PARTS - 2 - 2 * i
        if i:
            pairs = [(device + 2, device)]
            mate = i + half if i + half < chips else i - half
            if 0 < mate < chips:
                at = PARTS - 2 - 2 * mate
                pairs.append((at + 2, at))
            got = lax.ppermute(states[2], "tm", sorted(pairs))
        states = two_steps([lambda at, device=device: at == device], [got], states, terms, mats)
    rows, states = lax.optimization_barrier((rows, states))

    rows = tall(lower_chip, rows, f_odd, *odd_mats)
    rows = tall(lower_chip, rows, f, *even_mats)
    moved_rows = lax.ppermute(rows, "tm", [(4 * k, 4 * k + 2) for k in groups if k % 2 == 0 and k > 0])
    rows, term = call(pick_body, [shape(BLOCK, N), shape(ROWS, N)], [VMEM] * 2, (rows, moved_rows))
    others = around(rows, [home(k) for k in groups if k > 0])

    rows, slab_left, slab_right, arrow_rows = lax.optimization_barrier((rows, slab_left, slab_right, arrow_rows))
    left = halves(slab_left[0].reshape(4 * N, BLOCK))
    right = halves(slab_right[0].reshape(4 * N, BLOCK))
    arrows = [arrow_rows[0]] + around(arrow_rows[0], range(PARTS))
    (arrow,) = call(arrow_body, [shape(64, N)], [VMEM] * 4, arrows)
    arrow_odd = lax.ppermute(arrow, "tm", down)
    others, left, right, arrow, arrow_odd, states = lax.optimization_barrier((others, left, right, arrow, arrow_odd, states))
    group_mats = call(place_body, [shape(N, N, dtype=BF16)] * 2, [VMEM] * 4, (rows, *others))

    x_in, x_odd, x_even = states
    message = x_even
    for k in reversed(groups):
        source = home(k + 1) if k + 1 < GROUPS else 4 * GROUPS
        pairs = [(source, home(k))]
        mate = (k + GROUPS // 2) % GROUPS
        pairs.append((home(mate + 1) if mate + 1 < GROUPS else 4 * GROUPS, home(mate)))
        got = lax.ppermute(message, "tm", sorted(pairs))
        if k:
            x_in, message = one_step(lambda at, k=k: at == home(k), got, (x_in, message), term, group_mats)
    last = got

    got = lax.ppermute(x_in, "tm", [(4 * k, 4 * k + 2) for k in groups if k % 2 == 1])
    x_in, x_odd, x_even = two_steps(
        [
            lambda at: at == home(0),
            lambda at: (at % 8 == 6) & (at < 4 * GROUPS),
            lambda at: moved(at) & (at != home(0)),
        ],
        [last, got, x_in],
        (x_in, x_odd, x_even),
        terms,
        mats,
    )
    got = lax.ppermute(x_even, "tm", inner)
    x_in, x_odd, x_even = two_steps([lower_chip], [got], (x_in, x_odd, x_even), terms, mats)

    send, keep, total = call(
        finish_body,
        [shape(2 * ROWS, N)] * 2 + [shape(ROWS, 64)],
        [VMEM] * 5,
        (x_in, x_odd, x_even, arrow_odd, arrow),
        12 * 16 * N * 64,
    )

    def exchange(total, bit):
        return total + lax.ppermute(total, "tm", [(j, j ^ bit) for j in range(0, PARTS, 2)])

    pair = lax.ppermute(send, "tm", up)
    total = exchange(total, 2)
    total, pair = lax.optimization_barrier((total, pair))
    pair = choose(pair, keep)
    blocks = around(pair, range(PARTS))
    total = exchange(total, 4)
    total, *blocks = lax.optimization_barrier((total, *blocks))
    columns, slab = call(
        slab_body,
        [shape(64, BLOCK), shape(4, 64, BLOCK)],
        [VMEM] * 8,
        (pair, *blocks, *left, *right),
        12 * 64 * N * N,
        scratch_shapes=[pltpu.VMEM((64, N), F32)] * 2,
    )
    for bit in (8, 16, 32):
        total = exchange(total, bit)
    total = choose(lax.ppermute(total, "tm", up), total)
    totals = [total] + around(total, range(PARTS))
    (corner,) = call(corner_body, [shape(64, 64)], [VMEM] * 5, (corner_base, *totals), scratch_shapes=[pltpu.VMEM((64, 64), F32)])
    return (columns[None], slab[None], corner)


def solution(mesh):
    placed = (
        P("tm", None, None),
        P("tm", None, None),
        P("tm", None, None, "col"),
        P("tm", None, None, "col"),
        P("tm", None, "col"),
        P(),
    )
    return jax.shard_map(
        local,
        mesh=mesh,
        in_specs=placed,
        out_specs=(P("tm", None, "col"), P("tm", None, None, "col"), P()),
        check_vma=False,
    )
```

```python
import functools
import jax
import jax.numpy as jnp
from jax import lax
from jax.experimental import pallas as pl
from jax.experimental.pallas import tpu as pltpu
from jax.sharding import PartitionSpec as P

PARTS = 64
N = 1024
COLS = 4
ROWS = 16
BLOCK = 256
WIDE = N + 128
TOP = 20
GROUPS = (PARTS - TOP) // 4
F32 = jnp.float32
BF16 = jnp.bfloat16
VMEM = pl.BlockSpec(memory_space=pltpu.VMEM)


def split(value):
    high = value.astype(BF16)
    return high, (value - high.astype(F32)).astype(BF16)


def product(left, high, low):
    rows = left.shape[0]
    left_high, left_low = split(left)
    both = jnp.dot(jnp.concatenate([left_high, left_low], 0), high, preferred_element_type=F32)
    return both[:rows] + both[rows:] + jnp.dot(left_high, low, preferred_element_type=F32)


def call(body, outs, specs, operands, flops=0, limit=8, **kw):
    return pl.pallas_call(
        body,
        out_shape=outs,
        in_specs=specs,
        out_specs=[VMEM] * len(outs),
        compiler_params=pltpu.CompilerParams(vmem_limit_bytes=limit << 20),
        cost_estimate=pl.CostEstimate(flops=flops, bytes_accessed=4 << 20, transcendentals=0),
        **kw,
    )(*operands)


def shape(*dims, dtype=F32):
    return jax.ShapeDtypeStruct(dims, dtype)


def when_at(test, run):
    pl.when(test(lax.axis_index("tm")))(run)


def upper_chip(at):
    return (at % 4 == 2) & (at < 4 * GROUPS)


def lower_chip(at):
    return (at % 4 == 0) & (at < 4 * GROUPS)


def moved(at):
    return (at % 8 == 2) & (at < 4 * (GROUPS - 1))


def moves(k):
    return k % 2 == 0 and k < GROUPS - 1


def home(k):
    return 4 * k + 2 if moves(k) else 4 * k


def is_home(at):
    return moved(at) | ((at % 8 == 4) & (at < 4 * GROUPS)) | (at == home(GROUPS - 1))


def across(x, arrow):
    rows = x.shape[0]
    (x_high, x_low), (high, low) = split(x), split(arrow)
    dims = (((1,), (1,)), ((), ()))
    both = lax.dot_general(jnp.concatenate([x_high, x_low], 0), high, dims, preferred_element_type=F32)
    return both[:rows] + both[rows:] + lax.dot_general(x_high, low, dims, preferred_element_type=F32)


def first_body(left_ref, bias_ref, high_ref, low_ref, odd_arrow, even_arrow, out_ref):
    def run():
        left = left_ref[...]
        x = product(left, high_ref[...], low_ref[...])
        out_ref[:, :N] = x
        out_ref[BLOCK:, :N] += bias_ref[...]
        out_ref[:, N:] = across(left, odd_arrow[...]) + across(out_ref[:, :N], even_arrow[...])

    when_at(upper_chip, run)


def tall_body(left_ref, bias_ref, high_ref, low_ref, arrow, out_ref):
    def run():
        out_ref[:, :N] = product(left_ref[:, :N], high_ref[...], low_ref[...])
        out_ref[BLOCK:, :N] += bias_ref[...]
        out_ref[:, N:] = left_ref[:, N:] + across(out_ref[:, :N], arrow[...])

    when_at(lower_chip, run)


def tall(body, *operands):
    (out,) = call(body, [shape(BLOCK + ROWS, WIDE)], [VMEM] * len(operands), operands, 7 * 272 * N * N, 12)
    return out


def pick_body(own_ref, got_ref, rows_ref, term_ref):
    def take(source):
        rows_ref[...] = source[:BLOCK, :]
        term_ref[...] = source[BLOCK:, :]

    when_at(moved, lambda: take(got_ref))
    when_at(lambda at: jnp.logical_not(moved(at)), lambda: take(own_ref))


def follow(state, mats, bias, arrow, out_ref):
    x = product(state[:, :N], mats[0][...], mats[1][...]) + bias[...]
    out_ref[:, :N] = x
    out_ref[:, N:] = state[:, N:] + across(x, arrow[...])


def two_body(tests, *refs):
    count = len(tests)
    gots, (in_0, odd_0, even_0, fo, fe, ao, ae, oh, ol, eh, el, in_1, odd_1, even_1) = refs[:count], refs[count:]

    def step(got):
        follow(got, (oh, ol), fo, ao, odd_1)
        follow(odd_1, (eh, el), fe, ae, even_1)
        in_1[...] = got[...]

    for test, got in zip(tests, gots):
        when_at(test, functools.partial(step, got))


def two_steps(tests, gots, states, terms, mats):
    count = len(gots)
    return call(
        functools.partial(two_body, tests),
        [shape(ROWS, WIDE)] * 3,
        [VMEM] * (11 + count),
        (*gots, *states, *terms, *mats),
        13 * 16 * N * N,
        input_output_aliases={count: 0, count + 1: 1, count + 2: 2},
    )


def one_body(test, got, in_0, state_0, term, high, low, side, in_1, state_1):
    def run():
        x = got[:, :N]
        in_1[...] = got[...]
        state_1[:, :N] = product(x, high[...], low[...]) + term[:, :N]
        side_high, side_low = split(side[...])
        state_1[:, N:] = got[:, N:] + product(x, side_high, side_low) + term[:, N:]

    when_at(test, run)


def one_step(test, got, states, term, mats):
    return call(
        functools.partial(one_body, test),
        [shape(ROWS, WIDE)] * 2,
        [VMEM] * 7,
        (got, *states, term, *mats),
        7 * 16 * N * N,
        input_output_aliases={1: 0, 2: 1},
    )


def places():
    c = lax.axis_index("col")
    return [c, (c + 3) % COLS, (c + 1) % COLS, (c + 2) % COLS]


def place_body(b0, b1, b2, b3, high_ref, low_ref, side_ref):
    def run():
        for place, block in zip(places(), (b0, b1, b2, b3)):
            high, low = split(block[:, :N])
            at = pl.ds(pl.multiple_of(place * BLOCK, BLOCK), BLOCK)
            high_ref[at, :] = high
            low_ref[at, :] = low
            side_ref[at, :] = block[:, N:]

    when_at(is_home, run)


def slab_body(b0, b1, b2, b3, lh, ll, rh, rl, own_ref, out_ref, x_ref, next_ref):
    for place, block in zip(places(), (b0, b1, b2, b3)):
        at = pl.ds(pl.multiple_of(place * ROWS, ROWS), ROWS)
        x_ref[at, :] = block[:ROWS, :]
        next_ref[at, :] = block[ROWS:, :]
    own = x_ref[...]
    later = next_ref[...]
    own_ref[...] = x_ref[:, pl.ds(pl.multiple_of(places()[0] * BLOCK, BLOCK), BLOCK)]
    for k in range(4):
        at = slice(k * N, k * N + N)
        out_ref[k] = product(own, lh[at, :], ll[at, :]) + product(later, rh[at, :], rl[at, :])


def finish_body(in_ref, odd_ref, even_ref, send_ref, keep_ref):
    send_ref[:ROWS, :] = odd_ref[:, :N]
    send_ref[ROWS:, :] = in_ref[:, :N]
    keep_ref[:ROWS, :] = even_ref[:, :N]
    keep_ref[ROWS:, :] = odd_ref[:, :N]


def choose_body(test, got_ref, keep_ref, out_ref):
    def take(source):
        out_ref[...] = source[...]

    when_at(test, lambda: take(got_ref))
    when_at(lambda at: jnp.logical_not(test(at)), lambda: take(keep_ref))


def choose(test, got, keep):
    (out,) = call(functools.partial(choose_body, test), [shape(*keep.shape)], [VMEM] * 2, (got, keep))
    return out


def sum_body(message_ref, out_ref):
    out_ref[...] = message_ref[:, N:]


def arrow_body(b0, b1, b2, b3, out_ref):
    out_ref[64:, :] = jnp.zeros((64, N), F32)
    for place, block in zip(places(), (b0, b1, b2, b3)):
        out_ref[:64, pl.ds(pl.multiple_of(place * BLOCK, BLOCK), BLOCK)] = block[...]


def corner_body(base_ref, b0, b1, b2, b3, out_ref, rows_ref):
    for place, block in zip(places(), (b0, b1, b2, b3)):
        rows_ref[pl.ds(pl.multiple_of(place * ROWS, ROWS), ROWS), :] = block[...]
    out_ref[...] = base_ref[...] + rows_ref[...].T[:64, :]


def split_body(value_ref, high_ref, low_ref):
    high_ref[...], low_ref[...] = split(value_ref[...])


def halves(value):
    rows, columns = value.shape
    tile = pl.BlockSpec((BLOCK, columns), lambda i: (i, 0))
    return pl.pallas_call(
        split_body,
        grid=(rows // BLOCK,),
        out_shape=[shape(rows, columns, dtype=BF16)] * 2,
        in_specs=[tile],
        out_specs=[tile, tile],
        compiler_params=pltpu.CompilerParams(vmem_limit_bytes=8 << 20),
        cost_estimate=pl.CostEstimate(flops=2 * rows * columns, bytes_accessed=8 * rows * columns, transcendentals=0),
    )(value)


def around(value, members):
    return [lax.ppermute(value, ("tm", "col"), [(t * COLS + j, t * COLS + (j + by) % COLS) for t in members for j in range(COLS)]) for by in (1, 3, 2)]


def local(couple, free_term, slab_left, slab_right, arrow_rows, corner_base):
    c = lax.axis_index("col")
    own = couple[0]
    f = lax.dynamic_slice_in_dim(free_term[0], c * ROWS, ROWS, 0)
    groups = range(GROUPS)
    down = [(2 * j + 1, 2 * j) for j in range(PARTS // 2)]
    up = [(b, a) for a, b in down]
    inner = [(4 * k + 2, 4 * k) for k in groups]

    start = jnp.concatenate([lax.dynamic_slice_in_dim(own, c * BLOCK, BLOCK, 0), f], 0)
    start = lax.ppermute(start, "tm", [(4 * k + 3, 4 * k + 2) for k in groups])
    other = lax.ppermute(own, "tm", down)
    arrows = [arrow_rows[0]] + around(arrow_rows[0], range(PARTS))
    (arrow,) = call(arrow_body, [shape(128, N)], [VMEM] * 4, arrows)
    extra = lax.ppermute(jnp.concatenate([arrow[:64], f], 0), "tm", down)
    arrow_odd = jnp.concatenate([extra[:64], jnp.zeros((64, N), F32)], 0)
    f_odd = extra[64:]
    even_mats = halves(own)
    odd_mats = halves(other)
    mats = (*odd_mats, *even_mats)
    terms = (f_odd, f, arrow_odd, arrow)
    rows = tall(first_body, start, f, *even_mats, arrow_odd, arrow)
    zero = jnp.zeros((ROWS, WIDE), F32)
    rows, zero = lax.optimization_barrier((rows, zero))
    rows = lax.ppermute(rows, "tm", inner)

    states = (zero, zero, zero)
    chips = TOP // 2
    half = chips // 2
    got = zero
    for i in range(chips):
        device = PARTS - 2 - 2 * i
        if i:
            pairs = [(device + 2, device)]
            mate = i + half if i + half < chips else i - half
            if 0 < mate < chips:
                at = PARTS - 2 - 2 * mate
                pairs.append((at + 2, at))
            got = lax.ppermute(states[2], "tm", sorted(pairs))
        states = two_steps([lambda at, device=device: at == device], [got], states, terms, mats)
        if i == 3:
            states, slab_left, slab_right = lax.optimization_barrier((states, slab_left, slab_right))
            left = halves(slab_left[0].reshape(4 * N, BLOCK))
            right = halves(slab_right[0].reshape(4 * N, BLOCK))
            states, left, right = lax.optimization_barrier((states, left, right))
    rows, states = lax.optimization_barrier((rows, states))

    rows = tall(tall_body, rows, f_odd, *odd_mats, arrow_odd)
    rows = tall(tall_body, rows, f, *even_mats, arrow)
    moved_rows = lax.ppermute(rows, "tm", [(4 * k, 4 * k + 2) for k in groups if moves(k)])
    rows, term = call(pick_body, [shape(BLOCK, WIDE), shape(ROWS, WIDE)], [VMEM] * 2, (rows, moved_rows))
    others = around(rows, sorted(home(k) for k in groups))
    group_mats = call(
        place_body,
        [shape(N, N, dtype=BF16)] * 2 + [shape(N, 128)],
        [VMEM] * 4,
        (rows, *others),
    )

    x_in, x_odd, x_even = states
    message = x_even
    sources = [home(k + 1) if k + 1 < GROUPS else 4 * GROUPS for k in groups]
    half = (GROUPS + 1) // 2
    for k in reversed(groups):
        pairs = [(sources[k], home(k))]
        mate = k + half if k + half < GROUPS else k - half
        if 0 <= mate:
            pairs.append((sources[mate], home(mate)))
        got = lax.ppermute(message, "tm", sorted(pairs))
        x_in, message = one_step(lambda at, k=k: at == home(k), got, (x_in, message), term, group_mats)

    (total,) = call(sum_body, [shape(ROWS, 128)], [VMEM], (message,))

    def spread(total, pairs, test):
        return choose(test, lax.ppermute(total, "tm", pairs), total)

    total = spread(total, [(2, 34)], lambda at: at == 34)
    got = lax.ppermute(x_in, "tm", [(4 * k, 4 * k + 2) for k in groups if not moves(k)])
    x_in, x_odd, x_even = two_steps(
        [lambda at: upper_chip(at) & jnp.logical_not(moved(at)), moved],
        [got, x_in],
        (x_in, x_odd, x_even),
        terms,
        mats,
    )
    total, x_even = lax.optimization_barrier((total, x_even))
    got = lax.ppermute(x_even, "tm", inner)
    total = spread(total, [(2, 18), (34, 50)], lambda at: at % 32 == 18)
    x_in, x_odd, x_even = two_steps([lower_chip], [got], (x_in, x_odd, x_even), terms, mats)
    send, keep = call(finish_body, [shape(2 * ROWS, N)] * 2, [VMEM] * 3, (x_in, x_odd, x_even))
    total, send = lax.optimization_barrier((total, send))
    pair = lax.ppermute(send, "tm", up)
    total = spread(total, [(a, a + 8) for a in range(2, PARTS, 16)], lambda at: at % 16 == 10)
    total, pair = lax.optimization_barrier((total, pair))
    odd_core = lambda at: at % 2 == 1
    pair = choose(odd_core, pair, keep)
    blocks = around(pair, range(PARTS))
    total = spread(total, [(a, a + 4) for a in range(2, PARTS, 8)], lambda at: at % 8 == 6)
    total, *blocks = lax.optimization_barrier((total, *blocks))
    columns, slab = call(
        slab_body,
        [shape(64, BLOCK), shape(4, 64, BLOCK)],
        [VMEM] * 8,
        (pair, *blocks, *left, *right),
        12 * 64 * N * N,
        scratch_shapes=[pltpu.VMEM((64, N), F32)] * 2,
    )
    pairs = [(a, a + 2) for a in range(2, PARTS, 8)] + [(a, a - 6) for a in range(6, PARTS, 8)]
    total = spread(total, sorted(pairs), lambda at: at % 4 == 0)
    total = spread(total, up, odd_core)
    totals = [total] + around(total, range(PARTS))
    (corner,) = call(corner_body, [shape(64, 64)], [VMEM] * 5, (corner_base, *totals), scratch_shapes=[pltpu.VMEM((64, 128), F32)])
    return (columns[None], slab[None], corner)


def solution(mesh):
    placed = (
        P("tm", None, None),
        P("tm", None, None),
        P("tm", None, None, "col"),
        P("tm", None, None, "col"),
        P("tm", None, "col"),
        P(),
    )
    return jax.shard_map(
        local,
        mesh=mesh,
        in_specs=placed,
        out_specs=(P("tm", None, "col"), P("tm", None, None, "col"), P()),
        check_vma=False,
    )
```

```python
import functools
import jax
import jax.numpy as jnp
from jax import lax
from jax.experimental import pallas as pl
from jax.experimental.pallas import tpu as pltpu
from jax.sharding import PartitionSpec as P

PARTS = 64
N = 1024
COLS = 4
ROWS = 16
BLOCK = 256
WIDE = N + 128
TOP = 20
SPLIT = 4
BUILD = 8
GROUPS = (PARTS - TOP) // 4
F32 = jnp.float32
BF16 = jnp.bfloat16
VMEM = pl.BlockSpec(memory_space=pltpu.VMEM)


def split(value):
    high = value.astype(BF16)
    return high, (value - high.astype(F32)).astype(BF16)


def product(left, high, low):
    rows = left.shape[0]
    left_high, left_low = split(left)
    both = jnp.dot(jnp.concatenate([left_high, left_low], 0), high, preferred_element_type=F32)
    return both[:rows] + both[rows:] + jnp.dot(left_high, low, preferred_element_type=F32)


def call(body, outs, specs, operands, flops=0, limit=8, **kw):
    return pl.pallas_call(
        body,
        out_shape=outs,
        in_specs=specs,
        out_specs=[VMEM] * len(outs),
        compiler_params=pltpu.CompilerParams(vmem_limit_bytes=limit << 20),
        cost_estimate=pl.CostEstimate(flops=flops, bytes_accessed=4 << 20, transcendentals=0),
        **kw,
    )(*operands)


def shape(*dims, dtype=F32):
    return jax.ShapeDtypeStruct(dims, dtype)


def when_at(test, run):
    pl.when(test(lax.axis_index("tm")))(run)


def upper_chip(at):
    return (at % 4 == 2) & (at < 4 * GROUPS)


def lower_chip(at):
    return (at % 4 == 0) & (at < 4 * GROUPS)


def moved(at):
    return (at % 8 == 2) & (at < 4 * (GROUPS - 1))


def moves(k):
    return k % 2 == 0 and k < GROUPS - 1


def home(k):
    return 4 * k + 2 if moves(k) else 4 * k


def is_home(at):
    return moved(at) | ((at % 8 == 4) & (at < 4 * GROUPS)) | (at == home(GROUPS - 1))


def first_body(left_ref, bias_ref, high_ref, low_ref, odd_high, odd_low, even_high, even_low, out_ref):
    def run():
        left = left_ref[...]
        x = product(left, high_ref[...], low_ref[...])
        out_ref[:, :N] = x
        out_ref[BLOCK:, :N] += bias_ref[...]
        out_ref[:, N:] = product(left, odd_high[...], odd_low[...]) + product(out_ref[:, :N], even_high[...], even_low[...])

    when_at(upper_chip, run)


def tall_body(left_ref, bias_ref, high_ref, low_ref, arrow_high, arrow_low, out_ref):
    def run():
        out_ref[:, :N] = product(left_ref[:, :N], high_ref[...], low_ref[...])
        out_ref[BLOCK:, :N] += bias_ref[...]
        out_ref[:, N:] = left_ref[:, N:] + product(out_ref[:, :N], arrow_high[...], arrow_low[...])

    when_at(lower_chip, run)


def tall(body, *operands):
    (out,) = call(body, [shape(BLOCK + ROWS, WIDE)], [VMEM] * len(operands), operands, 7 * 272 * N * N, 12)
    return out


def pick_body(own_ref, got_ref, rows_ref, term_ref):
    def take(source):
        rows_ref[...] = source[:BLOCK, :]
        term_ref[...] = source[BLOCK:, :]

    when_at(moved, lambda: take(got_ref))
    when_at(lambda at: jnp.logical_not(moved(at)), lambda: take(own_ref))


def follow(state, mats, bias, arrow, out_ref):
    x = product(state[:, :N], mats[0][...], mats[1][...]) + bias[...]
    out_ref[:, :N] = x
    out_ref[:, N:] = state[:, N:] + product(x, arrow[0][...], arrow[1][...])


def two_body(tests, *refs):
    count = len(tests)
    gots, (in_0, odd_0, even_0, fo, fe, oah, oal, eah, eal, oh, ol, eh, el, in_1, odd_1, even_1) = refs[:count], refs[count:]

    def step(got):
        follow(got, (oh, ol), fo, (oah, oal), odd_1)
        follow(odd_1, (eh, el), fe, (eah, eal), even_1)
        in_1[...] = got[...]

    for test, got in zip(tests, gots):
        when_at(test, functools.partial(step, got))


def two_steps(tests, gots, states, terms, mats):
    count = len(gots)
    return call(
        functools.partial(two_body, tests),
        [shape(ROWS, WIDE)] * 3,
        [VMEM] * (13 + count),
        (*gots, *states, *terms, *mats),
        13 * 16 * N * N,
        input_output_aliases={count: 0, count + 1: 1, count + 2: 2},
    )


def one_body(test, got, in_0, state_0, term, high, low, side, in_1, state_1):
    def run():
        x = got[:, :N]
        in_1[...] = got[...]
        state_1[:, :N] = product(x, high[...], low[...]) + term[:, :N]
        side_high, side_low = split(side[...])
        state_1[:, N:] = got[:, N:] + product(x, side_high, side_low) + term[:, N:]

    when_at(test, run)


def one_step(test, got, states, term, mats):
    return call(
        functools.partial(one_body, test),
        [shape(ROWS, WIDE)] * 2,
        [VMEM] * 7,
        (got, *states, term, *mats),
        7 * 16 * N * N,
        input_output_aliases={1: 0, 2: 1},
    )


def places():
    c = lax.axis_index("col")
    return [c, (c + 3) % COLS, (c + 1) % COLS, (c + 2) % COLS]


def place_body(b0, b1, b2, b3, high_ref, low_ref, side_ref):
    def run():
        for place, block in zip(places(), (b0, b1, b2, b3)):
            high, low = split(block[:, :N])
            at = pl.ds(pl.multiple_of(place * BLOCK, BLOCK), BLOCK)
            high_ref[at, :] = high
            low_ref[at, :] = low
            side_ref[at, :] = block[:, N:]

    when_at(is_home, run)


def slab_body(b0, b1, b2, b3, lh, ll, rh, rl, own_ref, out_ref, x_ref, next_ref):
    for place, block in zip(places(), (b0, b1, b2, b3)):
        at = pl.ds(pl.multiple_of(place * ROWS, ROWS), ROWS)
        x_ref[at, :] = block[:ROWS, :]
        next_ref[at, :] = block[ROWS:, :]
    own = x_ref[...]
    later = next_ref[...]
    own_ref[...] = x_ref[:, pl.ds(pl.multiple_of(places()[0] * BLOCK, BLOCK), BLOCK)]
    for k in range(4):
        at = slice(k * N, k * N + N)
        out_ref[k] = product(own, lh[at, :], ll[at, :]) + product(later, rh[at, :], rl[at, :])


def finish_body(in_ref, odd_ref, even_ref, send_ref, keep_ref):
    send_ref[:ROWS, :] = odd_ref[:, :N]
    send_ref[ROWS:, :] = in_ref[:, :N]
    keep_ref[:ROWS, :] = even_ref[:, :N]
    keep_ref[ROWS:, :] = odd_ref[:, :N]


def choose_body(test, got_ref, keep_ref, out_ref):
    def take(source):
        out_ref[...] = source[...]

    when_at(test, lambda: take(got_ref))
    when_at(lambda at: jnp.logical_not(test(at)), lambda: take(keep_ref))


def choose(test, got, keep):
    (out,) = call(functools.partial(choose_body, test), [shape(*keep.shape)], [VMEM] * 2, (got, keep))
    return out


def sum_body(message_ref, out_ref):
    out_ref[...] = message_ref[:, N:]


def arrow_body(b0, b1, b2, b3, odd_high, odd_low, even_high, even_low, even_ref, odd_ref):
    def run():
        for ref in (even_ref, odd_ref):
            ref[64:, :] = jnp.zeros((64, N), F32)
        for place, block in zip(places(), (b0, b1, b2, b3)):
            at = pl.ds(pl.multiple_of(place * BLOCK, BLOCK), BLOCK)
            even_ref[:64, at] = block[:64, :]
            odd_ref[:64, at] = block[64:, :]
        odd_high[...], odd_low[...] = split(odd_ref[...].T)
        even_high[...], even_low[...] = split(even_ref[...].T)

    when_at(lambda at: at % 2 == 0, run)


def corner_body(base_ref, b0, b1, b2, b3, out_ref, rows_ref):
    for place, block in zip(places(), (b0, b1, b2, b3)):
        rows_ref[pl.ds(pl.multiple_of(place * ROWS, ROWS), ROWS), :] = block[...]
    out_ref[...] = base_ref[...] + rows_ref[...].T[:64, :]


def split_body(value_ref, high_ref, low_ref):
    high_ref[...], low_ref[...] = split(value_ref[...])


def halves(value, step=BLOCK):
    rows, columns = value.shape
    tile = pl.BlockSpec((step, columns), lambda i: (i, 0))
    return pl.pallas_call(
        split_body,
        grid=(rows // step,),
        out_shape=[shape(rows, columns, dtype=BF16)] * 2,
        in_specs=[tile],
        out_specs=[tile, tile],
        compiler_params=pltpu.CompilerParams(vmem_limit_bytes=8 << 20),
        cost_estimate=pl.CostEstimate(flops=2 * rows * columns, bytes_accessed=8 * rows * columns, transcendentals=0),
    )(value)


def around(value, members):
    return [lax.ppermute(value, ("tm", "col"), [(t * COLS + j, t * COLS + (j + by) % COLS) for t in members for j in range(COLS)]) for by in (1, 3, 2)]


def local(couple, free_term, slab_left, slab_right, arrow_rows, corner_base):
    c = lax.axis_index("col")
    own = couple[0]
    f = lax.dynamic_slice_in_dim(free_term[0], c * ROWS, ROWS, 0)
    groups = range(GROUPS)
    down = [(2 * j + 1, 2 * j) for j in range(PARTS // 2)]
    up = [(b, a) for a, b in down]
    inner = [(4 * k + 2, 4 * k) for k in groups]

    evens = range(0, PARTS, 2)
    arrow = arrow_rows[0]
    arrow_odd = lax.ppermute(arrow, "tm", down)
    other = lax.ppermute(own, "tm", down)
    start = jnp.concatenate([lax.dynamic_slice_in_dim(own, c * BLOCK, BLOCK, 0), f], 0)
    start = lax.ppermute(start, "tm", [(4 * k + 3, 4 * k + 2) for k in groups])
    arrow = jnp.concatenate([arrow, arrow_odd], 0)
    others = around(arrow, evens)
    f_odd = lax.ppermute(f, "tm", down)
    even_mats = halves(own)
    odd_mats = halves(other, 128)
    others, f_odd, even_mats, odd_mats = lax.optimization_barrier((others, f_odd, even_mats, odd_mats))
    arrows = call(
        arrow_body,
        [shape(N, 128, dtype=BF16)] * 4,
        [VMEM] * 4,
        (arrow, *others),
        scratch_shapes=[pltpu.VMEM((128, N), F32)] * 2,
    )
    odd_arrow, even_arrow = arrows[:2], arrows[2:]
    mats = (*odd_mats, *even_mats)
    terms = (f_odd, f, *odd_arrow, *even_arrow)
    rows = tall(first_body, start, f, *even_mats, *odd_arrow, *even_arrow)
    zero = jnp.zeros((ROWS, WIDE), F32)
    rows, zero = lax.optimization_barrier((rows, zero))
    rows = lax.ppermute(rows, "tm", inner)

    states = (zero, zero, zero)
    chips = TOP // 2
    half = chips // 2
    got = zero
    for i in range(chips):
        device = PARTS - 2 - 2 * i
        if i:
            pairs = [(device + 2, device)]
            mate = i + half if i + half < chips else i - half
            if 0 < mate < chips:
                at = PARTS - 2 - 2 * mate
                pairs.append((at + 2, at))
            got = lax.ppermute(states[2], "tm", sorted(pairs))
        if i == SPLIT:
            _, slab_left, slab_right = lax.optimization_barrier((states[0], slab_left, slab_right))
            left = halves(slab_left[0].reshape(4 * N, BLOCK))
            right = halves(slab_right[0].reshape(4 * N, BLOCK))
            got, left, right = lax.optimization_barrier((got, left, right))
        if i == BUILD:
            rows, _ = lax.optimization_barrier((rows, states[0]))
            rows = tall(tall_body, rows, f_odd, *odd_mats, *odd_arrow)
            rows = tall(tall_body, rows, f, *even_mats, *even_arrow)
            moved_rows = lax.ppermute(rows, "tm", [(4 * k, 4 * k + 2) for k in groups if moves(k)])
            rows, term = call(pick_body, [shape(BLOCK, WIDE), shape(ROWS, WIDE)], [VMEM] * 2, (rows, moved_rows))
            others = around(rows, sorted(home(k) for k in groups))
            got, rows, others = lax.optimization_barrier((got, rows, others))
        states = two_steps([lambda at, device=device: at == device], [got], states, terms, mats)
    group_mats = call(
        place_body,
        [shape(N, N, dtype=BF16)] * 2 + [shape(N, 128)],
        [VMEM] * 4,
        (rows, *others),
    )

    x_in, x_odd, x_even = states
    message = x_even
    sources = [home(k + 1) if k + 1 < GROUPS else 4 * GROUPS for k in groups]
    half = (GROUPS + 1) // 2
    for k in reversed(groups):
        pairs = [(sources[k], home(k))]
        mate = k + half if k + half < GROUPS else k - half
        if 0 <= mate:
            pairs.append((sources[mate], home(mate)))
        got = lax.ppermute(message, "tm", sorted(pairs))
        x_in, message = one_step(lambda at, k=k: at == home(k), got, (x_in, message), term, group_mats)

    (total,) = call(sum_body, [shape(ROWS, 128)], [VMEM], (message,))

    def spread(total, pairs, test):
        return choose(test, lax.ppermute(total, "tm", pairs), total)

    total = spread(total, [(2, 34)], lambda at: at == 34)
    got = lax.ppermute(x_in, "tm", [(4 * k, 4 * k + 2) for k in groups if not moves(k)])
    x_in, x_odd, x_even = two_steps(
        [lambda at: upper_chip(at) & jnp.logical_not(moved(at)), moved],
        [got, x_in],
        (x_in, x_odd, x_even),
        terms,
        mats,
    )
    total, x_even = lax.optimization_barrier((total, x_even))
    got = lax.ppermute(x_even, "tm", inner)
    total = spread(total, [(2, 18), (34, 50)], lambda at: at % 32 == 18)
    x_in, x_odd, x_even = two_steps([lower_chip], [got], (x_in, x_odd, x_even), terms, mats)
    send, keep = call(finish_body, [shape(2 * ROWS, N)] * 2, [VMEM] * 3, (x_in, x_odd, x_even))
    total, send = lax.optimization_barrier((total, send))
    pair = lax.ppermute(send, "tm", up)
    total = spread(total, [(a, a + 8) for a in range(2, PARTS, 16)], lambda at: at % 16 == 10)
    total, pair = lax.optimization_barrier((total, pair))
    odd_core = lambda at: at % 2 == 1
    pair = choose(odd_core, pair, keep)
    blocks = around(pair, range(PARTS))
    total = spread(total, [(a, a + 4) for a in range(2, PARTS, 8)], lambda at: at % 8 == 6)
    total, *blocks = lax.optimization_barrier((total, *blocks))
    columns, slab = call(
        slab_body,
        [shape(64, BLOCK), shape(4, 64, BLOCK)],
        [VMEM] * 8,
        (pair, *blocks, *left, *right),
        12 * 64 * N * N,
        scratch_shapes=[pltpu.VMEM((64, N), F32)] * 2,
    )
    pairs = [(a, a + 2) for a in range(2, PARTS, 8)] + [(a, a - 6) for a in range(6, PARTS, 8)]
    total = spread(total, sorted(pairs), lambda at: at % 4 == 0)
    total = spread(total, up, odd_core)
    totals = [total] + around(total, range(PARTS))
    (corner,) = call(corner_body, [shape(64, 64)], [VMEM] * 5, (corner_base, *totals), scratch_shapes=[pltpu.VMEM((64, 128), F32)])
    return (columns[None], slab[None], corner)


def solution(mesh):
    placed = (
        P("tm", None, None),
        P("tm", None, None),
        P("tm", None, None, "col"),
        P("tm", None, None, "col"),
        P("tm", None, "col"),
        P(),
    )
    return jax.shard_map(
        local,
        mesh=mesh,
        in_specs=placed,
        out_specs=(P("tm", None, "col"), P("tm", None, None, "col"), P()),
        check_vma=False,
    )
```

```python
import functools
import jax
import jax.numpy as jnp
from jax import lax
from jax.experimental import pallas as pl
from jax.experimental.pallas import tpu as pltpu
from jax.sharding import PartitionSpec as P

PARTS = 64
N = 1024
COLS = 4
ROWS = 16
BLOCK = 256
WIDE = N + 128
TOP = 16
SPLIT = 4
BUILD = 7
KEPT = 10
GROUPS = (PARTS - TOP) // 4
F32 = jnp.float32
BF16 = jnp.bfloat16
VMEM = pl.BlockSpec(memory_space=pltpu.VMEM)


def split(value):
    high = value.astype(BF16)
    return high, (value - high.astype(F32)).astype(BF16)


def product(left, high, low):
    rows = left.shape[0]
    left_high, left_low = split(left)
    both = jnp.dot(jnp.concatenate([left_high, left_low], 0), high, preferred_element_type=F32)
    return both[:rows] + both[rows:] + jnp.dot(left_high, low, preferred_element_type=F32)


def call(body, outs, specs, operands, flops=0, limit=8, **kw):
    return pl.pallas_call(
        body,
        out_shape=outs,
        in_specs=specs,
        out_specs=[VMEM] * len(outs),
        compiler_params=pltpu.CompilerParams(vmem_limit_bytes=limit << 20),
        cost_estimate=pl.CostEstimate(flops=flops, bytes_accessed=4 << 20, transcendentals=0),
        **kw,
    )(*operands)


def shape(*dims, dtype=F32):
    return jax.ShapeDtypeStruct(dims, dtype)


def when_at(test, run):
    pl.when(test(lax.axis_index("tm")))(run)


def upper_chip(at):
    return (at % 4 == 2) & (at < 4 * GROUPS)


def lower_chip(at):
    return (at % 4 == 0) & (at < 4 * GROUPS)


def moved(at):
    return (at % 8 == 2) & (at < 4 * KEPT)


def moves(k):
    return k % 2 == 0 and k < KEPT


def home(k):
    return 4 * k + 2 if moves(k) else 4 * k


def is_home(at):
    return moved(at) | ((at % 8 == 4) & (at < 4 * GROUPS)) | ((at % 8 == 0) & (at >= 4 * KEPT) & (at < 4 * GROUPS))


def first_body(left_ref, bias_ref, high_ref, low_ref, odd_high, odd_low, even_high, even_low, out_ref):
    def run():
        left = left_ref[...]
        x = product(left, high_ref[...], low_ref[...])
        out_ref[:, :N] = x
        out_ref[BLOCK:, :N] += bias_ref[...]
        out_ref[:, N:] = product(left, odd_high[...], odd_low[...]) + product(out_ref[:, :N], even_high[...], even_low[...])

    when_at(upper_chip, run)


def tall_body(left_ref, bias_ref, high_ref, low_ref, arrow_high, arrow_low, out_ref):
    def run():
        out_ref[:, :N] = product(left_ref[:, :N], high_ref[...], low_ref[...])
        out_ref[BLOCK:, :N] += bias_ref[...]
        out_ref[:, N:] = left_ref[:, N:] + product(out_ref[:, :N], arrow_high[...], arrow_low[...])

    when_at(lower_chip, run)


def tall(body, *operands):
    (out,) = call(body, [shape(BLOCK + ROWS, WIDE)], [VMEM] * len(operands), operands, 7 * 272 * N * N, 12)
    return out


def pick_body(own_ref, got_ref, rows_ref, term_ref):
    def take(source):
        rows_ref[...] = source[:BLOCK, :]
        term_ref[...] = source[BLOCK:, :]

    when_at(moved, lambda: take(got_ref))
    when_at(lambda at: jnp.logical_not(moved(at)), lambda: take(own_ref))


def follow(state, mats, bias, arrow, out_ref):
    x = product(state[:, :N], mats[0][...], mats[1][...]) + bias[...]
    out_ref[:, :N] = x
    out_ref[:, N:] = state[:, N:] + product(x, arrow[0][...], arrow[1][...])


def two_body(tests, *refs):
    count = len(tests)
    gots, (in_0, odd_0, even_0, fo, fe, oah, oal, eah, eal, oh, ol, eh, el, in_1, odd_1, even_1) = refs[:count], refs[count:]

    def step(got):
        follow(got, (oh, ol), fo, (oah, oal), odd_1)
        follow(odd_1, (eh, el), fe, (eah, eal), even_1)
        in_1[...] = got[...]

    for test, got in zip(tests, gots):
        when_at(test, functools.partial(step, got))


def two_steps(tests, gots, states, terms, mats):
    count = len(gots)
    return call(
        functools.partial(two_body, tests),
        [shape(ROWS, WIDE)] * 3,
        [VMEM] * (13 + count),
        (*gots, *states, *terms, *mats),
        13 * 16 * N * N,
        input_output_aliases={count: 0, count + 1: 1, count + 2: 2},
    )


def one_body(test, got, in_0, state_0, term, high, low, side, in_1, state_1):
    def run():
        x = got[:, :N]
        in_1[...] = got[...]
        state_1[:, :N] = product(x, high[...], low[...]) + term[:, :N]
        side_high, side_low = split(side[...])
        state_1[:, N:] = got[:, N:] + product(x, side_high, side_low) + term[:, N:]

    when_at(test, run)


def one_step(test, got, states, term, mats):
    return call(
        functools.partial(one_body, test),
        [shape(ROWS, WIDE)] * 2,
        [VMEM] * 7,
        (got, *states, term, *mats),
        7 * 16 * N * N,
        input_output_aliases={1: 0, 2: 1},
    )


def places():
    c = lax.axis_index("col")
    return [c, (c + 3) % COLS, (c + 1) % COLS, (c + 2) % COLS]


def place_body(b0, b1, b2, b3, high_ref, low_ref, side_ref):
    def run():
        for place, block in zip(places(), (b0, b1, b2, b3)):
            high, low = split(block[:, :N])
            at = pl.ds(pl.multiple_of(place * BLOCK, BLOCK), BLOCK)
            high_ref[at, :] = high
            low_ref[at, :] = low
            side_ref[at, :] = block[:, N:]

    when_at(is_home, run)


def slab_body(b0, b1, b2, b3, lh, ll, rh, rl, own_ref, out_ref, x_ref, next_ref):
    for place, block in zip(places(), (b0, b1, b2, b3)):
        at = pl.ds(pl.multiple_of(place * ROWS, ROWS), ROWS)
        x_ref[at, :] = block[:ROWS, :]
        next_ref[at, :] = block[ROWS:, :]
    own = x_ref[...]
    later = next_ref[...]
    own_ref[...] = x_ref[:, pl.ds(pl.multiple_of(places()[0] * BLOCK, BLOCK), BLOCK)]
    for k in range(4):
        at = slice(k * N, k * N + N)
        out_ref[k] = product(own, lh[at, :], ll[at, :]) + product(later, rh[at, :], rl[at, :])


def finish_body(in_ref, odd_ref, even_ref, send_ref, keep_ref):
    send_ref[:ROWS, :] = odd_ref[:, :N]
    send_ref[ROWS:, :] = in_ref[:, :N]
    keep_ref[:ROWS, :] = even_ref[:, :N]
    keep_ref[ROWS:, :] = odd_ref[:, :N]


def choose_body(test, got_ref, keep_ref, out_ref):
    def take(source):
        out_ref[...] = source[...]

    when_at(test, lambda: take(got_ref))
    when_at(lambda at: jnp.logical_not(test(at)), lambda: take(keep_ref))


def choose(test, got, keep):
    (out,) = call(functools.partial(choose_body, test), [shape(*keep.shape)], [VMEM] * 2, (got, keep))
    return out


def sum_body(message_ref, out_ref):
    out_ref[...] = message_ref[:, N:]


def gather_body(b0, b1, b2, b3, f_ref, out_ref):
    for place, block in zip(places(), (b0, b1, b2, b3)):
        out_ref[:64, pl.ds(pl.multiple_of(place * BLOCK, BLOCK), BLOCK)] = block[...]
    out_ref[64:, :] = f_ref[...]


def arrow_body(odd_in, even_in, odd_high, odd_low, even_high, even_low, f_ref, rows_ref):
    def run():
        for source, high, low in ((odd_in, odd_high, odd_low), (even_in, even_high, even_low)):
            rows_ref[:64, :] = source[:64, :]
            rows_ref[64:, :] = jnp.zeros((64, N), F32)
            high[...], low[...] = split(rows_ref[...].T)
        f_ref[...] = odd_in[64:, :]

    when_at(lambda at: at % 2 == 0, run)


def whole_body(value_ref, high_ref, low_ref):
    @pl.loop(0, N // 64)
    def _(i):
        at = pl.ds(pl.multiple_of(i * 64, 64), 64)
        high_ref[at, :], low_ref[at, :] = split(value_ref[at, :])


def whole(value):
    return call(whole_body, [shape(N, N, dtype=BF16)] * 2, [VMEM], (value,), 2 * N * N)


def corner_body(base_ref, b0, b1, b2, b3, out_ref, rows_ref):
    for place, block in zip(places(), (b0, b1, b2, b3)):
        rows_ref[pl.ds(pl.multiple_of(place * ROWS, ROWS), ROWS), :] = block[...]
    out_ref[...] = base_ref[...] + rows_ref[...].T[:64, :]


def split_body(value_ref, high_ref, low_ref):
    high_ref[...], low_ref[...] = split(value_ref[...])


def halves(value, step=BLOCK):
    rows, columns = value.shape
    tile = pl.BlockSpec((step, columns), lambda i: (i, 0))
    return pl.pallas_call(
        split_body,
        grid=(rows // step,),
        out_shape=[shape(rows, columns, dtype=BF16)] * 2,
        in_specs=[tile],
        out_specs=[tile, tile],
        compiler_params=pltpu.CompilerParams(vmem_limit_bytes=8 << 20),
        cost_estimate=pl.CostEstimate(flops=2 * rows * columns, bytes_accessed=8 * rows * columns, transcendentals=0),
    )(value)


def around(value, members):
    return [lax.ppermute(value, ("tm", "col"), [(t * COLS + j, t * COLS + (j + by) % COLS) for t in members for j in range(COLS)]) for by in (1, 3, 2)]


def local(couple, free_term, slab_left, slab_right, arrow_rows, corner_base):
    c = lax.axis_index("col")
    own = couple[0]
    f = lax.dynamic_slice_in_dim(free_term[0], c * ROWS, ROWS, 0)
    groups = range(GROUPS)
    down = [(2 * j + 1, 2 * j) for j in range(PARTS // 2)]
    up = [(b, a) for a, b in down]
    inner = [(4 * k + 2, 4 * k) for k in groups]

    other = lax.ppermute(own, "tm", down)
    start = jnp.concatenate([lax.dynamic_slice_in_dim(own, c * BLOCK, BLOCK, 0), f], 0)
    start = lax.ppermute(start, "tm", [(4 * k + 3, 4 * k + 2) for k in groups])
    arrow = arrow_rows[0]
    others = around(arrow, range(PARTS))
    even_mats = whole(own)
    odd_mats = whole(other)
    others, even_mats, odd_mats = lax.optimization_barrier((others, even_mats, odd_mats))
    (arrow,) = call(gather_body, [shape(64 + ROWS, N)], [VMEM] * 5, (arrow, *others, f))
    arrows = call(
        arrow_body,
        [shape(N, 128, dtype=BF16)] * 4 + [shape(ROWS, N)],
        [VMEM] * 2,
        (lax.ppermute(arrow, "tm", down), arrow),
        scratch_shapes=[pltpu.VMEM((128, N), F32)],
    )
    odd_arrow, even_arrow, f_odd = arrows[:2], arrows[2:4], arrows[4]
    mats = (*odd_mats, *even_mats)
    terms = (f_odd, f, *odd_arrow, *even_arrow)
    rows = tall(first_body, start, f, *even_mats, *odd_arrow, *even_arrow)
    zero = jnp.zeros((ROWS, WIDE), F32)
    rows, zero = lax.optimization_barrier((rows, zero))
    rows = lax.ppermute(rows, "tm", inner)

    states = (zero, zero, zero)
    chips = TOP // 2
    half = chips // 2
    got = zero
    for i in range(chips):
        device = PARTS - 2 - 2 * i
        if i:
            pairs = [(device + 2, device)]
            mate = i + half if i + half < chips else i - half
            if 0 < mate < chips:
                at = PARTS - 2 - 2 * mate
                pairs.append((at + 2, at))
            got = lax.ppermute(states[2], "tm", sorted(pairs))
        if i == SPLIT:
            _, slab_left, slab_right = lax.optimization_barrier((states[0], slab_left, slab_right))
            left = halves(slab_left[0].reshape(4 * N, BLOCK))
            right = halves(slab_right[0].reshape(4 * N, BLOCK))
            got, left, right = lax.optimization_barrier((got, left, right))
        if i == BUILD:
            rows, _ = lax.optimization_barrier((rows, states[0]))
            rows = tall(tall_body, rows, f_odd, *odd_mats, *odd_arrow)
            rows = tall(tall_body, rows, f, *even_mats, *even_arrow)
            moved_rows = lax.ppermute(rows, "tm", [(4 * k, 4 * k + 2) for k in groups if moves(k)])
            rows, term = call(pick_body, [shape(BLOCK, WIDE), shape(ROWS, WIDE)], [VMEM] * 2, (rows, moved_rows))
            others = around(rows, sorted(home(k) for k in groups))
            got, rows, others = lax.optimization_barrier((got, rows, others))
        states = two_steps([lambda at, device=device: at == device], [got], states, terms, mats)
    group_mats = call(
        place_body,
        [shape(N, N, dtype=BF16)] * 2 + [shape(N, 128)],
        [VMEM] * 4,
        (rows, *others),
    )

    x_in, x_odd, x_even = states
    message = x_even
    sources = [home(k + 1) if k + 1 < GROUPS else 4 * GROUPS for k in groups]
    half = (GROUPS + 1) // 2
    for k in reversed(groups):
        pairs = [(sources[k], home(k))]
        mate = k + half if k + half < GROUPS else k - half
        if 0 <= mate:
            pairs.append((sources[mate], home(mate)))
        got = lax.ppermute(message, "tm", sorted(pairs))
        x_in, message = one_step(lambda at, k=k: at == home(k), got, (x_in, message), term, group_mats)

    (total,) = call(sum_body, [shape(ROWS, 128)], [VMEM], (message,))

    def spread(total, pairs, test):
        return choose(test, lax.ppermute(total, "tm", pairs), total)

    total = spread(total, [(2, 34)], lambda at: at == 34)
    got = lax.ppermute(x_in, "tm", [(4 * k, 4 * k + 2) for k in groups if not moves(k)])
    x_in, x_odd, x_even = two_steps(
        [lambda at: upper_chip(at) & jnp.logical_not(moved(at)), moved],
        [got, x_in],
        (x_in, x_odd, x_even),
        terms,
        mats,
    )
    total, x_even = lax.optimization_barrier((total, x_even))
    got = lax.ppermute(x_even, "tm", inner)
    total = spread(total, [(2, 18), (34, 50)], lambda at: at % 32 == 18)
    x_in, x_odd, x_even = two_steps([lower_chip], [got], (x_in, x_odd, x_even), terms, mats)
    send, keep = call(finish_body, [shape(2 * ROWS, N)] * 2, [VMEM] * 3, (x_in, x_odd, x_even))
    total, send = lax.optimization_barrier((total, send))
    pair = lax.ppermute(send, "tm", up)
    total = spread(total, [(a, a + 8) for a in range(2, PARTS, 16)], lambda at: at % 16 == 10)
    total, pair = lax.optimization_barrier((total, pair))
    odd_core = lambda at: at % 2 == 1
    pair = choose(odd_core, pair, keep)
    blocks = around(pair, range(PARTS))
    total = spread(total, [(a, a + 4) for a in range(2, PARTS, 8)], lambda at: at % 8 == 6)
    total, *blocks = lax.optimization_barrier((total, *blocks))
    columns, slab = call(
        slab_body,
        [shape(64, BLOCK), shape(4, 64, BLOCK)],
        [VMEM] * 8,
        (pair, *blocks, *left, *right),
        12 * 64 * N * N,
        scratch_shapes=[pltpu.VMEM((64, N), F32)] * 2,
    )
    pairs = [(a, a + 2) for a in range(2, PARTS, 8)] + [(a, a - 6) for a in range(6, PARTS, 8)]
    total = spread(total, sorted(pairs), lambda at: at % 4 == 0)
    total = spread(total, up, odd_core)
    totals = [total] + around(total, range(PARTS))
    (corner,) = call(corner_body, [shape(64, 64)], [VMEM] * 5, (corner_base, *totals), scratch_shapes=[pltpu.VMEM((64, 128), F32)])
    return (columns[None], slab[None], corner)


def solution(mesh):
    placed = (
        P("tm", None, None),
        P("tm", None, None),
        P("tm", None, None, "col"),
        P("tm", None, None, "col"),
        P("tm", None, "col"),
        P(),
    )
    return jax.shard_map(
        local,
        mesh=mesh,
        in_specs=placed,
        out_specs=(P("tm", None, "col"), P("tm", None, None, "col"), P()),
        check_vma=False,
    )
```

```python
import functools
import jax
import jax.numpy as jnp
from jax import lax
from jax.experimental import pallas as pl
from jax.experimental.pallas import tpu as pltpu
from jax.sharding import PartitionSpec as P

PARTS = 64
N = 1024
COLS = 4
ROWS = 16
BLOCK = 256
WIDE = N + 128
TOP = 16
SPLIT = 4
BUILD = 7
KEPT = 10
GROUPS = (PARTS - TOP) // 4
F32 = jnp.float32
BF16 = jnp.bfloat16
VMEM = pl.BlockSpec(memory_space=pltpu.VMEM)


def split(value):
    high = value.astype(BF16)
    return high, (value - high.astype(F32)).astype(BF16)


def product(left, high, low):
    rows = left.shape[0]
    left_high, left_low = split(left)
    both = jnp.dot(jnp.concatenate([left_high, left_low], 0), high, preferred_element_type=F32)
    return both[:rows] + both[rows:] + jnp.dot(left_high, low, preferred_element_type=F32)


def call(body, outs, specs, operands, flops=0, limit=8, **kw):
    return pl.pallas_call(
        body,
        out_shape=outs,
        in_specs=specs,
        out_specs=[VMEM] * len(outs),
        compiler_params=pltpu.CompilerParams(vmem_limit_bytes=limit << 20),
        cost_estimate=pl.CostEstimate(flops=flops, bytes_accessed=4 << 20, transcendentals=0),
        **kw,
    )(*operands)


def shape(*dims, dtype=F32):
    return jax.ShapeDtypeStruct(dims, dtype)


def when_at(test, run):
    pl.when(test(lax.axis_index("tm")))(run)


def upper_chip(at):
    return (at % 4 == 2) & (at < 4 * GROUPS)


def lower_chip(at):
    return (at % 4 == 0) & (at < 4 * GROUPS)


def moved(at):
    return (at % 8 == 2) & (at < 4 * KEPT)


def moves(k):
    return k % 2 == 0 and k < KEPT


def home(k):
    return 4 * k + 2 if moves(k) else 4 * k


def is_home(at):
    return moved(at) | ((at % 8 == 4) & (at < 4 * GROUPS)) | ((at % 8 == 0) & (at >= 4 * KEPT) & (at < 4 * GROUPS))


def first_body(left_ref, bias_ref, high_ref, low_ref, odd_high, odd_low, even_high, even_low, out_ref):
    def run():
        left = left_ref[...]
        x = product(left, high_ref[...], low_ref[...])
        out_ref[:, :N] = x
        out_ref[BLOCK:, :N] += bias_ref[...]
        out_ref[:, N:] = product(left, odd_high[...], odd_low[...]) + product(out_ref[:, :N], even_high[...], even_low[...])

    when_at(upper_chip, run)


def tall_body(left_ref, bias_ref, high_ref, low_ref, arrow_high, arrow_low, out_ref):
    def run():
        out_ref[:, :N] = product(left_ref[:, :N], high_ref[...], low_ref[...])
        out_ref[BLOCK:, :N] += bias_ref[...]
        out_ref[:, N:] = left_ref[:, N:] + product(out_ref[:, :N], arrow_high[...], arrow_low[...])

    when_at(lower_chip, run)


def tall(body, *operands):
    (out,) = call(body, [shape(BLOCK + ROWS, WIDE)], [VMEM] * len(operands), operands, 7 * 272 * N * N, 12)
    return out


def pick_body(own_ref, got_ref, rows_ref, term_ref):
    def take(source):
        rows_ref[...] = source[:BLOCK, :]
        term_ref[...] = source[BLOCK:, :]

    when_at(moved, lambda: take(got_ref))
    when_at(lambda at: jnp.logical_not(moved(at)), lambda: take(own_ref))


def follow(state, mats, bias, arrow, out_ref):
    x = product(state[:, :N], mats[0][...], mats[1][...]) + bias[...]
    out_ref[:, :N] = x
    out_ref[:, N:] = state[:, N:] + product(x, arrow[0][...], arrow[1][...])


def two_body(tests, *refs):
    count = len(tests)
    gots, (in_0, odd_0, even_0, fo, fe, oah, oal, eah, eal, oh, ol, eh, el, in_1, odd_1, even_1) = refs[:count], refs[count:]

    def step(got):
        follow(got, (oh, ol), fo, (oah, oal), odd_1)
        follow(odd_1, (eh, el), fe, (eah, eal), even_1)
        in_1[...] = got[...]

    for test, got in zip(tests, gots):
        when_at(test, functools.partial(step, got))


def two_steps(tests, gots, states, terms, mats):
    count = len(gots)
    return call(
        functools.partial(two_body, tests),
        [shape(ROWS, WIDE)] * 3,
        [VMEM] * (13 + count),
        (*gots, *states, *terms, *mats),
        13 * 16 * N * N,
        input_output_aliases={count: 0, count + 1: 1, count + 2: 2},
    )


def one_body(test, got, in_0, state_0, term, high, low, side, in_1, state_1):
    def run():
        x = got[:, :N]
        in_1[...] = got[...]
        state_1[:, :N] = product(x, high[...], low[...]) + term[:, :N]
        side_high, side_low = split(side[...])
        state_1[:, N:] = got[:, N:] + product(x, side_high, side_low) + term[:, N:]

    when_at(test, run)


def one_step(test, got, states, term, mats):
    return call(
        functools.partial(one_body, test),
        [shape(ROWS, WIDE)] * 2,
        [VMEM] * 7,
        (got, *states, term, *mats),
        7 * 16 * N * N,
        input_output_aliases={1: 0, 2: 1},
    )


def places():
    c = lax.axis_index("col")
    return [c, (c + 3) % COLS, (c + 1) % COLS, (c + 2) % COLS]


def place_body(b0, b1, b2, b3, b4, high_ref, low_ref, side_ref):
    def put(place, offset, block):
        rows = block.shape[0]
        at = pl.ds(pl.multiple_of(place * BLOCK + offset, 128), rows)
        high_ref[at, :], low_ref[at, :] = split(block[:, :N])
        side_ref[at, :] = block[:, N:]

    def run():
        own, behind, ahead, across = places()
        put(own, 0, b0)
        put(behind, 0, b1)
        put(ahead, 0, b2)
        put(across, 0, b3)
        put(across, BLOCK // 2, b4)

    when_at(is_home, run)


def slab_body(b0, b1, b2, b3, lh, ll, rh, rl, own_ref, out_ref, x_ref, next_ref):
    for place, block in zip(places(), (b0, b1, b2, b3)):
        at = pl.ds(pl.multiple_of(place * ROWS, ROWS), ROWS)
        x_ref[at, :] = block[:ROWS, :]
        next_ref[at, :] = block[ROWS:, :]
    own = x_ref[...]
    later = next_ref[...]
    own_ref[...] = x_ref[:, pl.ds(pl.multiple_of(places()[0] * BLOCK, BLOCK), BLOCK)]
    for k in range(4):
        at = slice(k * N, k * N + N)
        out_ref[k] = product(own, lh[at, :], ll[at, :]) + product(later, rh[at, :], rl[at, :])


def finish_body(in_ref, odd_ref, even_ref, send_ref, keep_ref):
    send_ref[:ROWS, :] = odd_ref[:, :N]
    send_ref[ROWS:, :] = in_ref[:, :N]
    keep_ref[:ROWS, :] = even_ref[:, :N]
    keep_ref[ROWS:, :] = odd_ref[:, :N]


def choose_body(test, got_ref, keep_ref, out_ref):
    def take(source):
        out_ref[...] = source[...]

    when_at(test, lambda: take(got_ref))
    when_at(lambda at: jnp.logical_not(test(at)), lambda: take(keep_ref))


def choose(test, got, keep):
    (out,) = call(functools.partial(choose_body, test), [shape(*keep.shape)], [VMEM] * 2, (got, keep))
    return out


def sum_body(message_ref, out_ref):
    out_ref[...] = message_ref[:, N:]


def gather_body(b0, b1, b2, b3, f_ref, out_ref):
    for place, block in zip(places(), (b0, b1, b2, b3)):
        out_ref[:64, pl.ds(pl.multiple_of(place * BLOCK, BLOCK), BLOCK)] = block[...]
    out_ref[64:, :] = f_ref[...]


def arrow_body(odd_in, even_in, odd_high, odd_low, even_high, even_low, f_ref, rows_ref):
    def run():
        for source, high, low in ((odd_in, odd_high, odd_low), (even_in, even_high, even_low)):
            rows_ref[:64, :] = source[:64, :]
            rows_ref[64:, :] = jnp.zeros((64, N), F32)
            high[...], low[...] = split(rows_ref[...].T)
        f_ref[...] = odd_in[64:, :]

    when_at(lambda at: at % 2 == 0, run)


def whole_body(value_ref, high_ref, low_ref):
    @pl.loop(0, N // 64)
    def _(i):
        at = pl.ds(pl.multiple_of(i * 64, 64), 64)
        high_ref[at, :], low_ref[at, :] = split(value_ref[at, :])


def whole(value):
    return call(whole_body, [shape(N, N, dtype=BF16)] * 2, [VMEM], (value,), 2 * N * N)


def corner_body(base_ref, b0, b1, b2, b3, out_ref, rows_ref):
    for place, block in zip(places(), (b0, b1, b2, b3)):
        rows_ref[pl.ds(pl.multiple_of(place * ROWS, ROWS), ROWS), :] = block[...]
    out_ref[...] = base_ref[...] + rows_ref[...].T[:64, :]


def split_body(value_ref, high_ref, low_ref):
    high_ref[...], low_ref[...] = split(value_ref[...])


def halves(value, step=BLOCK):
    rows, columns = value.shape
    tile = pl.BlockSpec((step, columns), lambda i: (i, 0))
    return pl.pallas_call(
        split_body,
        grid=(rows // step,),
        out_shape=[shape(rows, columns, dtype=BF16)] * 2,
        in_specs=[tile],
        out_specs=[tile, tile],
        compiler_params=pltpu.CompilerParams(vmem_limit_bytes=8 << 20),
        cost_estimate=pl.CostEstimate(flops=2 * rows * columns, bytes_accessed=8 * rows * columns, transcendentals=0),
    )(value)


def around(value, members):
    return [lax.ppermute(value, ("tm", "col"), [(t * COLS + j, t * COLS + (j + by) % COLS) for t in members for j in range(COLS)]) for by in (1, 3, 2)]


def relay(value, members):
    def shift(block, by):
        pairs = [(t * COLS + j, t * COLS + (j + by) % COLS) for t in members for j in range(COLS)]
        return lax.ppermute(block, ("tm", "col"), pairs)

    half = value.shape[0] // 2
    behind, ahead = shift(value, 1), shift(value, 3)
    return behind, ahead, shift(behind[:half], 1), shift(ahead[half:], 3)


def local(couple, free_term, slab_left, slab_right, arrow_rows, corner_base):
    c = lax.axis_index("col")
    own = couple[0]
    f = lax.dynamic_slice_in_dim(free_term[0], c * ROWS, ROWS, 0)
    groups = range(GROUPS)
    down = [(2 * j + 1, 2 * j) for j in range(PARTS // 2)]
    up = [(b, a) for a, b in down]
    inner = [(4 * k + 2, 4 * k) for k in groups]

    other = lax.ppermute(own, "tm", down)
    start = jnp.concatenate([lax.dynamic_slice_in_dim(own, c * BLOCK, BLOCK, 0), f], 0)
    start = lax.ppermute(start, "tm", [(4 * k + 3, 4 * k + 2) for k in groups])
    arrow = arrow_rows[0]
    others = around(arrow, range(PARTS))
    even_mats = whole(own)
    odd_mats = whole(other)
    others, even_mats, odd_mats = lax.optimization_barrier((others, even_mats, odd_mats))
    (arrow,) = call(gather_body, [shape(64 + ROWS, N)], [VMEM] * 5, (arrow, *others, f))
    arrows = call(
        arrow_body,
        [shape(N, 128, dtype=BF16)] * 4 + [shape(ROWS, N)],
        [VMEM] * 2,
        (lax.ppermute(arrow, "tm", down), arrow),
        scratch_shapes=[pltpu.VMEM((128, N), F32)],
    )
    odd_arrow, even_arrow, f_odd = arrows[:2], arrows[2:4], arrows[4]
    mats = (*odd_mats, *even_mats)
    terms = (f_odd, f, *odd_arrow, *even_arrow)
    rows = tall(first_body, start, f, *even_mats, *odd_arrow, *even_arrow)
    zero = jnp.zeros((ROWS, WIDE), F32)
    rows, zero = lax.optimization_barrier((rows, zero))
    rows = lax.ppermute(rows, "tm", inner)

    states = (zero, zero, zero)
    chips = TOP // 2
    half = chips // 2
    got = zero
    for i in range(chips):
        device = PARTS - 2 - 2 * i
        if i:
            pairs = [(device + 2, device)]
            mate = i + half if i + half < chips else i - half
            if 0 < mate < chips:
                at = PARTS - 2 - 2 * mate
                pairs.append((at + 2, at))
            got = lax.ppermute(states[2], "tm", sorted(pairs))
        if i == SPLIT:
            _, slab_left, slab_right = lax.optimization_barrier((states[0], slab_left, slab_right))
            left = halves(slab_left[0].reshape(4 * N, BLOCK))
            right = halves(slab_right[0].reshape(4 * N, BLOCK))
            got, left, right = lax.optimization_barrier((got, left, right))
        if i == BUILD:
            rows, _ = lax.optimization_barrier((rows, states[0]))
            rows = tall(tall_body, rows, f_odd, *odd_mats, *odd_arrow)
            rows = tall(tall_body, rows, f, *even_mats, *even_arrow)
            moved_rows = lax.ppermute(rows, "tm", [(4 * k, 4 * k + 2) for k in groups if moves(k)])
            rows, term = call(pick_body, [shape(BLOCK, WIDE), shape(ROWS, WIDE)], [VMEM] * 2, (rows, moved_rows))
            others = relay(rows, sorted(home(k) for k in groups))
            got, rows, others = lax.optimization_barrier((got, rows, others))
        states = two_steps([lambda at, device=device: at == device], [got], states, terms, mats)
    group_mats = call(
        place_body,
        [shape(N, N, dtype=BF16)] * 2 + [shape(N, 128)],
        [VMEM] * 5,
        (rows, *others),
    )

    x_in, x_odd, x_even = states
    message = x_even
    sources = [home(k + 1) if k + 1 < GROUPS else 4 * GROUPS for k in groups]
    half = (GROUPS + 1) // 2
    for k in reversed(groups):
        pairs = [(sources[k], home(k))]
        mate = k + half if k + half < GROUPS else k - half
        if 0 <= mate:
            pairs.append((sources[mate], home(mate)))
        got = lax.ppermute(message, "tm", sorted(pairs))
        x_in, message = one_step(lambda at, k=k: at == home(k), got, (x_in, message), term, group_mats)

    (total,) = call(sum_body, [shape(ROWS, 128)], [VMEM], (message,))

    def spread(total, pairs, test):
        return choose(test, lax.ppermute(total, "tm", pairs), total)

    total = spread(total, [(2, 34)], lambda at: at == 34)
    got = lax.ppermute(x_in, "tm", [(4 * k, 4 * k + 2) for k in groups if not moves(k)])
    x_in, x_odd, x_even = two_steps(
        [lambda at: upper_chip(at) & jnp.logical_not(moved(at)), moved],
        [got, x_in],
        (x_in, x_odd, x_even),
        terms,
        mats,
    )
    total, x_even = lax.optimization_barrier((total, x_even))
    got = lax.ppermute(x_even, "tm", inner)
    total = spread(total, [(2, 18), (34, 50)], lambda at: at % 32 == 18)
    x_in, x_odd, x_even = two_steps([lower_chip], [got], (x_in, x_odd, x_even), terms, mats)
    send, keep = call(finish_body, [shape(2 * ROWS, N)] * 2, [VMEM] * 3, (x_in, x_odd, x_even))
    total, send = lax.optimization_barrier((total, send))
    pair = lax.ppermute(send, "tm", up)
    total = spread(total, [(a, a + 8) for a in range(2, PARTS, 16)], lambda at: at % 16 == 10)
    total, pair = lax.optimization_barrier((total, pair))
    odd_core = lambda at: at % 2 == 1
    pair = choose(odd_core, pair, keep)
    blocks = around(pair, range(PARTS))
    total = spread(total, [(a, a + 4) for a in range(2, PARTS, 8)], lambda at: at % 8 == 6)
    total, *blocks = lax.optimization_barrier((total, *blocks))
    columns, slab = call(
        slab_body,
        [shape(64, BLOCK), shape(4, 64, BLOCK)],
        [VMEM] * 8,
        (pair, *blocks, *left, *right),
        12 * 64 * N * N,
        scratch_shapes=[pltpu.VMEM((64, N), F32)] * 2,
    )
    pairs = [(a, a + 2) for a in range(2, PARTS, 8)] + [(a, a - 6) for a in range(6, PARTS, 8)]
    total = spread(total, sorted(pairs), lambda at: at % 4 == 0)
    total = spread(total, up, odd_core)
    totals = [total] + around(total, range(PARTS))
    (corner,) = call(corner_body, [shape(64, 64)], [VMEM] * 5, (corner_base, *totals), scratch_shapes=[pltpu.VMEM((64, 128), F32)])
    return (columns[None], slab[None], corner)


def solution(mesh):
    placed = (
        P("tm", None, None),
        P("tm", None, None),
        P("tm", None, None, "col"),
        P("tm", None, None, "col"),
        P("tm", None, "col"),
        P(),
    )
    return jax.shard_map(
        local,
        mesh=mesh,
        in_specs=placed,
        out_specs=(P("tm", None, "col"), P("tm", None, None, "col"), P()),
        check_vma=False,
    )
```

```python
import functools
import jax
import jax.numpy as jnp
from jax import lax
from jax.experimental import pallas as pl
from jax.experimental.pallas import tpu as pltpu
from jax.sharding import PartitionSpec as P

PARTS = 64
N = 1024
COLS = 4
ROWS = 16
BLOCK = 256
WIDE = N + 128
TOP = 20
SPLIT = 4
BUILD = 8
KEPT = 10
ROOT = 2
GROUPS = (PARTS - TOP) // 4
F32 = jnp.float32
BF16 = jnp.bfloat16
VMEM = pl.BlockSpec(memory_space=pltpu.VMEM)


def split(value):
    high = value.astype(BF16)
    return high, (value - high.astype(F32)).astype(BF16)


def product(left, high, low):
    rows = left.shape[0]
    left_high, left_low = split(left)
    both = jnp.dot(jnp.concatenate([left_high, left_low], 0), high, preferred_element_type=F32)
    return both[:rows] + both[rows:] + jnp.dot(left_high, low, preferred_element_type=F32)


def call(body, outs, specs, operands, flops=0, limit=8, **kw):
    return pl.pallas_call(
        body,
        out_shape=outs,
        in_specs=specs,
        out_specs=[VMEM] * len(outs),
        compiler_params=pltpu.CompilerParams(vmem_limit_bytes=limit << 20),
        cost_estimate=pl.CostEstimate(flops=flops, bytes_accessed=4 << 20, transcendentals=0),
        **kw,
    )(*operands)


def shape(*dims, dtype=F32):
    return jax.ShapeDtypeStruct(dims, dtype)


def when_at(test, run):
    pl.when(test(lax.axis_index("tm")))(run)


def upper_chip(at):
    return (at % 4 == 2) & (at < 4 * GROUPS)


def lower_chip(at):
    return (at % 4 == 0) & (at < 4 * GROUPS)


def moved(at):
    return (at % 8 == 2) & (at < 4 * KEPT)


def moves(k):
    return k % 2 == 0 and k < KEPT


def home(k):
    return 4 * k + 2 if moves(k) else 4 * k


def is_home(at):
    return moved(at) | ((at % 8 == 4) & (at < 4 * GROUPS)) | ((at % 8 == 0) & (at >= 4 * KEPT) & (at < 4 * GROUPS))


def first_body(left_ref, bias_ref, high_ref, low_ref, odd_high, odd_low, even_high, even_low, out_ref):
    def run():
        left = left_ref[...]
        x = product(left, high_ref[...], low_ref[...])
        out_ref[:, :N] = x
        out_ref[BLOCK:, :N] += bias_ref[...]
        out_ref[:, N:] = product(left, odd_high[...], odd_low[...]) + product(out_ref[:, :N], even_high[...], even_low[...])

    when_at(upper_chip, run)


def tall_body(left_ref, bias_ref, high_ref, low_ref, arrow_high, arrow_low, out_ref):
    def run():
        out_ref[:, :N] = product(left_ref[:, :N], high_ref[...], low_ref[...])
        out_ref[BLOCK:, :N] += bias_ref[...]
        out_ref[:, N:] = left_ref[:, N:] + product(out_ref[:, :N], arrow_high[...], arrow_low[...])

    when_at(lower_chip, run)


def tall(body, *operands):
    (out,) = call(body, [shape(BLOCK + ROWS, WIDE)], [VMEM] * len(operands), operands, 7 * 272 * N * N, 12)
    return out


def pick_body(own_ref, got_ref, rows_ref, term_ref):
    def take(source):
        rows_ref[...] = source[:BLOCK, :]
        term_ref[...] = source[BLOCK:, :]

    when_at(moved, lambda: take(got_ref))
    when_at(lambda at: jnp.logical_not(moved(at)), lambda: take(own_ref))


def follow(state, mats, bias, arrow, out_ref):
    x = product(state[:, :N], mats[0][...], mats[1][...]) + bias[...]
    out_ref[:, :N] = x
    out_ref[:, N:] = state[:, N:] + product(x, arrow[0][...], arrow[1][...])


def two_body(tests, *refs):
    count = len(tests)
    gots, (in_0, odd_0, even_0, fo, fe, oah, oal, eah, eal, oh, ol, eh, el, in_1, odd_1, even_1) = refs[:count], refs[count:]

    def step(got):
        follow(got, (oh, ol), fo, (oah, oal), odd_1)
        follow(odd_1, (eh, el), fe, (eah, eal), even_1)
        in_1[...] = got[...]

    for test, got in zip(tests, gots):
        when_at(test, functools.partial(step, got))


def two_steps(tests, gots, states, terms, mats):
    count = len(gots)
    return call(
        functools.partial(two_body, tests),
        [shape(ROWS, WIDE)] * 3,
        [VMEM] * (13 + count),
        (*gots, *states, *terms, *mats),
        13 * 16 * N * N,
        input_output_aliases={count: 0, count + 1: 1, count + 2: 2},
    )


def one_body(test, got, in_0, state_0, term, high, low, side, in_1, state_1):
    def run():
        x = got[:, :N]
        in_1[...] = got[...]
        state_1[:, :N] = product(x, high[...], low[...]) + term[:, :N]
        side_high, side_low = split(side[:N, :])
        state_1[:, N:] = got[:, N:] + product(x, side_high, side_low) + side[N:, :]

    when_at(test, run)


def one_step(test, got, states, term, mats):
    return call(
        functools.partial(one_body, test),
        [shape(ROWS, WIDE)] * 2,
        [VMEM] * 7,
        (got, *states, term, *mats),
        7 * 16 * N * N,
        input_output_aliases={1: 0, 2: 1},
    )


def places():
    c = lax.axis_index("col")
    return [c, (c + 3) % COLS, (c + 1) % COLS, (c + 2) % COLS]


def place_body(b0, b1, b2, b3, term, high_ref, low_ref, side_ref):
    def run():
        for place, block in zip(places(), (b0, b1, b2, b3)):
            high, low = split(block[:, :N])
            at = pl.ds(pl.multiple_of(place * BLOCK, BLOCK), BLOCK)
            high_ref[at, :] = high
            low_ref[at, :] = low
            side_ref[at, :] = block[:, N:]
        side_ref[N:, :] = term[:, N:]

    when_at(is_home, run)


def adjoint_body(test, got, side_0, high, low, term, side_1):
    def run():
        got_high, got_low = split(got[:N, :])
        for i in range(N // BLOCK):
            at = slice(i * BLOCK, (i + 1) * BLOCK)
            both = jnp.dot(jnp.concatenate([high[at, :], low[at, :]], 0), got_high, preferred_element_type=F32)
            rest = jnp.dot(high[at, :], got_low, preferred_element_type=F32)
            side_1[at, :] = side_0[at, :] + both[:BLOCK] + both[BLOCK:] + rest
        side_1[N:, :] = side_0[N:, :] + got[N:, :] + product(term[:, :N], got_high, got_low)

    when_at(test, run)


def adjoint(test, got, side, high, low, term):
    (out,) = call(
        functools.partial(adjoint_body, test),
        [shape(N + ROWS, 128)],
        [VMEM] * 5,
        (got, side, high, low, term),
        6 * N * N * 128,
        input_output_aliases={1: 0},
    )
    return out


def slab_body(b0, b1, b2, b3, lh, ll, rh, rl, own_ref, out_ref, x_ref, next_ref):
    for place, block in zip(places(), (b0, b1, b2, b3)):
        at = pl.ds(pl.multiple_of(place * ROWS, ROWS), ROWS)
        x_ref[at, :] = block[:ROWS, :]
        next_ref[at, :] = block[ROWS:, :]
    own = x_ref[...]
    later = next_ref[...]
    own_ref[...] = x_ref[:, pl.ds(pl.multiple_of(places()[0] * BLOCK, BLOCK), BLOCK)]
    for k in range(4):
        at = slice(k * N, k * N + N)
        out_ref[k] = product(own, lh[at, :], ll[at, :]) + product(later, rh[at, :], rl[at, :])


def finish_body(in_ref, odd_ref, even_ref, send_ref, keep_ref):
    send_ref[:ROWS, :] = odd_ref[:, :N]
    send_ref[ROWS:, :] = in_ref[:, :N]
    keep_ref[:ROWS, :] = even_ref[:, :N]
    keep_ref[ROWS:, :] = odd_ref[:, :N]


def choose_body(test, got_ref, keep_ref, out_ref):
    def take(source):
        out_ref[...] = source[...]

    when_at(test, lambda: take(got_ref))
    when_at(lambda at: jnp.logical_not(test(at)), lambda: take(keep_ref))


def choose(test, got, keep):
    (out,) = call(functools.partial(choose_body, test), [shape(*keep.shape)], [VMEM] * 2, (got, keep))
    return out


def sum_body(message_ref, out_ref):
    out_ref[...] = message_ref[:, N:]


def gather_body(b0, b1, b2, b3, f_ref, out_ref):
    for place, block in zip(places(), (b0, b1, b2, b3)):
        out_ref[:64, pl.ds(pl.multiple_of(place * BLOCK, BLOCK), BLOCK)] = block[...]
    out_ref[64:, :] = f_ref[...]


def arrow_body(odd_in, even_in, odd_high, odd_low, even_high, even_low, f_ref, rows_ref):
    def run():
        for source, high, low in ((odd_in, odd_high, odd_low), (even_in, even_high, even_low)):
            rows_ref[:64, :] = source[:64, :]
            rows_ref[64:, :] = jnp.zeros((64, N), F32)
            high[...], low[...] = split(rows_ref[...].T)
        f_ref[...] = odd_in[64:, :]

    when_at(lambda at: at % 2 == 0, run)


def whole_body(value_ref, high_ref, low_ref):
    @pl.loop(0, N // 64)
    def _(i):
        at = pl.ds(pl.multiple_of(i * 64, 64), 64)
        high_ref[at, :], low_ref[at, :] = split(value_ref[at, :])


def whole(value):
    return call(whole_body, [shape(N, N, dtype=BF16)] * 2, [VMEM], (value,), 2 * N * N)


def corner_body(base_ref, b0, b1, b2, b3, out_ref, rows_ref):
    for place, block in zip(places(), (b0, b1, b2, b3)):
        rows_ref[pl.ds(pl.multiple_of(place * ROWS, ROWS), ROWS), :] = block[...]
    out_ref[...] = base_ref[...] + rows_ref[...].T[:64, :]


def split_body(value_ref, high_ref, low_ref):
    high_ref[...], low_ref[...] = split(value_ref[...])


def halves(value, step=BLOCK):
    rows, columns = value.shape
    tile = pl.BlockSpec((step, columns), lambda i: (i, 0))
    return pl.pallas_call(
        split_body,
        grid=(rows // step,),
        out_shape=[shape(rows, columns, dtype=BF16)] * 2,
        in_specs=[tile],
        out_specs=[tile, tile],
        compiler_params=pltpu.CompilerParams(vmem_limit_bytes=8 << 20),
        cost_estimate=pl.CostEstimate(flops=2 * rows * columns, bytes_accessed=8 * rows * columns, transcendentals=0),
    )(value)


def around(value, members):
    return [lax.ppermute(value, ("tm", "col"), [(t * COLS + j, t * COLS + (j + by) % COLS) for t in members for j in range(COLS)]) for by in (1, 3, 2)]


def local(couple, free_term, slab_left, slab_right, arrow_rows, corner_base):
    c = lax.axis_index("col")
    own = couple[0]
    f = lax.dynamic_slice_in_dim(free_term[0], c * ROWS, ROWS, 0)
    groups = range(GROUPS)
    down = [(2 * j + 1, 2 * j) for j in range(PARTS // 2)]
    up = [(b, a) for a, b in down]
    inner = [(4 * k + 2, 4 * k) for k in groups]

    other = lax.ppermute(own, "tm", down)
    start = jnp.concatenate([lax.dynamic_slice_in_dim(own, c * BLOCK, BLOCK, 0), f], 0)
    start = lax.ppermute(start, "tm", [(4 * k + 3, 4 * k + 2) for k in groups])
    arrow = arrow_rows[0]
    others = around(arrow, range(PARTS))
    even_mats = whole(own)
    odd_mats = whole(other)
    others, even_mats, odd_mats = lax.optimization_barrier((others, even_mats, odd_mats))
    (arrow,) = call(gather_body, [shape(64 + ROWS, N)], [VMEM] * 5, (arrow, *others, f))
    arrows = call(
        arrow_body,
        [shape(N, 128, dtype=BF16)] * 4 + [shape(ROWS, N)],
        [VMEM] * 2,
        (lax.ppermute(arrow, "tm", down), arrow),
        scratch_shapes=[pltpu.VMEM((128, N), F32)],
    )
    odd_arrow, even_arrow, f_odd = arrows[:2], arrows[2:4], arrows[4]
    mats = (*odd_mats, *even_mats)
    terms = (f_odd, f, *odd_arrow, *even_arrow)
    rows = tall(first_body, start, f, *even_mats, *odd_arrow, *even_arrow)
    zero = jnp.zeros((ROWS, WIDE), F32)
    rows, zero = lax.optimization_barrier((rows, zero))
    rows = lax.ppermute(rows, "tm", inner)

    states = (zero, zero, zero)
    chips = TOP // 2
    half = chips // 2
    got = zero
    for i in range(chips):
        device = PARTS - 2 - 2 * i
        if i:
            pairs = [(device + 2, device)]
            mate = i + half if i + half < chips else i - half
            if 0 < mate < chips:
                at = PARTS - 2 - 2 * mate
                pairs.append((at + 2, at))
            got = lax.ppermute(states[2], "tm", sorted(pairs))
        if i == SPLIT:
            _, slab_left, slab_right = lax.optimization_barrier((states[0], slab_left, slab_right))
            left = halves(slab_left[0].reshape(4 * N, BLOCK))
            right = halves(slab_right[0].reshape(4 * N, BLOCK))
            got, left, right = lax.optimization_barrier((got, left, right))
        if i == BUILD:
            rows, _ = lax.optimization_barrier((rows, states[0]))
            rows = tall(tall_body, rows, f_odd, *odd_mats, *odd_arrow)
            rows = tall(tall_body, rows, f, *even_mats, *even_arrow)
            moved_rows = lax.ppermute(rows, "tm", [(4 * k, 4 * k + 2) for k in groups if moves(k)])
            rows, term = call(pick_body, [shape(BLOCK, WIDE), shape(ROWS, WIDE)], [VMEM] * 2, (rows, moved_rows))
            others = around(rows, sorted(home(k) for k in groups))
            got, rows, others = lax.optimization_barrier((got, rows, others))
        states = two_steps([lambda at, device=device: at == device], [got], states, terms, mats)
    high, low, side = call(
        place_body,
        [shape(N, N, dtype=BF16)] * 2 + [shape(N + ROWS, 128)],
        [VMEM] * 5,
        (rows, *others, term),
    )
    for k in range(1, ROOT + 1):
        got = lax.ppermute(side, "tm", [(home(k - 1), home(k))])
        side = adjoint(lambda at, k=k: at == home(k), got, side, high, low, term)
    group_mats = (high, low, side)

    x_in, x_odd, x_even = states
    message = x_even
    sources = [home(k + 1) if k + 1 < GROUPS else 4 * GROUPS for k in groups]
    half = (GROUPS + 1) // 2
    for k in reversed(groups):
        pairs = [(sources[k], home(k))]
        mate = k + half if k + half < GROUPS else k - half
        if 0 <= mate:
            pairs.append((sources[mate], home(mate)))
        got = lax.ppermute(message, "tm", sorted(pairs))
        if k:
            x_in, message = one_step(lambda at, k=k: at == home(k), got, (x_in, message), term, group_mats)
    last = got

    got = lax.ppermute(x_in, "tm", [(4 * k, 4 * k + 2) for k in groups if not moves(k)])
    x_in, x_odd, x_even = two_steps(
        [
            lambda at: upper_chip(at) & jnp.logical_not(moved(at)),
            lambda at: at == home(0),
            lambda at: moved(at) & (at != home(0)),
        ],
        [got, last, x_in],
        (x_in, x_odd, x_even),
        terms,
        mats,
    )
    got = lax.ppermute(x_even, "tm", inner)
    x_in, x_odd, x_even = two_steps([lower_chip], [got], (x_in, x_odd, x_even), terms, mats)
    send, keep = call(finish_body, [shape(2 * ROWS, N)] * 2, [VMEM] * 3, (x_in, x_odd, x_even))

    message, send = lax.optimization_barrier((message, send))
    (total,) = call(sum_body, [shape(ROWS, 128)], [VMEM], (message,))

    def spread(total, pairs, test):
        return choose(test, lax.ppermute(total, "tm", sorted(pairs)), total)

    root = home(ROOT)
    ring = [(root + 8 * i) % PARTS for i in range(8)]
    for step in (4, 2, 1):
        members = range(0, 8, 2 * step)
        reached = [ring[i + step] for i in members]
        total = spread(
            total,
            [(ring[i], ring[i + step]) for i in members],
            lambda at, reached=reached: functools.reduce(jnp.logical_or, [at == r for r in reached]),
        )
    pair = lax.ppermute(send, "tm", up)
    odd_core = lambda at: at % 2 == 1
    pair = choose(odd_core, pair, keep)
    total = spread(total, [(a, a + 4) for a in range(2, PARTS, 8)], lambda at: at % 8 == 6)
    pairs = [(a, a + 2) for a in range(2, PARTS, 8)] + [(a, a - 6) for a in range(6, PARTS, 8)]
    total = spread(total, pairs, lambda at: at % 4 == 0)
    total, pair = lax.optimization_barrier((total, pair))
    blocks = around(pair, range(PARTS))
    total = spread(total, up, odd_core)
    totals = [total] + around(total, range(PARTS))
    columns, slab = call(
        slab_body,
        [shape(64, BLOCK), shape(4, 64, BLOCK)],
        [VMEM] * 8,
        (pair, *blocks, *left, *right),
        12 * 64 * N * N,
        scratch_shapes=[pltpu.VMEM((64, N), F32)] * 2,
    )
    *totals, slab = lax.optimization_barrier((*totals, slab))
    (corner,) = call(corner_body, [shape(64, 64)], [VMEM] * 5, (corner_base, *totals), scratch_shapes=[pltpu.VMEM((64, 128), F32)])
    return (columns[None], slab[None], corner)


def solution(mesh):
    placed = (
        P("tm", None, None),
        P("tm", None, None),
        P("tm", None, None, "col"),
        P("tm", None, None, "col"),
        P("tm", None, "col"),
        P(),
    )
    return jax.shard_map(
        local,
        mesh=mesh,
        in_specs=placed,
        out_specs=(P("tm", None, "col"), P("tm", None, None, "col"), P()),
        check_vma=False,
    )
```

```python
import functools
import jax
import jax.numpy as jnp
from jax import lax
from jax.experimental import pallas as pl
from jax.experimental.pallas import tpu as pltpu
from jax.sharding import PartitionSpec as P

PARTS = 64
N = 1024
COLS = 4
ROWS = 16
BLOCK = 256
WIDE = N + 128
TOP = 24
EARLY = (62, 60)
SPLIT = 5
BUILD = 9
KEPT = 10
ROOT = 2
GROUPS = (PARTS - TOP) // 4
F32 = jnp.float32
BF16 = jnp.bfloat16
VMEM = pl.BlockSpec(memory_space=pltpu.VMEM)


def split(value):
    high = value.astype(BF16)
    return high, (value - high.astype(F32)).astype(BF16)


def product(left, high, low):
    rows = left.shape[0]
    left_high, left_low = split(left)
    both = jnp.dot(jnp.concatenate([left_high, left_low], 0), high, preferred_element_type=F32)
    return both[:rows] + both[rows:] + jnp.dot(left_high, low, preferred_element_type=F32)


def call(body, outs, specs, operands, flops=0, limit=8, **kw):
    return pl.pallas_call(
        body,
        out_shape=outs,
        in_specs=specs,
        out_specs=[VMEM] * len(outs),
        compiler_params=pltpu.CompilerParams(vmem_limit_bytes=limit << 20),
        cost_estimate=pl.CostEstimate(flops=flops, bytes_accessed=4 << 20, transcendentals=0),
        **kw,
    )(*operands)


def shape(*dims, dtype=F32):
    return jax.ShapeDtypeStruct(dims, dtype)


def when_at(test, run):
    pl.when(test(lax.axis_index("tm")))(run)


def upper_chip(at):
    return (at % 4 == 2) & (at < 4 * GROUPS)


def lower_chip(at):
    return (at % 4 == 0) & (at < 4 * GROUPS)


def moved(at):
    return (at % 8 == 2) & (at < 4 * KEPT)


def moves(k):
    return k % 2 == 0 and k < KEPT


def home(k):
    return 4 * k + 2 if moves(k) else 4 * k


def is_home(at):
    return moved(at) | ((at % 8 == 4) & (at < 4 * GROUPS)) | ((at % 8 == 0) & (at >= 4 * KEPT) & (at < 4 * GROUPS))


def first_body(left_ref, bias_ref, high_ref, low_ref, odd_high, odd_low, even_high, even_low, out_ref):
    def run():
        left = left_ref[...]
        x = product(left, high_ref[...], low_ref[...])
        out_ref[:, :N] = x
        out_ref[BLOCK:, :N] += bias_ref[...]
        out_ref[:, N:] = product(left, odd_high[...], odd_low[...]) + product(out_ref[:, :N], even_high[...], even_low[...])

    when_at(upper_chip, run)


def tall_body(left_ref, bias_ref, high_ref, low_ref, arrow_high, arrow_low, out_ref):
    def run():
        out_ref[:, :N] = product(left_ref[:, :N], high_ref[...], low_ref[...])
        out_ref[BLOCK:, :N] += bias_ref[...]
        out_ref[:, N:] = left_ref[:, N:] + product(out_ref[:, :N], arrow_high[...], arrow_low[...])

    when_at(lower_chip, run)


def tall(body, *operands):
    (out,) = call(body, [shape(BLOCK + ROWS, WIDE)], [VMEM] * len(operands), operands, 7 * 272 * N * N, 12)
    return out


def pick_body(own_ref, got_ref, rows_ref, term_ref):
    def take(source):
        rows_ref[...] = source[:BLOCK, :]
        term_ref[...] = source[BLOCK:, :]

    when_at(moved, lambda: take(got_ref))
    when_at(lambda at: jnp.logical_not(moved(at)), lambda: take(own_ref))


def follow(state, mats, bias, arrow, out_ref):
    x = product(state[:, :N], mats[0][...], mats[1][...]) + bias[...]
    out_ref[:, :N] = x
    out_ref[:, N:] = state[:, N:] + product(x, arrow[0][...], arrow[1][...])


def two_body(tests, *refs):
    count = len(tests)
    gots, (in_0, odd_0, even_0, fo, fe, oah, oal, eah, eal, oh, ol, eh, el, in_1, odd_1, even_1) = refs[:count], refs[count:]

    def step(got):
        follow(got, (oh, ol), fo, (oah, oal), odd_1)
        follow(odd_1, (eh, el), fe, (eah, eal), even_1)
        in_1[...] = got[...]

    for test, got in zip(tests, gots):
        when_at(test, functools.partial(step, got))


def launch_body(fo, fe, high, low, odd_ref, even_ref):
    def run():
        for ref, x in ((odd_ref, fo[...]), (even_ref, product(fo[...], high[...], low[...]) + fe[...])):
            ref[:, :N] = x
            ref[:, N:] = jnp.zeros((ROWS, 128), F32)

    when_at(lambda at: at == EARLY[0], run)


def early_body(got, in_0, odd_0, even_0, fo, fe, oh, ol, eh, el, in_1, odd_1, even_1):
    def run():
        in_1[...] = got[...]
        x = product(got[:, :N], oh[...], ol[...]) + fo[...]
        for ref, x in ((odd_1, x), (even_1, product(x, eh[...], el[...]) + fe[...])):
            ref[:, :N] = x
            ref[:, N:] = jnp.zeros((ROWS, 128), F32)

    when_at(lambda at: at == EARLY[1], run)


def two_steps(tests, gots, states, terms, mats):
    count = len(gots)
    return call(
        functools.partial(two_body, tests),
        [shape(ROWS, WIDE)] * 3,
        [VMEM] * (13 + count),
        (*gots, *states, *terms, *mats),
        13 * 16 * N * N,
        input_output_aliases={count: 0, count + 1: 1, count + 2: 2},
    )


def one_body(test, got, in_0, state_0, term, high, low, side, in_1, state_1):
    def run():
        x = got[:, :N]
        in_1[...] = got[...]
        state_1[:, :N] = product(x, high[...], low[...]) + term[:, :N]
        side_high, side_low = split(side[:N, :])
        state_1[:, N:] = got[:, N:] + product(x, side_high, side_low) + side[N:, :]

    when_at(test, run)


def one_step(test, got, states, term, mats):
    return call(
        functools.partial(one_body, test),
        [shape(ROWS, WIDE)] * 2,
        [VMEM] * 7,
        (got, *states, term, *mats),
        7 * 16 * N * N,
        input_output_aliases={1: 0, 2: 1},
    )


def places():
    c = lax.axis_index("col")
    return [c, (c + 3) % COLS, (c + 1) % COLS, (c + 2) % COLS]


def place_body(b0, b1, b2, b3, term, odd, even, odd_high, odd_low, even_high, even_low, high_ref, low_ref, side_ref):
    def run():
        for place, block in zip(places(), (b0, b1, b2, b3)):
            high, low = split(block[:, :N])
            at = pl.ds(pl.multiple_of(place * BLOCK, BLOCK), BLOCK)
            high_ref[at, :] = high
            low_ref[at, :] = low
            side_ref[at, :] = block[:, N:]
        side_ref[N:, :] = term[:, N:]

    def early():
        total = product(odd[:, :N], odd_high[...], odd_low[...])
        side_ref[N:, :] = total + product(even[:, :N], even_high[...], even_low[...])

    when_at(is_home, run)
    when_at(lambda at: (at == EARLY[0]) | (at == EARLY[1]), early)


def adjoint_body(test, first, got, side_0, high, low, term, side_1):
    def run():
        got_high, got_low = split(got[:N, :])
        for i in range(N // BLOCK):
            at = slice(i * BLOCK, (i + 1) * BLOCK)
            both = jnp.dot(jnp.concatenate([high[at, :], low[at, :]], 0), got_high, preferred_element_type=F32)
            rest = jnp.dot(high[at, :], got_low, preferred_element_type=F32)
            side_1[at, :] = side_0[at, :] + both[:BLOCK] + both[BLOCK:] + rest
        side_1[N:, :] = side_0[N:, :] + got[N:, :] + product(term[:, :N], got_high, got_low)

    def add():
        side_1[N:, :] = side_0[N:, :] + got[N:, :]

    when_at(test, run)
    when_at(lambda at: jnp.logical_not(test(at)) & ((at == home(5)) | (at == home(3))) & first, add)


def adjoint(test, first, got, side, high, low, term):
    (out,) = call(
        functools.partial(adjoint_body, test, first),
        [shape(N + ROWS, 128)],
        [VMEM] * 5,
        (got, side, high, low, term),
        6 * N * N * 128,
        input_output_aliases={1: 0},
    )
    return out


def slab_body(b0, b1, b2, b3, lh, ll, rh, rl, base, own_ref, out_ref, corner_ref, x_ref, next_ref, rows_ref):
    for place, block in zip(places(), (b0, b1, b2, b3)):
        at = pl.ds(pl.multiple_of(place * ROWS, ROWS), ROWS)
        x_ref[at, :] = block[:ROWS, :N]
        next_ref[at, :] = block[ROWS:, :N]
        rows_ref[at, :] = block[:ROWS, N:]
    corner_ref[...] = base[...] + rows_ref[...].T[:64, :]
    own = x_ref[...]
    later = next_ref[...]
    own_ref[...] = x_ref[:, pl.ds(pl.multiple_of(places()[0] * BLOCK, BLOCK), BLOCK)]
    for k in range(4):
        at = slice(k * N, k * N + N)
        out_ref[k] = product(own, lh[at, :], ll[at, :]) + product(later, rh[at, :], rl[at, :])


def finish_body(in_ref, odd_ref, even_ref, total_ref, send_ref, keep_ref):
    for ref, own, later in ((send_ref, odd_ref, in_ref), (keep_ref, even_ref, odd_ref)):
        ref[:ROWS, :N] = own[:, :N]
        ref[ROWS:, :N] = later[:, :N]
        ref[:ROWS, N:] = total_ref[...]
        ref[ROWS:, N:] = total_ref[...]


def choose_body(test, got_ref, keep_ref, out_ref):
    def take(source):
        out_ref[...] = source[...]

    when_at(test, lambda: take(got_ref))
    when_at(lambda at: jnp.logical_not(test(at)), lambda: take(keep_ref))


def choose(test, got, keep):
    (out,) = call(functools.partial(choose_body, test), [shape(*keep.shape)], [VMEM] * 2, (got, keep))
    return out


def sum_body(message_ref, out_ref):
    out_ref[...] = message_ref[:, N:]


def gather_body(b0, b1, b2, b3, out_ref):
    for place, block in zip(places(), (b0, b1, b2, b3)):
        out_ref[:, pl.ds(pl.multiple_of(place * BLOCK, BLOCK), BLOCK)] = block[...]


def arrow_body(odd_in, even_in, odd_high, odd_low, even_high, even_low, rows_ref):
    def run():
        for source, high, low in ((odd_in, odd_high, odd_low), (even_in, even_high, even_low)):
            rows_ref[:64, :] = source[...]
            rows_ref[64:, :] = jnp.zeros((64, N), F32)
            high[...], low[...] = split(rows_ref[...].T)

    when_at(lambda at: at % 2 == 0, run)


def whole_body(value_ref, high_ref, low_ref):
    @pl.loop(0, N // 64)
    def _(i):
        at = pl.ds(pl.multiple_of(i * 64, 64), 64)
        high_ref[at, :], low_ref[at, :] = split(value_ref[at, :])


def whole(value):
    return call(whole_body, [shape(N, N, dtype=BF16)] * 2, [VMEM], (value,), 2 * N * N)


def split_body(value_ref, high_ref, low_ref):
    high_ref[...], low_ref[...] = split(value_ref[...])


def halves(value, step=BLOCK):
    rows, columns = value.shape
    tile = pl.BlockSpec((step, columns), lambda i: (i, 0))
    return pl.pallas_call(
        split_body,
        grid=(rows // step,),
        out_shape=[shape(rows, columns, dtype=BF16)] * 2,
        in_specs=[tile],
        out_specs=[tile, tile],
        compiler_params=pltpu.CompilerParams(vmem_limit_bytes=8 << 20),
        cost_estimate=pl.CostEstimate(flops=2 * rows * columns, bytes_accessed=8 * rows * columns, transcendentals=0),
    )(value)


def around(value, members):
    return [lax.ppermute(value, ("tm", "col"), [(t * COLS + j, t * COLS + (j + by) % COLS) for t in members for j in range(COLS)]) for by in (1, 3, 2)]


def hop_pairs(i):
    chips = TOP // 2
    half = chips // 2
    device = PARTS - 2 - 2 * i
    pairs = [(device + 2, device)]
    mate = i + half if i + half < chips else i - half
    if 0 < mate < chips:
        at = PARTS - 2 - 2 * mate
        pairs.append((at + 2, at))
    return sorted(pairs)


def local(couple, free_term, slab_left, slab_right, arrow_rows, corner_base):
    c = lax.axis_index("col")
    own = couple[0]
    f = lax.dynamic_slice_in_dim(free_term[0], c * ROWS, ROWS, 0)
    groups = range(GROUPS)
    down = [(2 * j + 1, 2 * j) for j in range(PARTS // 2)]
    up = [(b, a) for a, b in down]
    inner = [(4 * k + 2, 4 * k) for k in groups]

    f_odd = lax.ppermute(f, "tm", down)
    other = lax.ppermute(own, "tm", down)
    even_mats = whole(own)
    odd, even = call(launch_body, [shape(ROWS, WIDE)] * 2, [VMEM] * 4, (f_odd, f, *even_mats))
    zero = jnp.zeros((ROWS, WIDE), F32)
    states = (zero, odd, even)
    start = jnp.concatenate([lax.dynamic_slice_in_dim(own, c * BLOCK, BLOCK, 0), f], 0)
    start = lax.ppermute(start, "tm", [(4 * k + 3, 4 * k + 2) for k in groups])
    arrow, _ = lax.optimization_barrier((arrow_rows[0], even))
    others = around(arrow, range(PARTS))
    odd_mats = whole(other)
    got = lax.ppermute(even, "tm", hop_pairs(1))
    states = call(
        early_body,
        [shape(ROWS, WIDE)] * 3,
        [VMEM] * 10,
        (got, *states, f_odd, f, *odd_mats, *even_mats),
        12 * 16 * N * N,
        input_output_aliases={1: 0, 2: 1, 3: 2},
    )
    others, states = lax.optimization_barrier((others, states))
    (arrow,) = call(gather_body, [shape(64, N)], [VMEM] * 4, (arrow, *others))
    arrows = call(
        arrow_body,
        [shape(N, 128, dtype=BF16)] * 4,
        [VMEM] * 2,
        (lax.ppermute(arrow, "tm", down), arrow),
        scratch_shapes=[pltpu.VMEM((128, N), F32)],
    )
    odd_arrow, even_arrow = arrows[:2], arrows[2:]
    mats = (*odd_mats, *even_mats)
    terms = (f_odd, f, *odd_arrow, *even_arrow)
    rows = tall(first_body, start, f, *even_mats, *odd_arrow, *even_arrow)
    rows = lax.ppermute(rows, "tm", inner)

    for i in range(2, TOP // 2):
        device = PARTS - 2 - 2 * i
        got = lax.ppermute(states[2], "tm", hop_pairs(i))
        if i == SPLIT:
            _, slab_left, slab_right = lax.optimization_barrier((states[0], slab_left, slab_right))
            left = halves(slab_left[0].reshape(4 * N, BLOCK))
            right = halves(slab_right[0].reshape(4 * N, BLOCK))
            got, left, right = lax.optimization_barrier((got, left, right))
        if i == BUILD:
            rows, _ = lax.optimization_barrier((rows, states[0]))
            rows = tall(tall_body, rows, f_odd, *odd_mats, *odd_arrow)
            rows = tall(tall_body, rows, f, *even_mats, *even_arrow)
            moved_rows = lax.ppermute(rows, "tm", [(4 * k, 4 * k + 2) for k in groups if moves(k)])
            rows, term = call(pick_body, [shape(BLOCK, WIDE), shape(ROWS, WIDE)], [VMEM] * 2, (rows, moved_rows))
            others = around(rows, sorted(home(k) for k in groups))
            got, rows, others = lax.optimization_barrier((got, rows, others))
        states = two_steps([lambda at, device=device: at == device], [got], states, terms, mats)
    high, low, side = call(
        place_body,
        [shape(N, N, dtype=BF16)] * 2 + [shape(N + ROWS, 128)],
        [VMEM] * 11,
        (rows, *others, term, *states[1:], *odd_arrow, *even_arrow),
    )
    for k in range(1, ROOT + 1):
        pairs = [(home(k - 1), home(k))]
        if k == 1:
            pairs += [(EARLY[0], home(5)), (EARLY[1], home(3))]
        got = lax.ppermute(side, "tm", pairs)
        side = adjoint(lambda at, k=k: at == home(k), k == 1, got, side, high, low, term)
    group_mats = (high, low, side)

    x_in, x_odd, x_even = states
    message = x_even
    sources = [home(k + 1) if k + 1 < GROUPS else 4 * GROUPS for k in groups]
    half = (GROUPS + 1) // 2
    for k in reversed(groups):
        pairs = [(sources[k], home(k))]
        mate = k + half if k + half < GROUPS else k - half
        if 0 <= mate:
            pairs.append((sources[mate], home(mate)))
        got = lax.ppermute(message, "tm", sorted(pairs))
        if k:
            x_in, message = one_step(lambda at, k=k: at == home(k), got, (x_in, message), term, group_mats)
    last = got

    got = lax.ppermute(x_in, "tm", [(4 * k, 4 * k + 2) for k in groups if not moves(k)])
    x_in, x_odd, x_even = two_steps(
        [
            lambda at: upper_chip(at) & jnp.logical_not(moved(at)),
            lambda at: at == home(0),
            lambda at: moved(at) & (at != home(0)),
        ],
        [got, last, x_in],
        (x_in, x_odd, x_even),
        terms,
        mats,
    )
    got = lax.ppermute(x_even, "tm", inner)
    x_in, x_odd, x_even = two_steps([lower_chip], [got], (x_in, x_odd, x_even), terms, mats)

    message, x_odd, x_even = lax.optimization_barrier((message, x_odd, x_even))
    (total,) = call(sum_body, [shape(ROWS, 128)], [VMEM], (message,))

    def spread(total, pairs, test):
        return choose(test, lax.ppermute(total, "tm", sorted(pairs)), total)

    root = home(ROOT)
    ring = [(root + 8 * i) % PARTS for i in range(8)]
    for step in (4, 2, 1):
        members = range(0, 8, 2 * step)
        reached = [ring[i + step] for i in members]
        total = spread(
            total,
            [(ring[i], ring[i + step]) for i in members],
            lambda at, reached=reached: functools.reduce(jnp.logical_or, [at == r for r in reached]),
        )
    total = spread(total, [(a, a + 4) for a in range(2, PARTS, 8)], lambda at: at % 8 == 6)
    pairs = [(a, a + 2) for a in range(2, PARTS, 8)] + [(a, a - 6) for a in range(6, PARTS, 8)]
    total = spread(total, pairs, lambda at: at % 4 == 0)
    send, keep = call(finish_body, [shape(2 * ROWS, WIDE)] * 2, [VMEM] * 4, (x_in, x_odd, x_even, total))
    pair = choose(lambda at: at % 2 == 1, lax.ppermute(send, "tm", up), keep)
    blocks = [pair] + around(pair, range(PARTS))
    columns, slab, corner = call(
        slab_body,
        [shape(64, BLOCK), shape(4, 64, BLOCK), shape(64, 64)],
        [VMEM] * 9,
        (*blocks, *left, *right, corner_base),
        12 * 64 * N * N,
        scratch_shapes=[pltpu.VMEM((64, N), F32)] * 2 + [pltpu.VMEM((64, 128), F32)],
    )
    return (columns[None], slab[None], corner)


def solution(mesh):
    placed = (
        P("tm", None, None),
        P("tm", None, None),
        P("tm", None, None, "col"),
        P("tm", None, None, "col"),
        P("tm", None, "col"),
        P(),
    )
    return jax.shard_map(
        local,
        mesh=mesh,
        in_specs=placed,
        out_specs=(P("tm", None, "col"), P("tm", None, None, "col"), P()),
        check_vma=False,
    )
```

```python
import functools
import jax
import jax.numpy as jnp
from jax import lax
from jax.experimental import pallas as pl
from jax.experimental.pallas import tpu as pltpu
from jax.sharding import PartitionSpec as P

PARTS = 64
N = 1024
COLS = 4
ROWS = 16
BLOCK = 256
WIDE = N + 128
TOP = 20
EARLY = (62, 60)
SPLIT = 4
BUILD = 8
KEPT = 10
ROOT = 2
GROUPS = (PARTS - TOP) // 4
F32 = jnp.float32
BF16 = jnp.bfloat16
VMEM = pl.BlockSpec(memory_space=pltpu.VMEM)


def split(value):
    high = value.astype(BF16)
    return high, (value - high.astype(F32)).astype(BF16)


def product(left, high, low):
    rows = left.shape[0]
    left_high, left_low = split(left)
    both = jnp.dot(jnp.concatenate([left_high, left_low], 0), high, preferred_element_type=F32)
    return both[:rows] + both[rows:] + jnp.dot(left_high, low, preferred_element_type=F32)


def call(body, outs, specs, operands, flops=0, limit=8, **kw):
    return pl.pallas_call(
        body,
        out_shape=outs,
        in_specs=specs,
        out_specs=[VMEM] * len(outs),
        compiler_params=pltpu.CompilerParams(vmem_limit_bytes=limit << 20),
        cost_estimate=pl.CostEstimate(flops=flops, bytes_accessed=4 << 20, transcendentals=0),
        **kw,
    )(*operands)


def shape(*dims, dtype=F32):
    return jax.ShapeDtypeStruct(dims, dtype)


def when_at(test, run):
    pl.when(test(lax.axis_index("tm")))(run)


def upper_chip(at):
    return (at % 4 == 2) & (at < 4 * GROUPS)


def lower_chip(at):
    return (at % 4 == 0) & (at < 4 * GROUPS)


def moved(at):
    return (at % 8 == 2) & (at < 4 * KEPT)


def moves(k):
    return k % 2 == 0 and k < KEPT


def home(k):
    return 4 * k + 2 if moves(k) else 4 * k


def is_home(at):
    return moved(at) | ((at % 8 == 4) & (at < 4 * GROUPS)) | ((at % 8 == 0) & (at >= 4 * KEPT) & (at < 4 * GROUPS))


def first_body(left_ref, bias_ref, high_ref, low_ref, odd_high, odd_low, even_high, even_low, out_ref):
    def run():
        left = left_ref[...]
        x = product(left, high_ref[...], low_ref[...])
        out_ref[:, :N] = x
        out_ref[BLOCK:, :N] += bias_ref[...]
        out_ref[:, N:] = product(left, odd_high[...], odd_low[...]) + product(out_ref[:, :N], even_high[...], even_low[...])

    when_at(upper_chip, run)


def tall_body(left_ref, bias_ref, high_ref, low_ref, arrow_high, arrow_low, out_ref):
    def run():
        out_ref[:, :N] = product(left_ref[:, :N], high_ref[...], low_ref[...])
        out_ref[BLOCK:, :N] += bias_ref[...]
        out_ref[:, N:] = left_ref[:, N:] + product(out_ref[:, :N], arrow_high[...], arrow_low[...])

    when_at(lower_chip, run)


def tall(body, *operands):
    (out,) = call(body, [shape(BLOCK + ROWS, WIDE)], [VMEM] * len(operands), operands, 7 * 272 * N * N, 12)
    return out


def pick_body(own_ref, got_ref, rows_ref, term_ref):
    def take(source):
        rows_ref[...] = source[:BLOCK, :]
        term_ref[...] = source[BLOCK:, :]

    when_at(moved, lambda: take(got_ref))
    when_at(lambda at: jnp.logical_not(moved(at)), lambda: take(own_ref))


def follow(state, mats, bias, arrow, out_ref):
    x = product(state[:, :N], mats[0][...], mats[1][...]) + bias[...]
    out_ref[:, :N] = x
    out_ref[:, N:] = state[:, N:] + product(x, arrow[0][...], arrow[1][...])


def two_body(tests, *refs):
    count = len(tests)
    gots, (in_0, odd_0, even_0, fo, fe, oah, oal, eah, eal, oh, ol, eh, el, in_1, odd_1, even_1) = refs[:count], refs[count:]

    def step(got):
        follow(got, (oh, ol), fo, (oah, oal), odd_1)
        follow(odd_1, (eh, el), fe, (eah, eal), even_1)
        in_1[...] = got[...]

    for test, got in zip(tests, gots):
        when_at(test, functools.partial(step, got))


def launch_body(fo, fe, high, low, odd_ref, even_ref):
    def run():
        for ref, x in ((odd_ref, fo[...]), (even_ref, product(fo[...], high[...], low[...]) + fe[...])):
            ref[:, :N] = x
            ref[:, N:] = jnp.zeros((ROWS, 128), F32)

    when_at(lambda at: at == EARLY[0], run)


def early_body(got, in_0, odd_0, even_0, fo, fe, oh, ol, eh, el, in_1, odd_1, even_1):
    def run():
        in_1[...] = got[...]
        x = product(got[:, :N], oh[...], ol[...]) + fo[...]
        for ref, x in ((odd_1, x), (even_1, product(x, eh[...], el[...]) + fe[...])):
            ref[:, :N] = x
            ref[:, N:] = jnp.zeros((ROWS, 128), F32)

    when_at(lambda at: at == EARLY[1], run)


def two_steps(tests, gots, states, terms, mats):
    count = len(gots)
    return call(
        functools.partial(two_body, tests),
        [shape(ROWS, WIDE)] * 3,
        [VMEM] * (13 + count),
        (*gots, *states, *terms, *mats),
        13 * 16 * N * N,
        input_output_aliases={count: 0, count + 1: 1, count + 2: 2},
    )


def one_body(test, got, in_0, state_0, term, high, low, side, in_1, state_1):
    def run():
        x = got[:, :N]
        in_1[...] = got[...]
        state_1[:, :N] = product(x, high[...], low[...]) + term[:, :N]
        side_high, side_low = split(side[:N, :])
        state_1[:, N:] = got[:, N:] + product(x, side_high, side_low) + side[N:, :]

    when_at(test, run)


def one_step(test, got, states, term, mats):
    return call(
        functools.partial(one_body, test),
        [shape(ROWS, WIDE)] * 2,
        [VMEM] * 7,
        (got, *states, term, *mats),
        7 * 16 * N * N,
        input_output_aliases={1: 0, 2: 1},
    )


def places():
    c = lax.axis_index("col")
    return [c, (c + 3) % COLS, (c + 1) % COLS, (c + 2) % COLS]


def place_body(b0, b1, b2, b3, term, odd, even, odd_high, odd_low, even_high, even_low, high_ref, low_ref, side_ref):
    def run():
        for place, block in zip(places(), (b0, b1, b2, b3)):
            high, low = split(block[:, :N])
            at = pl.ds(pl.multiple_of(place * BLOCK, BLOCK), BLOCK)
            high_ref[at, :] = high
            low_ref[at, :] = low
            side_ref[at, :] = block[:, N:]
        side_ref[N:, :] = term[:, N:]

    def early():
        total = product(odd[:, :N], odd_high[...], odd_low[...])
        side_ref[N:, :] = total + product(even[:, :N], even_high[...], even_low[...])

    when_at(is_home, run)
    when_at(lambda at: (at == EARLY[0]) | (at == EARLY[1]), early)


def adjoint_body(test, first, got, side_0, high, low, term, side_1):
    def run():
        got_high, got_low = split(got[:N, :])
        for i in range(N // BLOCK):
            at = slice(i * BLOCK, (i + 1) * BLOCK)
            both = jnp.dot(jnp.concatenate([high[at, :], low[at, :]], 0), got_high, preferred_element_type=F32)
            rest = jnp.dot(high[at, :], got_low, preferred_element_type=F32)
            side_1[at, :] = side_0[at, :] + both[:BLOCK] + both[BLOCK:] + rest
        side_1[N:, :] = side_0[N:, :] + got[N:, :] + product(term[:, :N], got_high, got_low)

    def add():
        side_1[N:, :] = side_0[N:, :] + got[N:, :]

    when_at(test, run)
    when_at(lambda at: jnp.logical_not(test(at)) & ((at == home(5)) | (at == home(3))) & first, add)


def adjoint(test, first, got, side, high, low, term):
    (out,) = call(
        functools.partial(adjoint_body, test, first),
        [shape(N + ROWS, 128)],
        [VMEM] * 5,
        (got, side, high, low, term),
        6 * N * N * 128,
        input_output_aliases={1: 0},
    )
    return out


def slab_body(b0, b1, b2, b3, lh, ll, rh, rl, base, own_ref, out_ref, corner_ref, x_ref, next_ref, rows_ref):
    for place, block in zip(places(), (b0, b1, b2, b3)):
        at = pl.ds(pl.multiple_of(place * ROWS, ROWS), ROWS)
        x_ref[at, :] = block[:ROWS, :N]
        next_ref[at, :] = block[ROWS:, :N]
        rows_ref[at, :] = block[:ROWS, N:]
    corner_ref[...] = base[...] + rows_ref[...].T[:64, :]
    own = x_ref[...]
    later = next_ref[...]
    own_ref[...] = x_ref[:, pl.ds(pl.multiple_of(places()[0] * BLOCK, BLOCK), BLOCK)]
    for k in range(4):
        at = slice(k * N, k * N + N)
        out_ref[k] = product(own, lh[at, :], ll[at, :]) + product(later, rh[at, :], rl[at, :])


def finish_body(in_ref, odd_ref, even_ref, total_ref, send_ref, keep_ref):
    for ref, own, later in ((send_ref, odd_ref, in_ref), (keep_ref, even_ref, odd_ref)):
        ref[:ROWS, :N] = own[:, :N]
        ref[ROWS:, :N] = later[:, :N]
        ref[:ROWS, N:] = total_ref[...]
        ref[ROWS:, N:] = total_ref[...]


def choose_body(test, got_ref, keep_ref, out_ref):
    def take(source):
        out_ref[...] = source[...]

    when_at(test, lambda: take(got_ref))
    when_at(lambda at: jnp.logical_not(test(at)), lambda: take(keep_ref))


def choose(test, got, keep):
    (out,) = call(functools.partial(choose_body, test), [shape(*keep.shape)], [VMEM] * 2, (got, keep))
    return out


def sum_body(message_ref, out_ref):
    out_ref[...] = message_ref[:, N:]


def gather_body(b0, b1, b2, b3, out_ref):
    for place, block in zip(places(), (b0, b1, b2, b3)):
        out_ref[:, pl.ds(pl.multiple_of(place * BLOCK, BLOCK), BLOCK)] = block[...]


def arrow_body(odd_in, even_in, odd_high, odd_low, even_high, even_low, rows_ref):
    def run():
        for source, high, low in ((odd_in, odd_high, odd_low), (even_in, even_high, even_low)):
            rows_ref[:64, :] = source[...]
            rows_ref[64:, :] = jnp.zeros((64, N), F32)
            high[...], low[...] = split(rows_ref[...].T)

    when_at(lambda at: at % 2 == 0, run)


def whole_body(value_ref, high_ref, low_ref):
    @pl.loop(0, N // 64)
    def _(i):
        at = pl.ds(pl.multiple_of(i * 64, 64), 64)
        high_ref[at, :], low_ref[at, :] = split(value_ref[at, :])


def whole(value):
    return call(whole_body, [shape(N, N, dtype=BF16)] * 2, [VMEM], (value,), 2 * N * N)


def split_body(value_ref, high_ref, low_ref):
    high_ref[...], low_ref[...] = split(value_ref[...])


def halves(value, step=BLOCK):
    rows, columns = value.shape
    tile = pl.BlockSpec((step, columns), lambda i: (i, 0))
    return pl.pallas_call(
        split_body,
        grid=(rows // step,),
        out_shape=[shape(rows, columns, dtype=BF16)] * 2,
        in_specs=[tile],
        out_specs=[tile, tile],
        compiler_params=pltpu.CompilerParams(vmem_limit_bytes=8 << 20),
        cost_estimate=pl.CostEstimate(flops=2 * rows * columns, bytes_accessed=8 * rows * columns, transcendentals=0),
    )(value)


def around(value, members):
    return [lax.ppermute(value, ("tm", "col"), [(t * COLS + j, t * COLS + (j + by) % COLS) for t in members for j in range(COLS)]) for by in (1, 3, 2)]


def hop_pairs(i):
    chips = TOP // 2
    half = chips // 2
    device = PARTS - 2 - 2 * i
    pairs = [(device + 2, device)]
    mate = i + half if i + half < chips else i - half
    if 0 < mate < chips:
        at = PARTS - 2 - 2 * mate
        pairs.append((at + 2, at))
    return sorted(pairs)


def local(couple, free_term, slab_left, slab_right, arrow_rows, corner_base):
    c = lax.axis_index("col")
    own = couple[0]
    f = lax.dynamic_slice_in_dim(free_term[0], c * ROWS, ROWS, 0)
    groups = range(GROUPS)
    down = [(2 * j + 1, 2 * j) for j in range(PARTS // 2)]
    up = [(b, a) for a, b in down]
    inner = [(4 * k + 2, 4 * k) for k in groups]

    f_odd = lax.ppermute(f, "tm", down)
    sent, _ = lax.optimization_barrier((own, f_odd))
    other = lax.ppermute(sent, "tm", down)
    even_mats = whole(own)
    odd, even = call(launch_body, [shape(ROWS, WIDE)] * 2, [VMEM] * 4, (f_odd, f, *even_mats))
    zero = jnp.zeros((ROWS, WIDE), F32)
    states = (zero, odd, even)
    start = jnp.concatenate([lax.dynamic_slice_in_dim(own, c * BLOCK, BLOCK, 0), f], 0)
    start = lax.ppermute(start, "tm", [(4 * k + 3, 4 * k + 2) for k in groups])
    arrow = arrow_rows[0]
    others = around(arrow, range(PARTS))
    odd_mats = whole(other)
    got = lax.ppermute(even, "tm", hop_pairs(1))
    states = call(
        early_body,
        [shape(ROWS, WIDE)] * 3,
        [VMEM] * 10,
        (got, *states, f_odd, f, *odd_mats, *even_mats),
        12 * 16 * N * N,
        input_output_aliases={1: 0, 2: 1, 3: 2},
    )
    others, states = lax.optimization_barrier((others, states))
    (arrow,) = call(gather_body, [shape(64, N)], [VMEM] * 4, (arrow, *others))
    arrows = call(
        arrow_body,
        [shape(N, 128, dtype=BF16)] * 4,
        [VMEM] * 2,
        (lax.ppermute(arrow, "tm", down), arrow),
        scratch_shapes=[pltpu.VMEM((128, N), F32)],
    )
    odd_arrow, even_arrow = arrows[:2], arrows[2:]
    mats = (*odd_mats, *even_mats)
    terms = (f_odd, f, *odd_arrow, *even_arrow)
    rows = tall(first_body, start, f, *even_mats, *odd_arrow, *even_arrow)
    rows = lax.ppermute(rows, "tm", inner)

    for i in range(2, TOP // 2):
        device = PARTS - 2 - 2 * i
        got = lax.ppermute(states[2], "tm", hop_pairs(i))
        if i == SPLIT:
            _, slab_left, slab_right = lax.optimization_barrier((states[0], slab_left, slab_right))
            left = halves(slab_left[0].reshape(4 * N, BLOCK))
            right = halves(slab_right[0].reshape(4 * N, BLOCK))
            got, left, right = lax.optimization_barrier((got, left, right))
        if i == BUILD:
            rows, _ = lax.optimization_barrier((rows, states[0]))
            rows = tall(tall_body, rows, f_odd, *odd_mats, *odd_arrow)
            rows = tall(tall_body, rows, f, *even_mats, *even_arrow)
            moved_rows = lax.ppermute(rows, "tm", [(4 * k, 4 * k + 2) for k in groups if moves(k)])
            rows, term = call(pick_body, [shape(BLOCK, WIDE), shape(ROWS, WIDE)], [VMEM] * 2, (rows, moved_rows))
            others = around(rows, sorted(home(k) for k in groups))
            got, rows, others = lax.optimization_barrier((got, rows, others))
        states = two_steps([lambda at, device=device: at == device], [got], states, terms, mats)
    high, low, side = call(
        place_body,
        [shape(N, N, dtype=BF16)] * 2 + [shape(N + ROWS, 128)],
        [VMEM] * 11,
        (rows, *others, term, *states[1:], *odd_arrow, *even_arrow),
    )
    for k in range(1, ROOT + 1):
        pairs = [(home(k - 1), home(k))]
        if k == 1:
            pairs += [(EARLY[0], home(5)), (EARLY[1], home(3))]
        got = lax.ppermute(side, "tm", pairs)
        side = adjoint(lambda at, k=k: at == home(k), k == 1, got, side, high, low, term)
    group_mats = (high, low, side)

    x_in, x_odd, x_even = states
    message = x_even
    sources = [home(k + 1) if k + 1 < GROUPS else 4 * GROUPS for k in groups]
    half = (GROUPS + 1) // 2
    for k in reversed(groups):
        pairs = [(sources[k], home(k))]
        mate = k + half if k + half < GROUPS else k - half
        if 0 <= mate:
            pairs.append((sources[mate], home(mate)))
        got = lax.ppermute(message, "tm", sorted(pairs))
        if k:
            x_in, message = one_step(lambda at, k=k: at == home(k), got, (x_in, message), term, group_mats)
    last = got

    (total,) = call(sum_body, [shape(ROWS, 128)], [VMEM], (message,))

    def spread(total, pairs):
        reached = [b for _, b in pairs]
        return choose(
            lambda at: functools.reduce(jnp.logical_or, [at == r for r in reached]),
            lax.ppermute(total, "tm", sorted(pairs)),
            total,
        )

    total = spread(total, [(10, 58)])
    total, x_in, x_odd, x_even, last = lax.optimization_barrier((total, x_in, x_odd, x_even, last))

    got = lax.ppermute(x_in, "tm", [(4 * k, 4 * k + 2) for k in groups if not moves(k)])
    x_in, x_odd, x_even = two_steps(
        [
            lambda at: upper_chip(at) & jnp.logical_not(moved(at)),
            lambda at: at == home(0),
            lambda at: moved(at) & (at != home(0)),
        ],
        [got, last, x_in],
        (x_in, x_odd, x_even),
        terms,
        mats,
    )
    got = lax.ppermute(x_even, "tm", inner)
    x_in, x_odd, x_even = two_steps([lower_chip], [got], (x_in, x_odd, x_even), terms, mats)
    total, x_odd, x_even = lax.optimization_barrier((total, x_odd, x_even))
    total = spread(total, [(58, 42), (10, 26)])
    total = spread(total, [(58, 2), (42, 50), (26, 34), (10, 18)])
    total = spread(total, [(a, a + 4) for a in range(2, PARTS, 8)])
    pairs = [(a, a + 2) for a in range(2, PARTS, 8)] + [(a, a - 6) for a in range(6, PARTS, 8)]
    total = spread(total, pairs)
    send, keep = call(finish_body, [shape(2 * ROWS, WIDE)] * 2, [VMEM] * 4, (x_in, x_odd, x_even, total))
    pair = choose(lambda at: at % 2 == 1, lax.ppermute(send, "tm", up), keep)
    blocks = [pair] + around(pair, range(PARTS))
    columns, slab, corner = call(
        slab_body,
        [shape(64, BLOCK), shape(4, 64, BLOCK), shape(64, 64)],
        [VMEM] * 9,
        (*blocks, *left, *right, corner_base),
        12 * 64 * N * N,
        scratch_shapes=[pltpu.VMEM((64, N), F32)] * 2 + [pltpu.VMEM((64, 128), F32)],
    )
    return (columns[None], slab[None], corner)


def solution(mesh):
    placed = (
        P("tm", None, None),
        P("tm", None, None),
        P("tm", None, None, "col"),
        P("tm", None, None, "col"),
        P("tm", None, "col"),
        P(),
    )
    return jax.shard_map(
        local,
        mesh=mesh,
        in_specs=placed,
        out_specs=(P("tm", None, "col"), P("tm", None, None, "col"), P()),
        check_vma=False,
    )
```

```python
import functools
import jax
import jax.numpy as jnp
from jax import lax
from jax.experimental import pallas as pl
from jax.experimental.pallas import tpu as pltpu
from jax.sharding import PartitionSpec as P

PARTS = 64
N = 1024
COLS = 4
ROWS = 16
BLOCK = 256
WIDE = N + 128
TOP = 20
SPLIT = 4
BUILD = 8
KEPT = 10
ROOT = 2
GROUPS = (PARTS - TOP) // 4
F32 = jnp.float32
BF16 = jnp.bfloat16
VMEM = pl.BlockSpec(memory_space=pltpu.VMEM)


def split(value):
    high = value.astype(BF16)
    return high, (value - high.astype(F32)).astype(BF16)


def product(left, high, low):
    rows = left.shape[0]
    left_high, left_low = split(left)
    both = jnp.dot(jnp.concatenate([left_high, left_low], 0), high, preferred_element_type=F32)
    return both[:rows] + both[rows:] + jnp.dot(left_high, low, preferred_element_type=F32)


def call(body, outs, specs, operands, flops=0, limit=8, **kw):
    return pl.pallas_call(
        body,
        out_shape=outs,
        in_specs=specs,
        out_specs=[VMEM] * len(outs),
        compiler_params=pltpu.CompilerParams(vmem_limit_bytes=limit << 20),
        cost_estimate=pl.CostEstimate(flops=flops, bytes_accessed=4 << 20, transcendentals=0),
        **kw,
    )(*operands)


def shape(*dims, dtype=F32):
    return jax.ShapeDtypeStruct(dims, dtype)


def when_at(test, run):
    pl.when(test(lax.axis_index("tm")))(run)


def upper_chip(at):
    return (at % 4 == 2) & (at < 4 * GROUPS)


def lower_chip(at):
    return (at % 4 == 0) & (at < 4 * GROUPS)


def moved(at):
    return (at % 8 == 2) & (at < 4 * KEPT)


def moves(k):
    return k % 2 == 0 and k < KEPT


def home(k):
    return 4 * k + 2 if moves(k) else 4 * k


def is_home(at):
    return moved(at) | ((at % 8 == 4) & (at < 4 * GROUPS)) | ((at % 8 == 0) & (at >= 4 * KEPT) & (at < 4 * GROUPS))


def first_body(left_ref, bias_ref, high_ref, low_ref, odd_high, odd_low, even_high, even_low, out_ref):
    def run():
        left = left_ref[...]
        x = product(left, high_ref[...], low_ref[...])
        out_ref[:, :N] = x
        out_ref[BLOCK:, :N] += bias_ref[...]
        out_ref[:, N:] = product(left, odd_high[...], odd_low[...]) + product(out_ref[:, :N], even_high[...], even_low[...])

    when_at(upper_chip, run)


def tall_body(left_ref, bias_ref, high_ref, low_ref, arrow_high, arrow_low, out_ref):
    def run():
        out_ref[:, :N] = product(left_ref[:, :N], high_ref[...], low_ref[...])
        out_ref[BLOCK:, :N] += bias_ref[...]
        out_ref[:, N:] = left_ref[:, N:] + product(out_ref[:, :N], arrow_high[...], arrow_low[...])

    when_at(lower_chip, run)


def tall(body, *operands):
    (out,) = call(body, [shape(BLOCK + ROWS, WIDE)], [VMEM] * len(operands), operands, 7 * 272 * N * N, 12)
    return out


def pick_body(own_ref, got_ref, rows_ref, term_ref):
    def take(source):
        rows_ref[...] = source[:BLOCK, :]
        term_ref[...] = source[BLOCK:, :]

    when_at(moved, lambda: take(got_ref))
    when_at(lambda at: jnp.logical_not(moved(at)), lambda: take(own_ref))


def follow(state, mats, bias, arrow, out_ref):
    x = product(state[:, :N], mats[0][...], mats[1][...]) + bias[...]
    out_ref[:, :N] = x
    out_ref[:, N:] = state[:, N:] + product(x, arrow[0][...], arrow[1][...])


def two_body(tests, *refs):
    count = len(tests)
    gots, (in_0, odd_0, even_0, fo, fe, oah, oal, eah, eal, oh, ol, eh, el, in_1, odd_1, even_1) = refs[:count], refs[count:]

    def step(got):
        follow(got, (oh, ol), fo, (oah, oal), odd_1)
        follow(odd_1, (eh, el), fe, (eah, eal), even_1)
        in_1[...] = got[...]

    for test, got in zip(tests, gots):
        when_at(test, functools.partial(step, got))


def two_steps(tests, gots, states, terms, mats):
    count = len(gots)
    return call(
        functools.partial(two_body, tests),
        [shape(ROWS, WIDE)] * 3,
        [VMEM] * (13 + count),
        (*gots, *states, *terms, *mats),
        13 * 16 * N * N,
        input_output_aliases={count: 0, count + 1: 1, count + 2: 2},
    )


def one_body(test, got, in_0, state_0, term, high, low, side, in_1, state_1):
    def run():
        x = got[:, :N]
        in_1[...] = got[...]
        state_1[:, :N] = product(x, high[...], low[...]) + term[:, :N]
        side_high, side_low = split(side[:N, :])
        state_1[:, N:] = got[:, N:] + product(x, side_high, side_low) + side[N:, :]

    when_at(test, run)


def one_step(test, got, states, term, mats):
    return call(
        functools.partial(one_body, test),
        [shape(ROWS, WIDE)] * 2,
        [VMEM] * 7,
        (got, *states, term, *mats),
        7 * 16 * N * N,
        input_output_aliases={1: 0, 2: 1},
    )


def places():
    c = lax.axis_index("col")
    return [c, (c + 3) % COLS, (c + 1) % COLS, (c + 2) % COLS]


def place_body(b0, b1, b2, b3, term, high_ref, low_ref, side_ref):
    def run():
        for place, block in zip(places(), (b0, b1, b2, b3)):
            high, low = split(block[:, :N])
            at = pl.ds(pl.multiple_of(place * BLOCK, BLOCK), BLOCK)
            high_ref[at, :] = high
            low_ref[at, :] = low
            side_ref[at, :] = block[:, N:]
        side_ref[N:, :] = term[:, N:]

    when_at(is_home, run)


def adjoint_body(test, got, side_0, high, low, term, side_1):
    def run():
        got_high, got_low = split(got[:N, :])
        for i in range(N // BLOCK):
            at = slice(i * BLOCK, (i + 1) * BLOCK)
            both = jnp.dot(jnp.concatenate([high[at, :], low[at, :]], 0), got_high, preferred_element_type=F32)
            rest = jnp.dot(high[at, :], got_low, preferred_element_type=F32)
            side_1[at, :] = side_0[at, :] + both[:BLOCK] + both[BLOCK:] + rest
        side_1[N:, :] = side_0[N:, :] + got[N:, :] + product(term[:, :N], got_high, got_low)

    when_at(test, run)


def adjoint(test, got, side, high, low, term):
    (out,) = call(
        functools.partial(adjoint_body, test),
        [shape(N + ROWS, 128)],
        [VMEM] * 5,
        (got, side, high, low, term),
        6 * N * N * 128,
        input_output_aliases={1: 0},
    )
    return out


def slab_body(b0, b1, b2, b3, lh, ll, rh, rl, base, own_ref, out_ref, corner_ref, x_ref, next_ref, rows_ref):
    for place, block in zip(places(), (b0, b1, b2, b3)):
        at = pl.ds(pl.multiple_of(place * ROWS, ROWS), ROWS)
        x_ref[at, :] = block[:ROWS, :N]
        next_ref[at, :] = block[ROWS:, :N]
        rows_ref[at, :] = block[:ROWS, N:]
    corner_ref[...] = base[...] + rows_ref[...].T[:64, :]
    own = x_ref[...]
    later = next_ref[...]
    own_ref[...] = x_ref[:, pl.ds(pl.multiple_of(places()[0] * BLOCK, BLOCK), BLOCK)]
    for k in range(4):
        at = slice(k * N, k * N + N)
        out_ref[k] = product(own, lh[at, :], ll[at, :]) + product(later, rh[at, :], rl[at, :])


def finish_body(in_ref, odd_ref, even_ref, total_ref, send_ref, keep_ref):
    for ref, own, later in ((send_ref, odd_ref, in_ref), (keep_ref, even_ref, odd_ref)):
        ref[:ROWS, :N] = own[:, :N]
        ref[ROWS:, :N] = later[:, :N]
        ref[:ROWS, N:] = total_ref[...]
        ref[ROWS:, N:] = total_ref[...]


def choose_body(test, got_ref, keep_ref, out_ref):
    def take(source):
        out_ref[...] = source[...]

    when_at(test, lambda: take(got_ref))
    when_at(lambda at: jnp.logical_not(test(at)), lambda: take(keep_ref))


def choose(test, got, keep):
    (out,) = call(functools.partial(choose_body, test), [shape(*keep.shape)], [VMEM] * 2, (got, keep))
    return out


def sum_body(message_ref, out_ref):
    out_ref[...] = message_ref[:, N:]


def gather_body(b0, b1, b2, b3, f_ref, out_ref):
    for place, block in zip(places(), (b0, b1, b2, b3)):
        out_ref[:64, pl.ds(pl.multiple_of(place * BLOCK, BLOCK), BLOCK)] = block[...]
    out_ref[64:, :] = f_ref[...]


def arrow_body(odd_in, even_in, odd_high, odd_low, even_high, even_low, f_ref, rows_ref):
    def run():
        for source, high, low in ((odd_in, odd_high, odd_low), (even_in, even_high, even_low)):
            rows_ref[:64, :] = source[:64, :]
            rows_ref[64:, :] = jnp.zeros((64, N), F32)
            high[...], low[...] = split(rows_ref[...].T)
        f_ref[...] = odd_in[64:, :]

    when_at(lambda at: at % 2 == 0, run)


def whole_body(value_ref, high_ref, low_ref):
    @pl.loop(0, N // 64)
    def _(i):
        at = pl.ds(pl.multiple_of(i * 64, 64), 64)
        high_ref[at, :], low_ref[at, :] = split(value_ref[at, :])


def whole(value):
    return call(whole_body, [shape(N, N, dtype=BF16)] * 2, [VMEM], (value,), 2 * N * N)


def split_body(value_ref, high_ref, low_ref):
    high_ref[...], low_ref[...] = split(value_ref[...])


def halves(value, step=BLOCK):
    rows, columns = value.shape
    tile = pl.BlockSpec((step, columns), lambda i: (i, 0))
    return pl.pallas_call(
        split_body,
        grid=(rows // step,),
        out_shape=[shape(rows, columns, dtype=BF16)] * 2,
        in_specs=[tile],
        out_specs=[tile, tile],
        compiler_params=pltpu.CompilerParams(vmem_limit_bytes=8 << 20),
        cost_estimate=pl.CostEstimate(flops=2 * rows * columns, bytes_accessed=8 * rows * columns, transcendentals=0),
    )(value)


def around(value, members):
    return [lax.ppermute(value, ("tm", "col"), [(t * COLS + j, t * COLS + (j + by) % COLS) for t in members for j in range(COLS)]) for by in (1, 3, 2)]


def local(couple, free_term, slab_left, slab_right, arrow_rows, corner_base):
    c = lax.axis_index("col")
    own = couple[0]
    f = lax.dynamic_slice_in_dim(free_term[0], c * ROWS, ROWS, 0)
    groups = range(GROUPS)
    down = [(2 * j + 1, 2 * j) for j in range(PARTS // 2)]
    up = [(b, a) for a, b in down]
    inner = [(4 * k + 2, 4 * k) for k in groups]

    other = lax.ppermute(own, "tm", down)
    start = jnp.concatenate([lax.dynamic_slice_in_dim(own, c * BLOCK, BLOCK, 0), f], 0)
    start = lax.ppermute(start, "tm", [(4 * k + 3, 4 * k + 2) for k in groups])
    arrow = arrow_rows[0]
    others = around(arrow, range(PARTS))
    even_mats = whole(own)
    odd_mats = whole(other)
    others, even_mats, odd_mats = lax.optimization_barrier((others, even_mats, odd_mats))
    (arrow,) = call(gather_body, [shape(64 + ROWS, N)], [VMEM] * 5, (arrow, *others, f))
    arrows = call(
        arrow_body,
        [shape(N, 128, dtype=BF16)] * 4 + [shape(ROWS, N)],
        [VMEM] * 2,
        (lax.ppermute(arrow, "tm", down), arrow),
        scratch_shapes=[pltpu.VMEM((128, N), F32)],
    )
    odd_arrow, even_arrow, f_odd = arrows[:2], arrows[2:4], arrows[4]
    mats = (*odd_mats, *even_mats)
    terms = (f_odd, f, *odd_arrow, *even_arrow)
    rows = tall(first_body, start, f, *even_mats, *odd_arrow, *even_arrow)
    zero = jnp.zeros((ROWS, WIDE), F32)
    rows, zero = lax.optimization_barrier((rows, zero))
    rows = lax.ppermute(rows, "tm", inner)

    states = (zero, zero, zero)
    chips = TOP // 2
    half = chips // 2
    got = zero
    for i in range(chips):
        device = PARTS - 2 - 2 * i
        if i:
            pairs = [(device + 2, device)]
            mate = i + half if i + half < chips else i - half
            if 0 < mate < chips:
                at = PARTS - 2 - 2 * mate
                pairs.append((at + 2, at))
            got = lax.ppermute(states[2], "tm", sorted(pairs))
        if i == SPLIT:
            _, slab_left, slab_right = lax.optimization_barrier((states[0], slab_left, slab_right))
            left = halves(slab_left[0].reshape(4 * N, BLOCK))
            right = halves(slab_right[0].reshape(4 * N, BLOCK))
            got, left, right = lax.optimization_barrier((got, left, right))
        if i == BUILD:
            rows, _ = lax.optimization_barrier((rows, states[0]))
            rows = tall(tall_body, rows, f_odd, *odd_mats, *odd_arrow)
            rows = tall(tall_body, rows, f, *even_mats, *even_arrow)
            moved_rows = lax.ppermute(rows, "tm", [(4 * k, 4 * k + 2) for k in groups if moves(k)])
            rows, term = call(pick_body, [shape(BLOCK, WIDE), shape(ROWS, WIDE)], [VMEM] * 2, (rows, moved_rows))
            others = around(rows, sorted(home(k) for k in groups))
            got, rows, others = lax.optimization_barrier((got, rows, others))
        states = two_steps([lambda at, device=device: at == device], [got], states, terms, mats)
    high, low, side = call(
        place_body,
        [shape(N, N, dtype=BF16)] * 2 + [shape(N + ROWS, 128)],
        [VMEM] * 5,
        (rows, *others, term),
    )
    for k in range(1, ROOT + 1):
        got = lax.ppermute(side, "tm", [(home(k - 1), home(k))])
        side = adjoint(lambda at, k=k: at == home(k), got, side, high, low, term)
    group_mats = (high, low, side)

    x_in, x_odd, x_even = states
    message = x_even
    sources = [home(k + 1) if k + 1 < GROUPS else 4 * GROUPS for k in groups]
    half = (GROUPS + 1) // 2
    for k in reversed(groups):
        pairs = [(sources[k], home(k))]
        mate = k + half if k + half < GROUPS else k - half
        if 0 <= mate:
            pairs.append((sources[mate], home(mate)))
        got = lax.ppermute(message, "tm", sorted(pairs))
        if k:
            x_in, message = one_step(lambda at, k=k: at == home(k), got, (x_in, message), term, group_mats)
    last = got

    (total,) = call(sum_body, [shape(ROWS, 128)], [VMEM], (message,))

    def spread(total, pairs):
        reached = [b for _, b in pairs]
        return choose(
            lambda at: functools.reduce(jnp.logical_or, [at == r for r in reached]),
            lax.ppermute(total, "tm", sorted(pairs)),
            total,
        )

    total = spread(total, [(10, 58)])
    total = spread(total, [(10, 42)])
    total, x_in, x_odd, x_even, last = lax.optimization_barrier((total, x_in, x_odd, x_even, last))

    got = lax.ppermute(x_in, "tm", [(4 * k, 4 * k + 2) for k in groups if not moves(k)])
    x_in, x_odd, x_even = two_steps(
        [
            lambda at: upper_chip(at) & jnp.logical_not(moved(at)),
            lambda at: at == home(0),
            lambda at: moved(at) & (at != home(0)),
        ],
        [got, last, x_in],
        (x_in, x_odd, x_even),
        terms,
        mats,
    )
    got = lax.ppermute(x_even, "tm", inner)
    x_in, x_odd, x_even = two_steps([lower_chip], [got], (x_in, x_odd, x_even), terms, mats)
    total, x_odd, x_even = lax.optimization_barrier((total, x_odd, x_even))
    total = spread(total, [(58, 2), (42, 34), (10, 26)])
    total = spread(total, [(58, 50), (26, 18)])
    total = spread(total, [(a, a + 4) for a in range(2, PARTS, 8)])
    pairs = [(a, a + 2) for a in range(2, PARTS, 8)] + [(a, a - 6) for a in range(6, PARTS, 8)]
    total = spread(total, pairs)
    send, keep = call(finish_body, [shape(2 * ROWS, WIDE)] * 2, [VMEM] * 4, (x_in, x_odd, x_even, total))
    pair = choose(lambda at: at % 2 == 1, lax.ppermute(send, "tm", up), keep)
    blocks = [pair] + around(pair, range(PARTS))
    columns, slab, corner = call(
        slab_body,
        [shape(64, BLOCK), shape(4, 64, BLOCK), shape(64, 64)],
        [VMEM] * 9,
        (*blocks, *left, *right, corner_base),
        12 * 64 * N * N,
        scratch_shapes=[pltpu.VMEM((64, N), F32)] * 2 + [pltpu.VMEM((64, 128), F32)],
    )
    return (columns[None], slab[None], corner)


def solution(mesh):
    placed = (
        P("tm", None, None),
        P("tm", None, None),
        P("tm", None, None, "col"),
        P("tm", None, None, "col"),
        P("tm", None, "col"),
        P(),
    )
    return jax.shard_map(
        local,
        mesh=mesh,
        in_specs=placed,
        out_specs=(P("tm", None, "col"), P("tm", None, None, "col"), P()),
        check_vma=False,
    )
```

```python
import functools
import jax
import jax.numpy as jnp
from jax import lax
from jax.experimental import pallas as pl
from jax.experimental.pallas import tpu as pltpu
from jax.sharding import PartitionSpec as P

PARTS = 64
N = 1024
COLS = 4
ROWS = 16
BLOCK = 256
WIDE = N + 128
TOP = 20
SPLIT = 4
BUILD = 8
KEPT = 10
ROOT = 2
GROUPS = (PARTS - TOP) // 4
F32 = jnp.float32
BF16 = jnp.bfloat16
VMEM = pl.BlockSpec(memory_space=pltpu.VMEM)


def split(value):
    high = value.astype(BF16)
    return high, (value - high.astype(F32)).astype(BF16)


def product(left, high, low):
    rows = left.shape[0]
    left_high, left_low = split(left)
    both = jnp.dot(jnp.concatenate([left_high, left_low], 0), high, preferred_element_type=F32)
    return both[:rows] + both[rows:] + jnp.dot(left_high, low, preferred_element_type=F32)


def call(body, outs, specs, operands, flops=0, limit=8, **kw):
    return pl.pallas_call(
        body,
        out_shape=outs,
        in_specs=specs,
        out_specs=[VMEM] * len(outs),
        compiler_params=pltpu.CompilerParams(vmem_limit_bytes=limit << 20),
        cost_estimate=pl.CostEstimate(flops=flops, bytes_accessed=4 << 20, transcendentals=0),
        **kw,
    )(*operands)


def shape(*dims, dtype=F32):
    return jax.ShapeDtypeStruct(dims, dtype)


def when_at(test, run):
    pl.when(test(lax.axis_index("tm")))(run)


def upper_chip(at):
    return (at % 4 == 2) & (at < 4 * GROUPS)


def lower_chip(at):
    return (at % 4 == 0) & (at < 4 * GROUPS)


def moved(at):
    return (at % 8 == 2) & (at < 4 * KEPT)


def moves(k):
    return k % 2 == 0 and k < KEPT


def home(k):
    return 4 * k + 2 if moves(k) else 4 * k


def is_home(at):
    return moved(at) | ((at % 8 == 4) & (at < 4 * GROUPS)) | ((at % 8 == 0) & (at >= 4 * KEPT) & (at < 4 * GROUPS))


def first_body(left_ref, bias_ref, high_ref, low_ref, odd_high, odd_low, even_high, even_low, out_ref):
    def run():
        left = left_ref[...]
        x = product(left, high_ref[...], low_ref[...])
        out_ref[:, :N] = x
        out_ref[BLOCK:, :N] += bias_ref[...]
        out_ref[:, N:] = product(left, odd_high[...], odd_low[...]) + product(out_ref[:, :N], even_high[...], even_low[...])

    when_at(upper_chip, run)


def tall_body(left_ref, bias_ref, high_ref, low_ref, arrow_high, arrow_low, out_ref):
    def run():
        out_ref[:, :N] = product(left_ref[:, :N], high_ref[...], low_ref[...])
        out_ref[BLOCK:, :N] += bias_ref[...]
        out_ref[:, N:] = left_ref[:, N:] + product(out_ref[:, :N], arrow_high[...], arrow_low[...])

    when_at(lower_chip, run)


def tall(body, *operands):
    (out,) = call(body, [shape(BLOCK + ROWS, WIDE)], [VMEM] * len(operands), operands, 7 * 272 * N * N, 12)
    return out


def pick_body(own_ref, got_ref, rows_ref, term_ref):
    def take(source):
        rows_ref[...] = source[:BLOCK, :]
        term_ref[...] = source[BLOCK:, :]

    when_at(moved, lambda: take(got_ref))
    when_at(lambda at: jnp.logical_not(moved(at)), lambda: take(own_ref))


def follow(state, mats, bias, arrow, out_ref):
    x = product(state[:, :N], mats[0][...], mats[1][...]) + bias[...]
    out_ref[:, :N] = x
    out_ref[:, N:] = state[:, N:] + product(x, arrow[0][...], arrow[1][...])


def two_body(tests, *refs):
    count = len(tests)
    gots, (in_0, odd_0, even_0, fo, fe, oah, oal, eah, eal, oh, ol, eh, el, in_1, odd_1, even_1) = refs[:count], refs[count:]

    def step(got):
        follow(got, (oh, ol), fo, (oah, oal), odd_1)
        follow(odd_1, (eh, el), fe, (eah, eal), even_1)
        in_1[...] = got[...]

    for test, got in zip(tests, gots):
        when_at(test, functools.partial(step, got))


def two_steps(tests, gots, states, terms, mats):
    count = len(gots)
    return call(
        functools.partial(two_body, tests),
        [shape(ROWS, WIDE)] * 3,
        [VMEM] * (13 + count),
        (*gots, *states, *terms, *mats),
        13 * 16 * N * N,
        input_output_aliases={count: 0, count + 1: 1, count + 2: 2},
    )


def one_body(test, got, in_0, state_0, term, high, low, side, in_1, state_1):
    def run():
        x = got[:, :N]
        in_1[...] = got[...]
        state_1[:, :N] = product(x, high[...], low[...]) + term[:, :N]
        side_high, side_low = split(side[:N, :])
        state_1[:, N:] = got[:, N:] + product(x, side_high, side_low) + side[N:, :]

    when_at(test, run)


def one_step(test, got, states, term, mats):
    return call(
        functools.partial(one_body, test),
        [shape(ROWS, WIDE)] * 2,
        [VMEM] * 7,
        (got, *states, term, *mats),
        7 * 16 * N * N,
        input_output_aliases={1: 0, 2: 1},
    )


def places():
    c = lax.axis_index("col")
    return [c, (c + 3) % COLS, (c + 1) % COLS, (c + 2) % COLS]


def place_body(b0, b1, b2, b3, term, high_ref, low_ref, side_ref):
    def run():
        for place, block in zip(places(), (b0, b1, b2, b3)):
            high, low = split(block[:, :N])
            at = pl.ds(pl.multiple_of(place * BLOCK, BLOCK), BLOCK)
            high_ref[at, :] = high
            low_ref[at, :] = low
            side_ref[at, :] = block[:, N:]
        side_ref[N:, :] = term[:, N:]

    when_at(is_home, run)


def adjoint_body(test, got, side_0, high, low, term, side_1):
    def run():
        got_high, got_low = split(got[:N, :])
        for i in range(N // BLOCK):
            at = slice(i * BLOCK, (i + 1) * BLOCK)
            both = jnp.dot(jnp.concatenate([high[at, :], low[at, :]], 0), got_high, preferred_element_type=F32)
            rest = jnp.dot(high[at, :], got_low, preferred_element_type=F32)
            side_1[at, :] = side_0[at, :] + both[:BLOCK] + both[BLOCK:] + rest
        side_1[N:, :] = side_0[N:, :] + got[N:, :] + product(term[:, :N], got_high, got_low)

    when_at(test, run)


def adjoint(test, got, side, high, low, term):
    (out,) = call(
        functools.partial(adjoint_body, test),
        [shape(N + ROWS, 128)],
        [VMEM] * 5,
        (got, side, high, low, term),
        6 * N * N * 128,
        input_output_aliases={1: 0},
    )
    return out


def slab_body(b0, b1, b2, b3, lh, ll, rh, rl, base, own_ref, out_ref, corner_ref, x_ref, next_ref, rows_ref):
    for place, block in zip(places(), (b0, b1, b2, b3)):
        at = pl.ds(pl.multiple_of(place * ROWS, ROWS), ROWS)
        x_ref[at, :] = block[:ROWS, :N]
        next_ref[at, :] = block[ROWS:, :N]
        rows_ref[at, :] = block[:ROWS, N:]
    corner_ref[...] = base[...] + rows_ref[...].T[:64, :]
    own = x_ref[...]
    later = next_ref[...]
    own_ref[...] = x_ref[:, pl.ds(pl.multiple_of(places()[0] * BLOCK, BLOCK), BLOCK)]
    for k in range(4):
        at = slice(k * N, k * N + N)
        out_ref[k] = product(own, lh[at, :], ll[at, :]) + product(later, rh[at, :], rl[at, :])


def finish_body(in_ref, odd_ref, even_ref, total_ref, send_ref, keep_ref):
    for ref, own, later in ((send_ref, odd_ref, in_ref), (keep_ref, even_ref, odd_ref)):
        ref[:ROWS, :N] = own[:, :N]
        ref[ROWS:, :N] = later[:, :N]
        ref[:ROWS, N:] = total_ref[...]
        ref[ROWS:, N:] = total_ref[...]


def choose_body(test, got_ref, keep_ref, out_ref):
    def take(source):
        out_ref[...] = source[...]

    when_at(test, lambda: take(got_ref))
    when_at(lambda at: jnp.logical_not(test(at)), lambda: take(keep_ref))


def choose(test, got, keep):
    (out,) = call(functools.partial(choose_body, test), [shape(*keep.shape)], [VMEM] * 2, (got, keep))
    return out


def sum_body(message_ref, out_ref):
    out_ref[...] = message_ref[:, N:]


def gather_body(b0, b1, b2, b3, f_ref, out_ref):
    for place, block in zip(places(), (b0, b1, b2, b3)):
        out_ref[:64, pl.ds(pl.multiple_of(place * BLOCK, BLOCK), BLOCK)] = block[...]
    out_ref[64:, :] = f_ref[...]


def arrow_body(odd_in, even_in, odd_high, odd_low, even_high, even_low, f_ref, rows_ref):
    def run():
        for source, high, low in ((odd_in, odd_high, odd_low), (even_in, even_high, even_low)):
            rows_ref[:64, :] = source[:64, :]
            rows_ref[64:, :] = jnp.zeros((64, N), F32)
            high[...], low[...] = split(rows_ref[...].T)
        f_ref[...] = odd_in[64:, :]

    when_at(lambda at: at % 2 == 0, run)


def whole_body(value_ref, high_ref, low_ref):
    @pl.loop(0, N // 64)
    def _(i):
        at = pl.ds(pl.multiple_of(i * 64, 64), 64)
        high_ref[at, :], low_ref[at, :] = split(value_ref[at, :])


def whole(value):
    return call(whole_body, [shape(N, N, dtype=BF16)] * 2, [VMEM], (value,), 2 * N * N)


def split_body(value_ref, high_ref, low_ref):
    high_ref[...], low_ref[...] = split(value_ref[...])


def halves(value, step=BLOCK):
    rows, columns = value.shape
    tile = pl.BlockSpec((step, columns), lambda i: (i, 0))
    return pl.pallas_call(
        split_body,
        grid=(rows // step,),
        out_shape=[shape(rows, columns, dtype=BF16)] * 2,
        in_specs=[tile],
        out_specs=[tile, tile],
        compiler_params=pltpu.CompilerParams(vmem_limit_bytes=8 << 20),
        cost_estimate=pl.CostEstimate(flops=2 * rows * columns, bytes_accessed=8 * rows * columns, transcendentals=0),
    )(value)


def around(value, members):
    return [lax.ppermute(value, ("tm", "col"), [(t * COLS + j, t * COLS + (j + by) % COLS) for t in members for j in range(COLS)]) for by in (1, 3, 2)]


def local(couple, free_term, slab_left, slab_right, arrow_rows, corner_base):
    c = lax.axis_index("col")
    own = couple[0]
    f = lax.dynamic_slice_in_dim(free_term[0], c * ROWS, ROWS, 0)
    groups = range(GROUPS)
    down = [(2 * j + 1, 2 * j) for j in range(PARTS // 2)]
    up = [(b, a) for a, b in down]
    inner = [(4 * k + 2, 4 * k) for k in groups]

    other = lax.ppermute(own, "tm", down)
    start = jnp.concatenate([lax.dynamic_slice_in_dim(own, c * BLOCK, BLOCK, 0), f], 0)
    start = lax.ppermute(start, "tm", [(4 * k + 3, 4 * k + 2) for k in groups])
    arrow = arrow_rows[0]
    others = around(arrow, range(PARTS))
    even_mats = whole(own)
    odd_mats = whole(other)
    others, even_mats, odd_mats = lax.optimization_barrier((others, even_mats, odd_mats))
    (arrow,) = call(gather_body, [shape(64 + ROWS, N)], [VMEM] * 5, (arrow, *others, f))
    arrows = call(
        arrow_body,
        [shape(N, 128, dtype=BF16)] * 4 + [shape(ROWS, N)],
        [VMEM] * 2,
        (lax.ppermute(arrow, "tm", down), arrow),
        scratch_shapes=[pltpu.VMEM((128, N), F32)],
    )
    odd_arrow, even_arrow, f_odd = arrows[:2], arrows[2:4], arrows[4]
    mats = (*odd_mats, *even_mats)
    terms = (f_odd, f, *odd_arrow, *even_arrow)
    rows = tall(first_body, start, f, *even_mats, *odd_arrow, *even_arrow)
    zero = jnp.zeros((ROWS, WIDE), F32)
    rows, zero = lax.optimization_barrier((rows, zero))
    rows = lax.ppermute(rows, "tm", inner)

    states = (zero, zero, zero)
    chips = TOP // 2
    half = chips // 2
    got = zero
    for i in range(chips):
        device = PARTS - 2 - 2 * i
        if i:
            pairs = [(device + 2, device)]
            mate = i + half if i + half < chips else i - half
            if 0 < mate < chips:
                at = PARTS - 2 - 2 * mate
                pairs.append((at + 2, at))
            got = lax.ppermute(states[2], "tm", sorted(pairs))
        if i == SPLIT:
            _, slab_left, slab_right = lax.optimization_barrier((states[0], slab_left, slab_right))
            left = halves(slab_left[0].reshape(4 * N, BLOCK))
            right = halves(slab_right[0].reshape(4 * N, BLOCK))
            got, left, right = lax.optimization_barrier((got, left, right))
        if i == BUILD:
            rows, _ = lax.optimization_barrier((rows, states[0]))
            rows = tall(tall_body, rows, f_odd, *odd_mats, *odd_arrow)
            rows = tall(tall_body, rows, f, *even_mats, *even_arrow)
            moved_rows = lax.ppermute(rows, "tm", [(4 * k, 4 * k + 2) for k in groups if moves(k)])
            rows, term = call(pick_body, [shape(BLOCK, WIDE), shape(ROWS, WIDE)], [VMEM] * 2, (rows, moved_rows))
            others = around(rows, sorted(home(k) for k in groups))
            got, rows, others = lax.optimization_barrier((got, rows, others))
        states = two_steps([lambda at, device=device: at == device], [got], states, terms, mats)
    high, low, side = call(
        place_body,
        [shape(N, N, dtype=BF16)] * 2 + [shape(N + ROWS, 128)],
        [VMEM] * 5,
        (rows, *others, term),
    )
    for k in range(1, ROOT + 1):
        got = lax.ppermute(side, "tm", [(home(k - 1), home(k))])
        side = adjoint(lambda at, k=k: at == home(k), got, side, high, low, term)
    group_mats = (high, low, side)

    x_in, x_odd, x_even = states
    message = x_even
    sources = [home(k + 1) if k + 1 < GROUPS else 4 * GROUPS for k in groups]
    half = (GROUPS + 1) // 2
    for k in reversed(groups):
        pairs = [(sources[k], home(k))]
        mate = k + half if k + half < GROUPS else k - half
        if 0 <= mate:
            pairs.append((sources[mate], home(mate)))
        got = lax.ppermute(message, "tm", sorted(pairs))
        if k:
            x_in, message = one_step(lambda at, k=k: at == home(k), got, (x_in, message), term, group_mats)
    last = got

    (total,) = call(sum_body, [shape(ROWS, 128)], [VMEM], (message,))

    def spread(total, pairs):
        reached = [b for _, b in pairs]
        return choose(
            lambda at: functools.reduce(jnp.logical_or, [at == r for r in reached]),
            lax.ppermute(total, "tm", sorted(pairs)),
            total,
        )

    total = spread(total, [(10, 58)])
    total = spread(total, [(58, 50)])
    total, x_in, x_odd, x_even, last = lax.optimization_barrier((total, x_in, x_odd, x_even, last))

    got = lax.ppermute(x_in, "tm", [(4 * k, 4 * k + 2) for k in groups if not moves(k)])
    x_in, x_odd, x_even = two_steps(
        [
            lambda at: upper_chip(at) & jnp.logical_not(moved(at)),
            lambda at: at == home(0),
            lambda at: moved(at) & (at != home(0)),
        ],
        [got, last, x_in],
        (x_in, x_odd, x_even),
        terms,
        mats,
    )
    got = lax.ppermute(x_even, "tm", inner)
    x_in, x_odd, x_even = two_steps([lower_chip], [got], (x_in, x_odd, x_even), terms, mats)
    total, x_odd, x_even = lax.optimization_barrier((total, x_odd, x_even))
    total = spread(total, [(58, 2), (50, 34), (10, 26)])
    total = spread(total, [(50, 42), (26, 18)])
    sets = [[(a, a + by) for a in range(2, PARTS, 8)] for by in (4, 2, -2)]
    gots = [lax.ppermute(total, "tm", pairs) for pairs in sets]
    for at_x, got in zip((6, 4, 0), gots):
        total = choose(lambda at, at_x=at_x: at % 8 == at_x, got, total)
    send, keep = call(finish_body, [shape(2 * ROWS, WIDE)] * 2, [VMEM] * 4, (x_in, x_odd, x_even, total))
    pair = choose(lambda at: at % 2 == 1, lax.ppermute(send, "tm", up), keep)
    blocks = [pair] + around(pair, range(PARTS))
    columns, slab, corner = call(
        slab_body,
        [shape(64, BLOCK), shape(4, 64, BLOCK), shape(64, 64)],
        [VMEM] * 9,
        (*blocks, *left, *right, corner_base),
        12 * 64 * N * N,
        scratch_shapes=[pltpu.VMEM((64, N), F32)] * 2 + [pltpu.VMEM((64, 128), F32)],
    )
    return (columns[None], slab[None], corner)


def solution(mesh):
    placed = (
        P("tm", None, None),
        P("tm", None, None),
        P("tm", None, None, "col"),
        P("tm", None, None, "col"),
        P("tm", None, "col"),
        P(),
    )
    return jax.shard_map(
        local,
        mesh=mesh,
        in_specs=placed,
        out_specs=(P("tm", None, "col"), P("tm", None, None, "col"), P()),
        check_vma=False,
    )
```

```python
import functools
import jax
import jax.numpy as jnp
from jax import lax
from jax.experimental import pallas as pl
from jax.experimental.pallas import tpu as pltpu
from jax.sharding import PartitionSpec as P

PARTS = 64
N = 1024
COLS = 4
ROWS = 16
BLOCK = 256
WIDE = N + 128
TOP = 20
SPLIT = 4
BUILD = 8
KEPT = 10
ROOT = 2
GROUPS = (PARTS - TOP) // 4
F32 = jnp.float32
BF16 = jnp.bfloat16
VMEM = pl.BlockSpec(memory_space=pltpu.VMEM)


def split(value):
    high = value.astype(BF16)
    return high, (value - high.astype(F32)).astype(BF16)


def product(left, high, low):
    rows = left.shape[0]
    left_high, left_low = split(left)
    both = jnp.dot(jnp.concatenate([left_high, left_low], 0), high, preferred_element_type=F32)
    return both[:rows] + both[rows:] + jnp.dot(left_high, low, preferred_element_type=F32)


def call(body, outs, specs, operands, flops=0, limit=8, **kw):
    return pl.pallas_call(
        body,
        out_shape=outs,
        in_specs=specs,
        out_specs=[VMEM] * len(outs),
        compiler_params=pltpu.CompilerParams(vmem_limit_bytes=limit << 20),
        cost_estimate=pl.CostEstimate(flops=flops, bytes_accessed=4 << 20, transcendentals=0),
        **kw,
    )(*operands)


def shape(*dims, dtype=F32):
    return jax.ShapeDtypeStruct(dims, dtype)


def when_at(test, run):
    pl.when(test(lax.axis_index("tm")))(run)


def upper_chip(at):
    return (at % 4 == 2) & (at < 4 * GROUPS)


def lower_chip(at):
    return (at % 4 == 0) & (at < 4 * GROUPS)


def moved(at):
    return (at % 8 == 2) & (at < 4 * KEPT)


def moves(k):
    return k % 2 == 0 and k < KEPT


def home(k):
    return 4 * k + 2 if moves(k) else 4 * k


def is_home(at):
    return moved(at) | ((at % 8 == 4) & (at < 4 * GROUPS)) | ((at % 8 == 0) & (at >= 4 * KEPT) & (at < 4 * GROUPS))


def first_body(left_ref, bias_ref, high_ref, low_ref, odd_high, odd_low, even_high, even_low, out_ref):
    def run():
        left = left_ref[...]
        x = product(left, high_ref[...], low_ref[...])
        out_ref[:, :N] = x
        out_ref[BLOCK:, :N] += bias_ref[...]
        out_ref[:, N:] = product(left, odd_high[...], odd_low[...]) + product(out_ref[:, :N], even_high[...], even_low[...])

    when_at(upper_chip, run)


def tall_body(left_ref, bias_ref, high_ref, low_ref, arrow_high, arrow_low, out_ref):
    def run():
        out_ref[:, :N] = product(left_ref[:, :N], high_ref[...], low_ref[...])
        out_ref[BLOCK:, :N] += bias_ref[...]
        out_ref[:, N:] = left_ref[:, N:] + product(out_ref[:, :N], arrow_high[...], arrow_low[...])

    when_at(lower_chip, run)


def tall(body, *operands):
    (out,) = call(body, [shape(BLOCK + ROWS, WIDE)], [VMEM] * len(operands), operands, 7 * 272 * N * N, 12)
    return out


def pick_body(own_ref, got_ref, rows_ref, term_ref):
    def take(source):
        rows_ref[...] = source[:BLOCK, :]
        term_ref[...] = source[BLOCK:, :]

    when_at(moved, lambda: take(got_ref))
    when_at(lambda at: jnp.logical_not(moved(at)), lambda: take(own_ref))


def follow(state, mats, bias, arrow, out_ref):
    x = product(state[:, :N], mats[0][...], mats[1][...]) + bias[...]
    out_ref[:, :N] = x
    out_ref[:, N:] = state[:, N:] + product(x, arrow[0][...], arrow[1][...])


def two_body(tests, *refs):
    count = len(tests)
    gots, (in_0, odd_0, even_0, fo, fe, oah, oal, eah, eal, oh, ol, eh, el, in_1, odd_1, even_1) = refs[:count], refs[count:]

    def step(got):
        follow(got, (oh, ol), fo, (oah, oal), odd_1)
        follow(odd_1, (eh, el), fe, (eah, eal), even_1)
        in_1[...] = got[...]

    for test, got in zip(tests, gots):
        when_at(test, functools.partial(step, got))


def two_steps(tests, gots, states, terms, mats):
    count = len(gots)
    return call(
        functools.partial(two_body, tests),
        [shape(ROWS, WIDE)] * 3,
        [VMEM] * (13 + count),
        (*gots, *states, *terms, *mats),
        13 * 16 * N * N,
        input_output_aliases={count: 0, count + 1: 1, count + 2: 2},
    )


def one_body(test, got, in_0, state_0, term, high, low, side, in_1, state_1):
    def run():
        x = got[:, :N]
        in_1[...] = got[...]
        state_1[:, :N] = product(x, high[...], low[...]) + term[:, :N]
        side_high, side_low = split(side[:N, :])
        state_1[:, N:] = got[:, N:] + product(x, side_high, side_low) + side[N:, :]

    when_at(test, run)


def one_step(test, got, states, term, mats):
    return call(
        functools.partial(one_body, test),
        [shape(ROWS, WIDE)] * 2,
        [VMEM] * 7,
        (got, *states, term, *mats),
        7 * 16 * N * N,
        input_output_aliases={1: 0, 2: 1},
    )


def places():
    c = lax.axis_index("col")
    return [c, (c + 3) % COLS, (c + 1) % COLS, (c + 2) % COLS]


def place_body(b0, b1, b2, b3, term, high_ref, low_ref, side_ref):
    def run():
        for place, block in zip(places(), (b0, b1, b2, b3)):
            high, low = split(block[:, :N])
            at = pl.ds(pl.multiple_of(place * BLOCK, BLOCK), BLOCK)
            high_ref[at, :] = high
            low_ref[at, :] = low
            side_ref[at, :] = block[:, N:]
        side_ref[N:, :] = term[:, N:]

    when_at(is_home, run)


def adjoint_body(test, got, side_0, high, low, term, side_1):
    def run():
        got_high, got_low = split(got[:N, :])
        for i in range(N // BLOCK):
            at = slice(i * BLOCK, (i + 1) * BLOCK)
            both = jnp.dot(jnp.concatenate([high[at, :], low[at, :]], 0), got_high, preferred_element_type=F32)
            rest = jnp.dot(high[at, :], got_low, preferred_element_type=F32)
            side_1[at, :] = side_0[at, :] + both[:BLOCK] + both[BLOCK:] + rest
        side_1[N:, :] = side_0[N:, :] + got[N:, :] + product(term[:, :N], got_high, got_low)

    when_at(test, run)


def adjoint(test, got, side, high, low, term):
    (out,) = call(
        functools.partial(adjoint_body, test),
        [shape(N + ROWS, 128)],
        [VMEM] * 5,
        (got, side, high, low, term),
        6 * N * N * 128,
        input_output_aliases={1: 0},
    )
    return out


def slab_body(b0, b1, b2, b3, lh, ll, rh, rl, base, own_ref, out_ref, corner_ref, x_ref, next_ref, rows_ref):
    for place, block in zip(places(), (b0, b1, b2, b3)):
        at = pl.ds(pl.multiple_of(place * ROWS, ROWS), ROWS)
        x_ref[at, :] = block[:ROWS, :N]
        next_ref[at, :] = block[ROWS:, :N]
        rows_ref[at, :] = block[:ROWS, N:]
    corner_ref[...] = base[...] + rows_ref[...].T[:64, :]
    own = x_ref[...]
    later = next_ref[...]
    own_ref[...] = x_ref[:, pl.ds(pl.multiple_of(places()[0] * BLOCK, BLOCK), BLOCK)]
    for k in range(4):
        at = slice(k * N, k * N + N)
        out_ref[k] = product(own, lh[at, :], ll[at, :]) + product(later, rh[at, :], rl[at, :])


def finish_body(in_ref, odd_ref, even_ref, total_ref, send_ref, keep_ref):
    for ref, own, later in ((send_ref, odd_ref, in_ref), (keep_ref, even_ref, odd_ref)):
        ref[:ROWS, :N] = own[:, :N]
        ref[ROWS:, :N] = later[:, :N]
        ref[:ROWS, N:] = total_ref[...]
        ref[ROWS:, N:] = total_ref[...]


def choose_body(test, got_ref, keep_ref, out_ref):
    def take(source):
        out_ref[...] = source[...]

    when_at(test, lambda: take(got_ref))
    when_at(lambda at: jnp.logical_not(test(at)), lambda: take(keep_ref))


def choose(test, got, keep):
    (out,) = call(functools.partial(choose_body, test), [shape(*keep.shape)], [VMEM] * 2, (got, keep))
    return out


def sum_body(message_ref, out_ref):
    out_ref[...] = message_ref[:, N:]


def gather_body(b0, b1, b2, b3, f_ref, out_ref):
    for place, block in zip(places(), (b0, b1, b2, b3)):
        out_ref[:64, pl.ds(pl.multiple_of(place * BLOCK, BLOCK), BLOCK)] = block[...]
    out_ref[64:, :] = f_ref[...]


def arrow_body(odd_in, even_in, odd_high, odd_low, even_high, even_low, f_ref, rows_ref):
    def run():
        for source, high, low in ((odd_in, odd_high, odd_low), (even_in, even_high, even_low)):
            rows_ref[:64, :] = source[:64, :]
            rows_ref[64:, :] = jnp.zeros((64, N), F32)
            high[...], low[...] = split(rows_ref[...].T)
        f_ref[...] = odd_in[64:, :]

    when_at(lambda at: at % 2 == 0, run)


def whole_body(value_ref, high_ref, low_ref):
    @pl.loop(0, N // 64)
    def _(i):
        at = pl.ds(pl.multiple_of(i * 64, 64), 64)
        high_ref[at, :], low_ref[at, :] = split(value_ref[at, :])


def whole(value):
    return call(whole_body, [shape(N, N, dtype=BF16)] * 2, [VMEM], (value,), 2 * N * N)


def split_body(value_ref, high_ref, low_ref):
    high_ref[...], low_ref[...] = split(value_ref[...])


def halves(value, step=BLOCK):
    rows, columns = value.shape
    tile = pl.BlockSpec((step, columns), lambda i: (i, 0))
    return pl.pallas_call(
        split_body,
        grid=(rows // step,),
        out_shape=[shape(rows, columns, dtype=BF16)] * 2,
        in_specs=[tile],
        out_specs=[tile, tile],
        compiler_params=pltpu.CompilerParams(vmem_limit_bytes=8 << 20),
        cost_estimate=pl.CostEstimate(flops=2 * rows * columns, bytes_accessed=8 * rows * columns, transcendentals=0),
    )(value)


def around(value, members):
    return [lax.ppermute(value, ("tm", "col"), [(t * COLS + j, t * COLS + (j + by) % COLS) for t in members for j in range(COLS)]) for by in (1, 3, 2)]


def local(couple, free_term, slab_left, slab_right, arrow_rows, corner_base):
    c = lax.axis_index("col")
    own = couple[0]
    f = lax.dynamic_slice_in_dim(free_term[0], c * ROWS, ROWS, 0)
    groups = range(GROUPS)
    down = [(2 * j + 1, 2 * j) for j in range(PARTS // 2)]
    up = [(b, a) for a, b in down]
    inner = [(4 * k + 2, 4 * k) for k in groups]

    other = lax.ppermute(own, "tm", down)
    start = jnp.concatenate([lax.dynamic_slice_in_dim(own, c * BLOCK, BLOCK, 0), f], 0)
    start = lax.ppermute(start, "tm", [(4 * k + 3, 4 * k + 2) for k in groups])
    arrow = arrow_rows[0]
    others = around(arrow, range(PARTS))
    even_mats = whole(own)
    odd_mats = whole(other)
    others, even_mats, odd_mats = lax.optimization_barrier((others, even_mats, odd_mats))
    (arrow,) = call(gather_body, [shape(64 + ROWS, N)], [VMEM] * 5, (arrow, *others, f))
    arrows = call(
        arrow_body,
        [shape(N, 128, dtype=BF16)] * 4 + [shape(ROWS, N)],
        [VMEM] * 2,
        (lax.ppermute(arrow, "tm", down), arrow),
        scratch_shapes=[pltpu.VMEM((128, N), F32)],
    )
    odd_arrow, even_arrow, f_odd = arrows[:2], arrows[2:4], arrows[4]
    mats = (*odd_mats, *even_mats)
    terms = (f_odd, f, *odd_arrow, *even_arrow)
    rows = tall(first_body, start, f, *even_mats, *odd_arrow, *even_arrow)
    zero = jnp.zeros((ROWS, WIDE), F32)
    rows, zero = lax.optimization_barrier((rows, zero))
    rows = lax.ppermute(rows, "tm", inner)

    states = (zero, zero, zero)
    chips = TOP // 2
    half = chips // 2
    got = zero
    for i in range(chips):
        device = PARTS - 2 - 2 * i
        if i:
            pairs = [(device + 2, device)]
            mate = i + half if i + half < chips else i - half
            if 0 < mate < chips:
                at = PARTS - 2 - 2 * mate
                pairs.append((at + 2, at))
            got = lax.ppermute(states[2], "tm", sorted(pairs))
        if i == SPLIT:
            _, slab_left, slab_right = lax.optimization_barrier((states[0], slab_left, slab_right))
            left = halves(slab_left[0].reshape(4 * N, BLOCK))
            right = halves(slab_right[0].reshape(4 * N, BLOCK))
            got, left, right = lax.optimization_barrier((got, left, right))
        if i == BUILD:
            rows, _ = lax.optimization_barrier((rows, states[0]))
            rows = tall(tall_body, rows, f_odd, *odd_mats, *odd_arrow)
            rows = tall(tall_body, rows, f, *even_mats, *even_arrow)
            moved_rows = lax.ppermute(rows, "tm", [(4 * k, 4 * k + 2) for k in groups if moves(k)])
            rows, term = call(pick_body, [shape(BLOCK, WIDE), shape(ROWS, WIDE)], [VMEM] * 2, (rows, moved_rows))
            others = around(rows, sorted(home(k) for k in groups))
            got, rows, others = lax.optimization_barrier((got, rows, others))
        states = two_steps([lambda at, device=device: at == device], [got], states, terms, mats)
    high, low, side = call(
        place_body,
        [shape(N, N, dtype=BF16)] * 2 + [shape(N + ROWS, 128)],
        [VMEM] * 5,
        (rows, *others, term),
    )
    for k in range(1, ROOT + 1):
        got = lax.ppermute(side, "tm", [(home(k - 1), home(k))])
        side = adjoint(lambda at, k=k: at == home(k), got, side, high, low, term)
    group_mats = (high, low, side)

    x_in, x_odd, x_even = states
    message = x_even
    sources = [home(k + 1) if k + 1 < GROUPS else 4 * GROUPS for k in groups]
    half = (GROUPS + 1) // 2
    for k in reversed(groups):
        pairs = [(sources[k], home(k))]
        mate = k + half if k + half < GROUPS else k - half
        if 0 <= mate:
            pairs.append((sources[mate], home(mate)))
        got = lax.ppermute(message, "tm", sorted(pairs))
        if k:
            x_in, message = one_step(lambda at, k=k: at == home(k), got, (x_in, message), term, group_mats)
    last = got

    (total,) = call(sum_body, [shape(ROWS, 128)], [VMEM], (message,))

    def spread(total, pairs):
        reached = [b for _, b in pairs]
        return choose(
            lambda at: functools.reduce(jnp.logical_or, [at == r for r in reached]),
            lax.ppermute(total, "tm", sorted(pairs)),
            total,
        )

    total = spread(total, [(10, 58)])
    total = spread(total, [(58, 2)])
    total = spread(total, [(58, 50)])
    total, x_in, x_odd, x_even, last = lax.optimization_barrier((total, x_in, x_odd, x_even, last))

    got = lax.ppermute(x_in, "tm", [(4 * k, 4 * k + 2) for k in groups if not moves(k)])
    x_in, x_odd, x_even = two_steps(
        [
            lambda at: upper_chip(at) & jnp.logical_not(moved(at)),
            lambda at: at == home(0),
            lambda at: moved(at) & (at != home(0)),
        ],
        [got, last, x_in],
        (x_in, x_odd, x_even),
        terms,
        mats,
    )
    got = lax.ppermute(x_even, "tm", inner)
    x_in, x_odd, x_even = two_steps([lower_chip], [got], (x_in, x_odd, x_even), terms, mats)
    total, x_odd, x_even = lax.optimization_barrier((total, x_odd, x_even))
    total = spread(total, [(50, 34), (10, 26)])
    total = spread(total, [(50, 42), (26, 18)])
    sets = [[(a, a + by) for a in range(2, PARTS, 8)] for by in (4, 2, -2)]
    gots = [lax.ppermute(total, "tm", pairs) for pairs in sets]
    for at_x, got in zip((6, 4, 0), gots):
        total = choose(lambda at, at_x=at_x: at % 8 == at_x, got, total)
    send, keep = call(finish_body, [shape(2 * ROWS, WIDE)] * 2, [VMEM] * 4, (x_in, x_odd, x_even, total))
    pair = choose(lambda at: at % 2 == 1, lax.ppermute(send, "tm", up), keep)
    blocks = [pair] + around(pair, range(PARTS))
    columns, slab, corner = call(
        slab_body,
        [shape(64, BLOCK), shape(4, 64, BLOCK), shape(64, 64)],
        [VMEM] * 9,
        (*blocks, *left, *right, corner_base),
        12 * 64 * N * N,
        scratch_shapes=[pltpu.VMEM((64, N), F32)] * 2 + [pltpu.VMEM((64, 128), F32)],
    )
    return (columns[None], slab[None], corner)


def solution(mesh):
    placed = (
        P("tm", None, None),
        P("tm", None, None),
        P("tm", None, None, "col"),
        P("tm", None, None, "col"),
        P("tm", None, "col"),
        P(),
    )
    return jax.shard_map(
        local,
        mesh=mesh,
        in_specs=placed,
        out_specs=(P("tm", None, "col"), P("tm", None, None, "col"), P()),
        check_vma=False,
    )
```

```python
import functools
import jax
import jax.numpy as jnp
from jax import lax
from jax.experimental import pallas as pl
from jax.experimental.pallas import tpu as pltpu
from jax.sharding import PartitionSpec as P

PARTS = 64
N = 1024
COLS = 4
ROWS = 16
BLOCK = 256
WIDE = N + 128
TOP = 20
SPLIT = 4
BUILD = 8
KEPT = 10
ROOT = 2
GROUPS = (PARTS - TOP) // 4
F32 = jnp.float32
BF16 = jnp.bfloat16
VMEM = pl.BlockSpec(memory_space=pltpu.VMEM)


def split(value):
    high = value.astype(BF16)
    return high, (value - high.astype(F32)).astype(BF16)


def product(left, high, low):
    rows = left.shape[0]
    left_high, left_low = split(left)
    both = jnp.dot(jnp.concatenate([left_high, left_low], 0), high, preferred_element_type=F32)
    return both[:rows] + both[rows:] + jnp.dot(left_high, low, preferred_element_type=F32)


def call(body, outs, specs, operands, flops=0, limit=8, **kw):
    return pl.pallas_call(
        body,
        out_shape=outs,
        in_specs=specs,
        out_specs=[VMEM] * len(outs),
        compiler_params=pltpu.CompilerParams(vmem_limit_bytes=limit << 20),
        cost_estimate=pl.CostEstimate(flops=flops, bytes_accessed=4 << 20, transcendentals=0),
        **kw,
    )(*operands)


def shape(*dims, dtype=F32):
    return jax.ShapeDtypeStruct(dims, dtype)


def when_at(test, run):
    pl.when(test(lax.axis_index("tm")))(run)


def upper_chip(at):
    return (at % 4 == 2) & (at < 4 * GROUPS)


def lower_chip(at):
    return (at % 4 == 0) & (at < 4 * GROUPS)


def moved(at):
    return (at % 8 == 2) & (at < 4 * KEPT)


def moves(k):
    return k % 2 == 0 and k < KEPT


def home(k):
    return 4 * k + 2 if moves(k) else 4 * k


def is_home(at):
    return moved(at) | ((at % 8 == 4) & (at < 4 * GROUPS)) | ((at % 8 == 0) & (at >= 4 * KEPT) & (at < 4 * GROUPS))


def first_body(left_ref, bias_ref, high_ref, low_ref, odd_high, odd_low, even_high, even_low, out_ref):
    def run():
        left = left_ref[...]
        x = product(left, high_ref[...], low_ref[...])
        out_ref[:, :N] = x
        out_ref[BLOCK:, :N] += bias_ref[...]
        out_ref[:, N:] = product(left, odd_high[...], odd_low[...]) + product(out_ref[:, :N], even_high[...], even_low[...])

    when_at(upper_chip, run)


def tall_body(left_ref, bias_ref, high_ref, low_ref, arrow_high, arrow_low, out_ref):
    def run():
        out_ref[:, :N] = product(left_ref[:, :N], high_ref[...], low_ref[...])
        out_ref[BLOCK:, :N] += bias_ref[...]
        out_ref[:, N:] = left_ref[:, N:] + product(out_ref[:, :N], arrow_high[...], arrow_low[...])

    when_at(lower_chip, run)


def tall(body, *operands):
    (out,) = call(body, [shape(BLOCK + ROWS, WIDE)], [VMEM] * len(operands), operands, 7 * 272 * N * N, 12)
    return out


def pick_body(own_ref, got_ref, rows_ref, term_ref):
    def take(source):
        rows_ref[...] = source[:BLOCK, :]
        term_ref[...] = source[BLOCK:, :]

    when_at(moved, lambda: take(got_ref))
    when_at(lambda at: jnp.logical_not(moved(at)), lambda: take(own_ref))


def follow(state, mats, bias, arrow, out_ref):
    x = product(state[:, :N], mats[0][...], mats[1][...]) + bias[...]
    out_ref[:, :N] = x
    out_ref[:, N:] = state[:, N:] + product(x, arrow[0][...], arrow[1][...])


def two_body(tests, *refs):
    count = len(tests)
    gots, (in_0, odd_0, even_0, fo, fe, oah, oal, eah, eal, oh, ol, eh, el, in_1, odd_1, even_1) = refs[:count], refs[count:]

    def step(got):
        follow(got, (oh, ol), fo, (oah, oal), odd_1)
        follow(odd_1, (eh, el), fe, (eah, eal), even_1)
        in_1[...] = got[...]

    for test, got in zip(tests, gots):
        when_at(test, functools.partial(step, got))


def launch_body(in_0, odd_0, even_0, fo, fe, oah, oal, eah, eal, eh, el, in_1, odd_1, even_1):
    def run():
        in_1[...] = jnp.zeros((ROWS, WIDE), F32)
        odd_1[:, :N] = fo[...]
        odd_1[:, N:] = product(fo[...], oah[...], oal[...])
        follow(odd_1, (eh, el), fe, (eah, eal), even_1)

    when_at(lambda at: at == PARTS - 2, run)


def launch(states, terms, mats):
    return call(
        launch_body,
        [shape(ROWS, WIDE)] * 3,
        [VMEM] * 11,
        (*states, *terms, *mats),
        7 * 16 * N * N,
        input_output_aliases={0: 0, 1: 1, 2: 2},
    )


def two_steps(tests, gots, states, terms, mats):
    count = len(gots)
    return call(
        functools.partial(two_body, tests),
        [shape(ROWS, WIDE)] * 3,
        [VMEM] * (13 + count),
        (*gots, *states, *terms, *mats),
        13 * 16 * N * N,
        input_output_aliases={count: 0, count + 1: 1, count + 2: 2},
    )


def one_body(test, got, in_0, state_0, term, high, low, side, in_1, state_1):
    def run():
        x = got[:, :N]
        in_1[...] = got[...]
        state_1[:, :N] = product(x, high[...], low[...]) + term[:, :N]
        side_high, side_low = split(side[:N, :])
        state_1[:, N:] = got[:, N:] + product(x, side_high, side_low) + side[N:, :]

    when_at(test, run)


def one_step(test, got, states, term, mats):
    return call(
        functools.partial(one_body, test),
        [shape(ROWS, WIDE)] * 2,
        [VMEM] * 7,
        (got, *states, term, *mats),
        7 * 16 * N * N,
        input_output_aliases={1: 0, 2: 1},
    )


def places():
    c = lax.axis_index("col")
    return [c, (c + 3) % COLS, (c + 1) % COLS, (c + 2) % COLS]


def place_body(b0, b1, b2, b3, term, high_ref, low_ref, side_ref):
    def run():
        for place, block in zip(places(), (b0, b1, b2, b3)):
            high, low = split(block[:, :N])
            at = pl.ds(pl.multiple_of(place * BLOCK, BLOCK), BLOCK)
            high_ref[at, :] = high
            low_ref[at, :] = low
            side_ref[at, :] = block[:, N:]
        side_ref[N:, :] = term[:, N:]

    when_at(is_home, run)


def adjoint_body(test, got, side_0, high, low, term, side_1):
    def run():
        got_high, got_low = split(got[:N, :])
        for i in range(N // BLOCK):
            at = slice(i * BLOCK, (i + 1) * BLOCK)
            both = jnp.dot(jnp.concatenate([high[at, :], low[at, :]], 0), got_high, preferred_element_type=F32)
            rest = jnp.dot(high[at, :], got_low, preferred_element_type=F32)
            side_1[at, :] = side_0[at, :] + both[:BLOCK] + both[BLOCK:] + rest
        side_1[N:, :] = side_0[N:, :] + got[N:, :] + product(term[:, :N], got_high, got_low)

    when_at(test, run)


def adjoint(test, got, side, high, low, term):
    (out,) = call(
        functools.partial(adjoint_body, test),
        [shape(N + ROWS, 128)],
        [VMEM] * 5,
        (got, side, high, low, term),
        6 * N * N * 128,
        input_output_aliases={1: 0},
    )
    return out


def slab_body(b0, b1, b2, b3, lh, ll, rh, rl, base, own_ref, out_ref, corner_ref, x_ref, next_ref, rows_ref):
    for place, block in zip(places(), (b0, b1, b2, b3)):
        at = pl.ds(pl.multiple_of(place * ROWS, ROWS), ROWS)
        x_ref[at, :] = block[:ROWS, :N]
        next_ref[at, :] = block[ROWS:, :N]
        rows_ref[at, :] = block[:ROWS, N:]
    corner_ref[...] = base[...] + rows_ref[...].T[:64, :]
    own = x_ref[...]
    later = next_ref[...]
    own_ref[...] = x_ref[:, pl.ds(pl.multiple_of(places()[0] * BLOCK, BLOCK), BLOCK)]
    for k in range(4):
        at = slice(k * N, k * N + N)
        out_ref[k] = product(own, lh[at, :], ll[at, :]) + product(later, rh[at, :], rl[at, :])


def finish_body(in_ref, odd_ref, even_ref, total_ref, send_ref, keep_ref):
    for ref, own, later in ((send_ref, odd_ref, in_ref), (keep_ref, even_ref, odd_ref)):
        ref[:ROWS, :N] = own[:, :N]
        ref[ROWS:, :N] = later[:, :N]
        ref[:ROWS, N:] = total_ref[...]
        ref[ROWS:, N:] = total_ref[...]


def choose_body(test, got_ref, keep_ref, out_ref):
    def take(source):
        out_ref[...] = source[...]

    when_at(test, lambda: take(got_ref))
    when_at(lambda at: jnp.logical_not(test(at)), lambda: take(keep_ref))


def choose(test, got, keep):
    (out,) = call(functools.partial(choose_body, test), [shape(*keep.shape)], [VMEM] * 2, (got, keep))
    return out


def sum_body(message_ref, out_ref):
    out_ref[...] = message_ref[:, N:]


def gather_body(b0, b1, b2, b3, f_ref, out_ref):
    for place, block in zip(places(), (b0, b1, b2, b3)):
        out_ref[:64, pl.ds(pl.multiple_of(place * BLOCK, BLOCK), BLOCK)] = block[...]
    out_ref[64:, :] = f_ref[...]


def arrow_body(odd_in, even_in, odd_high, odd_low, even_high, even_low, f_ref, rows_ref):
    def run():
        for source, high, low in ((odd_in, odd_high, odd_low), (even_in, even_high, even_low)):
            rows_ref[:64, :] = source[:64, :]
            rows_ref[64:, :] = jnp.zeros((64, N), F32)
            high[...], low[...] = split(rows_ref[...].T)
        f_ref[...] = odd_in[64:, :]

    when_at(lambda at: at % 2 == 0, run)


def whole_body(value_ref, high_ref, low_ref):
    @pl.loop(0, N // 64)
    def _(i):
        at = pl.ds(pl.multiple_of(i * 64, 64), 64)
        high_ref[at, :], low_ref[at, :] = split(value_ref[at, :])


def whole(value):
    return call(whole_body, [shape(N, N, dtype=BF16)] * 2, [VMEM], (value,), 2 * N * N)


def split_body(value_ref, high_ref, low_ref):
    high_ref[...], low_ref[...] = split(value_ref[...])


def halves(value, step=BLOCK):
    rows, columns = value.shape
    tile = pl.BlockSpec((step, columns), lambda i: (i, 0))
    return pl.pallas_call(
        split_body,
        grid=(rows // step,),
        out_shape=[shape(rows, columns, dtype=BF16)] * 2,
        in_specs=[tile],
        out_specs=[tile, tile],
        compiler_params=pltpu.CompilerParams(vmem_limit_bytes=8 << 20),
        cost_estimate=pl.CostEstimate(flops=2 * rows * columns, bytes_accessed=8 * rows * columns, transcendentals=0),
    )(value)


def around(value, members):
    return [lax.ppermute(value, ("tm", "col"), [(t * COLS + j, t * COLS + (j + by) % COLS) for t in members for j in range(COLS)]) for by in (1, 3, 2)]


def local(couple, free_term, slab_left, slab_right, arrow_rows, corner_base):
    c = lax.axis_index("col")
    own = couple[0]
    f = lax.dynamic_slice_in_dim(free_term[0], c * ROWS, ROWS, 0)
    groups = range(GROUPS)
    down = [(2 * j + 1, 2 * j) for j in range(PARTS // 2)]
    up = [(b, a) for a, b in down]
    inner = [(4 * k + 2, 4 * k) for k in groups]

    other = lax.ppermute(own, "tm", down)
    start = jnp.concatenate([lax.dynamic_slice_in_dim(own, c * BLOCK, BLOCK, 0), f], 0)
    start = lax.ppermute(start, "tm", [(4 * k + 3, 4 * k + 2) for k in groups])
    arrow = arrow_rows[0]
    others = around(arrow, range(PARTS))
    even_mats = whole(own)
    odd_mats = whole(other)
    others, even_mats, odd_mats = lax.optimization_barrier((others, even_mats, odd_mats))
    (arrow,) = call(gather_body, [shape(64 + ROWS, N)], [VMEM] * 5, (arrow, *others, f))
    arrows = call(
        arrow_body,
        [shape(N, 128, dtype=BF16)] * 4 + [shape(ROWS, N)],
        [VMEM] * 2,
        (lax.ppermute(arrow, "tm", down), arrow),
        scratch_shapes=[pltpu.VMEM((128, N), F32)],
    )
    odd_arrow, even_arrow, f_odd = arrows[:2], arrows[2:4], arrows[4]
    mats = (*odd_mats, *even_mats)
    terms = (f_odd, f, *odd_arrow, *even_arrow)
    rows = tall(first_body, start, f, *even_mats, *odd_arrow, *even_arrow)
    zero = jnp.zeros((ROWS, WIDE), F32)
    rows, zero = lax.optimization_barrier((rows, zero))
    rows = lax.ppermute(rows, "tm", inner)

    states = (zero, zero, zero)
    chips = TOP // 2
    half = chips // 2
    got = zero
    for i in range(chips):
        device = PARTS - 2 - 2 * i
        if i:
            pairs = [(device + 2, device)]
            mate = i + half if i + half < chips else i - half
            if 0 < mate < chips:
                at = PARTS - 2 - 2 * mate
                pairs.append((at + 2, at))
            got = lax.ppermute(states[2], "tm", sorted(pairs))
        if i == SPLIT:
            _, slab_left, slab_right = lax.optimization_barrier((states[0], slab_left, slab_right))
            left = halves(slab_left[0].reshape(4 * N, BLOCK))
            right = halves(slab_right[0].reshape(4 * N, BLOCK))
            got, left, right = lax.optimization_barrier((got, left, right))
        if i == BUILD:
            rows, _ = lax.optimization_barrier((rows, states[0]))
            rows = tall(tall_body, rows, f_odd, *odd_mats, *odd_arrow)
            rows = tall(tall_body, rows, f, *even_mats, *even_arrow)
            moved_rows = lax.ppermute(rows, "tm", [(4 * k, 4 * k + 2) for k in groups if moves(k)])
            rows, term = call(pick_body, [shape(BLOCK, WIDE), shape(ROWS, WIDE)], [VMEM] * 2, (rows, moved_rows))
            others = around(rows, sorted(home(k) for k in groups))
            got, rows, others = lax.optimization_barrier((got, rows, others))
        if i == 0:
            states = launch(states, terms, even_mats)
            continue
        states = two_steps([lambda at, device=device: at == device], [got], states, terms, mats)
    high, low, side = call(
        place_body,
        [shape(N, N, dtype=BF16)] * 2 + [shape(N + ROWS, 128)],
        [VMEM] * 5,
        (rows, *others, term),
    )
    for k in range(1, ROOT + 1):
        got = lax.ppermute(side, "tm", [(home(k - 1), home(k))])
        side = adjoint(lambda at, k=k: at == home(k), got, side, high, low, term)
    group_mats = (high, low, side)

    x_in, x_odd, x_even = states
    message = x_even
    sources = [home(k + 1) if k + 1 < GROUPS else 4 * GROUPS for k in groups]
    half = (GROUPS + 1) // 2
    for k in reversed(groups):
        pairs = [(sources[k], home(k))]
        mate = k + half if k + half < GROUPS else k - half
        if 0 <= mate:
            pairs.append((sources[mate], home(mate)))
        got = lax.ppermute(message, "tm", sorted(pairs))
        if k:
            x_in, message = one_step(lambda at, k=k: at == home(k), got, (x_in, message), term, group_mats)
    last = got

    (total,) = call(sum_body, [shape(ROWS, 128)], [VMEM], (message,))

    def spread(total, pairs):
        reached = [b for _, b in pairs]
        return choose(
            lambda at: functools.reduce(jnp.logical_or, [at == r for r in reached]),
            lax.ppermute(total, "tm", sorted(pairs)),
            total,
        )

    total = spread(total, [(10, 58)])
    total = spread(total, [(58, 50)])
    total, x_in, x_odd, x_even, last = lax.optimization_barrier((total, x_in, x_odd, x_even, last))

    got = lax.ppermute(x_in, "tm", [(4 * k, 4 * k + 2) for k in groups if not moves(k)])
    x_in, x_odd, x_even = two_steps(
        [
            lambda at: upper_chip(at) & jnp.logical_not(moved(at)),
            lambda at: at == home(0),
            lambda at: moved(at) & (at != home(0)),
        ],
        [got, last, x_in],
        (x_in, x_odd, x_even),
        terms,
        mats,
    )
    got = lax.ppermute(x_even, "tm", inner)
    x_in, x_odd, x_even = two_steps([lower_chip], [got], (x_in, x_odd, x_even), terms, mats)
    total, x_odd, x_even = lax.optimization_barrier((total, x_odd, x_even))
    total = spread(total, [(58, 2), (50, 34), (10, 26)])
    total = spread(total, [(50, 42), (26, 18)])
    sets = [[(a, a + by) for a in range(2, PARTS, 8)] for by in (4, 2, -2)]
    gots = [lax.ppermute(total, "tm", pairs) for pairs in sets]
    for at_x, got in zip((6, 4, 0), gots):
        total = choose(lambda at, at_x=at_x: at % 8 == at_x, got, total)
    send, keep = call(finish_body, [shape(2 * ROWS, WIDE)] * 2, [VMEM] * 4, (x_in, x_odd, x_even, total))
    pair = choose(lambda at: at % 2 == 1, lax.ppermute(send, "tm", up), keep)
    blocks = [pair] + around(pair, range(PARTS))
    columns, slab, corner = call(
        slab_body,
        [shape(64, BLOCK), shape(4, 64, BLOCK), shape(64, 64)],
        [VMEM] * 9,
        (*blocks, *left, *right, corner_base),
        12 * 64 * N * N,
        scratch_shapes=[pltpu.VMEM((64, N), F32)] * 2 + [pltpu.VMEM((64, 128), F32)],
    )
    return (columns[None], slab[None], corner)


def solution(mesh):
    placed = (
        P("tm", None, None),
        P("tm", None, None),
        P("tm", None, None, "col"),
        P("tm", None, None, "col"),
        P("tm", None, "col"),
        P(),
    )
    return jax.shard_map(
        local,
        mesh=mesh,
        in_specs=placed,
        out_specs=(P("tm", None, "col"), P("tm", None, None, "col"), P()),
        check_vma=False,
    )
```
